32 devices in a mesh: dp: 16 (over z, x, core), mp: 2 (over y).
Axes of the slice: x: 2, y: 2, z: 4, core: 2. Of those that a mesh axis runs over, the one named last changes fastest.
Arguments:
- tokens: bfloat16 [32, 512, 768], P('dp'), may hold values from -6 to 6
- lengths: int32 [32], P('dp'), may hold values from 64 to 512, as said below
- ln1_gain: float32 [768], replicated, may hold values from 0.25 to 1.75
- ln1_shift: float32 [768], replicated, may hold values from -1.75 to 1.75
- w_qkv: bfloat16 [3, 768, 768], P(None, None, 'mp'), may hold values from -0.21875 to 0.21875
- w_out: bfloat16 [768, 768], P('mp'), may hold values from -1.75 to 1.75
- b_out: float32 [768], replicated, may hold values from -3 to 3
- ln2_gain: float32 [768], replicated, may hold values from 0.25 to 1.75
- ln2_shift: float32 [768], replicated, may hold values from -1.75 to 1.75
- w_up: bfloat16 [768, 3072], P(None, 'mp'), may hold values from -0.21875 to 0.21875
- b_up: float32 [3072], P('mp'), may hold values from -3 to 3
- w_down: bfloat16 [3072, 768], P('mp'), may hold values from -0.109375 to 0.109375
- b_down: float32 [768], replicated, may hold values from -3 to 3
- cotangent: bfloat16 [32, 512, 768], P('dp'), may hold values from -6 to 6
Outputs:
- output: bfloat16 [32, 512, 768], P('dp')
- grad_tokens: float32 [32, 512, 768], P('dp')
- grad_ln1_gain: float32 [768], P('dp')
- grad_ln1_shift: float32 [768], P('dp')
- grad_qkv: float32 [3, 768, 768], P(None, 'dp', 'mp')
- grad_out: float32 [768, 768], P('mp', 'dp')
- grad_b_out: float32 [768], P('dp')
- grad_ln2_gain: float32 [768], P('dp')
- grad_ln2_shift: float32 [768], P('dp')
- grad_up: float32 [768, 3072], P('dp', 'mp')
- grad_b_up: float32 [2, 1536], P('mp', 'dp')
- grad_down: float32 [3072, 768], P('mp', 'dp')
- grad_b_down: float32 [768], P('dp')
The draws below stay inside these ranges and needn't reach their ends.
Inputs may be any that keep to these rules, and one draw needn't show every extreme that they name: `lengths`: the visible tokens of a chip fill its first slots, the rest are padding; some chip has all 512 slots visible and some chip only 64.
All inputs are finite; a program needn't handle non-finite values.
Results may differ from the reference program's by a relative error of at most 0.015.
Values may be sent and summed in bfloat16 or wider, within the bound.
A program may use at most 192 MiB of HBM per device.

```python
import jax
import jax.numpy as jnp
from jax import lax

D = 768
HEADS = 12
HEAD_DIM = 64
FF = 3072
SEQ = 512
CHIPS = 32


def draw_lengths(key, part):
    base_lengths = jax.random.randint(jax.random.fold_in(key, 11), (CHIPS,), SEQ // 8, SEQ + 1)
    order = jax.random.permutation(jax.random.fold_in(key, 12), CHIPS)
    positions = jnp.arange(CHIPS)
    base_lengths = jnp.where(positions == order[0], SEQ, base_lengths)
    base_lengths = jnp.where(positions == order[1], SEQ // 8, base_lengths)
    return base_lengths.astype(jnp.int32)


def spiked(values, own_key, source, target, shards_of, factor):
    owner, partner = [(jnp.arange(values.shape[position]) // (values.shape[position] // shards_of)).reshape([-1 if axis == position else 1 for axis in range(values.ndim)]) for position in (source, target)]
    chosen = jax.random.permutation(own_key, shards_of)[partner]
    strong = (owner == chosen) | (owner == (partner + shards_of // 2) % shards_of)
    return jnp.where(strong, factor * values, values)


def steps_of(stream_key, dims, split, least, high):
    def one(axis_at, parts):
        draws = jax.random.uniform(jax.random.fold_in(jax.random.fold_in(stream_key, 6), axis_at), (parts,), jnp.float32, least / len(split), high / len(split))
        return jnp.repeat(jnp.exp(draws), dims[axis_at] // parts).reshape((-1,) + (1,) * (len(dims) - axis_at - 1))

    loudness = one(*split[0])
    for cut in split[1:]:
        loudness = loudness * one(*cut)
    return loudness


def bell_draw(stream_key, extent, deviation, reach, cuts=(), held_as=jnp.bfloat16):
    loudness = steps_of(stream_key, extent, cuts, -0.22, 0.18) if cuts else 1.0
    drawn = jax.random.normal(stream_key, extent, jnp.float32) * deviation * loudness
    return jnp.minimum(jnp.maximum(drawn, -reach), reach).astype(held_as)


def gaussian_with(stream_key, dims, scale, reach, shards, heavy, dtype=jnp.bfloat16):
    values = scale * jax.random.normal(stream_key, dims, jnp.float32)
    if shards:
        values = values * steps_of(stream_key, dims, shards, -0.22, 0.18)
    return jnp.clip(spiked(values, jax.random.fold_in(stream_key, 3), *heavy), -reach, reach).astype(dtype)


def setup_inputs(seed: int = 0) -> dict:
    seeds = jax.random.split(jax.random.key(seed), 15)
    tokens = gaussian_with(seeds[0], (CHIPS, SEQ, D), 1.0, 6.0, ((0, 16),), (0, 2, 16, 2.0))
    lengths = draw_lengths(jax.random.fold_in(seeds[14], 71), 0)
    ln1_gain = jnp.clip(1.0 + 0.15 * jax.random.normal(seeds[2], (D,), jnp.float32), 0.25, 1.75)
    ln1_shift = bell_draw(seeds[3], (D,), 0.3, 1.75, (), jnp.float32)
    w_qkv = bell_draw(seeds[4], (3, D, D), D ** -0.5, 0.21875, ((2, 2),))
    w_out = bell_draw(seeds[5], (D, D), (D // 64) ** -0.5, 1.75, ((0, 2),))
    b_out = bell_draw(seeds[6], (D,), 0.5, 3.0, (), jnp.float32)
    ln2_gain = jnp.clip(1.0 + 0.15 * jax.random.normal(seeds[7], (D,), jnp.float32), 0.25, 1.75)
    ln2_shift = bell_draw(seeds[8], (D,), 0.3, 1.75, (), jnp.float32)
    w_up = bell_draw(seeds[9], (D, FF), D ** -0.5, 0.21875, ((1, 2),))
    b_up = bell_draw(seeds[10], (FF,), 0.5, 3.0, ((0, 2),), jnp.float32)
    w_down = bell_draw(seeds[11], (FF, D), FF ** -0.5, 0.109375, ((0, 2),))
    b_down = bell_draw(seeds[12], (D,), 0.5, 3.0, (), jnp.float32)
    cotangent = gaussian_with(seeds[13], (CHIPS, SEQ, D), 1.0, 6.0, ((0, 16),), (0, 2, 16, 2.0))
    return dict(tokens=tokens, lengths=lengths, ln1_gain=ln1_gain, ln1_shift=ln1_shift, w_qkv=w_qkv, w_out=w_out, b_out=b_out, ln2_gain=ln2_gain, ln2_shift=ln2_shift, w_up=w_up, b_up=b_up, w_down=w_down, b_down=b_down, cotangent=cotangent)


@jax.custom_vjp
def low(v):
    return lax.optimization_barrier(v.astype(jnp.bfloat16)).astype(jnp.float32)

@jax.custom_vjp
def low_back(v):
    return v

def low_keep(v):
    return (low(v), None)

def low_pass(kept, grad):
    return (grad,)

def back_keep(v):
    return (v, None)

def back_low(kept, grad):
    return (low(grad),)
low.defvjp(low_keep, low_pass)
low_back.defvjp(back_keep, back_low)
highest = lax.Precision.HIGHEST

def layer_norm(values, gain, shift):
    center = values - lax.optimization_barrier(jnp.mean(values, -1, keepdims=True))
    spread = lax.optimization_barrier(jnp.mean(center * center, -1, keepdims=True))
    return center * lax.rsqrt(spread + 1e-05) * gain + shift

def exact_gelu(values):
    return jax.nn.gelu(values, approximate=False)

def chip_forward(weights, inputs, length):
    ln1_gain, ln1_shift, w_qkv, w_out, b_out, ln2_gain, ln2_shift, w_up, b_up, w_down, b_down = weights
    normed_one = low(layer_norm(inputs, ln1_gain, ln1_shift))
    projected = jnp.einsum('td,cde->cte', normed_one, w_qkv, precision=highest)
    projected = low_back(low(projected))
    queries = projected[0].reshape(SEQ, HEADS, HEAD_DIM)
    key_rows = projected[1].reshape(SEQ, HEADS, HEAD_DIM)
    value_rows = projected[2].reshape(SEQ, HEADS, HEAD_DIM)
    key_valid = jnp.arange(SEQ) < length
    block_rows = min(512, SEQ)

    def score_block(query_block):
        raw_scores = jnp.einsum('qhe,khe->hqk', query_block, key_rows, precision=highest)
        scores = low_back(raw_scores) * HEAD_DIM ** (-0.5)
        scores = jnp.where(key_valid[None, None, :], scores, -1e+30)
        log_total = jax.scipy.special.logsumexp(scores, axis=-1, keepdims=True)
        soft_probs = jnp.exp(scores - log_total)
        return jnp.einsum('hqk,khe->qhe', low(soft_probs), value_rows, precision=highest)
    query_blocks = queries.reshape(SEQ // block_rows, block_rows, HEADS, HEAD_DIM)
    attended = lax.map(jax.checkpoint(score_block), query_blocks).reshape(SEQ, D)
    attended = low_back(low(attended))
    head_halves = jnp.einsum('tgc,gcd->gtd', attended.reshape(SEQ, 2, D // 2), w_out.reshape(2, D // 2, D), precision=highest)
    attn_out = low_back(lax.optimization_barrier(jnp.sum(low(head_halves), 0)))
    resid = inputs + attn_out + b_out
    normed_two = low(layer_norm(resid, ln2_gain, ln2_shift))
    up_pre = low_back(jnp.dot(normed_two, w_up, precision=highest) + b_up)
    gelu_out = low(exact_gelu(up_pre))
    unit_halves = jnp.einsum('tgc,gcd->gtd', gelu_out.reshape(SEQ, 2, FF // 2), w_down.reshape(2, FF // 2, D), precision=highest)
    mlp_out = low_back(lax.optimization_barrier(jnp.sum(low(unit_halves), 0)))
    return resid + mlp_out + b_down

def reference(tokens, lengths, ln1_gain, ln1_shift, w_qkv, w_out, b_out, ln2_gain, ln2_shift, w_up, b_up, w_down, b_down, cotangent):
    weights = (ln1_gain.astype(jnp.float32), ln1_shift.astype(jnp.float32), w_qkv.astype(jnp.float32), w_out.astype(jnp.float32), b_out.astype(jnp.float32), ln2_gain.astype(jnp.float32), ln2_shift.astype(jnp.float32), w_up.astype(jnp.float32), b_up.astype(jnp.float32), w_down.astype(jnp.float32), b_down.astype(jnp.float32))
    inputs = tokens.astype(jnp.float32)
    visible = (jnp.arange(SEQ)[None, :] < lengths[:, None])[:, :, None]

    def forward(weight_set, values):

        def one_chip(chip_item):
            return jax.checkpoint(chip_forward)(weight_set, chip_item[0], chip_item[1])
        return lax.map(one_chip, (values, lengths))
    result, pullback = jax.vjp(forward, weights, inputs)
    upstream = jnp.where(visible, cotangent.astype(jnp.float32), jnp.zeros((), jnp.float32))
    weight_grads, input_grad = pullback(upstream)
    grad_g1, grad_s1, grad_qkv, grad_out, grad_bo, grad_g2, grad_s2, grad_up, grad_bu, grad_down, grad_bd = weight_grads
    output = jnp.where(visible, result, jnp.zeros((), jnp.float32)).astype(jnp.bfloat16)
    return (output, input_grad, grad_g1, grad_s1, grad_qkv, grad_out, grad_bo, grad_g2, grad_s2, grad_up, grad_bu.reshape(2, FF // 2), grad_down, grad_bd)
```

```python
import functools

import jax
import jax.numpy as jnp
from jax import lax
from jax.experimental import pallas as pl
from jax.experimental.pallas import tpu as pltpu
from jax.sharding import PartitionSpec as P

HEAD_DIM = 64
PAIR = 2 * HEAD_DIM
BF = jnp.bfloat16
F32 = jnp.float32
EPS = 1e-05
LIMIT = 40 * 1024 * 1024

TAIL_P = 0.3
TAIL_C = (
    0.11962929256864907,
    0.12075406313917503,
    0.09991275007605285,
    0.12856432480895655,
    -0.05368921426491713,
    0.2063600527786208,
    -0.1572071533588575,
    0.03567581131365836,
)


def mm(a, b):
    return lax.dot_general(a, b, (((1,), (0,)), ((), ())), preferred_element_type=F32)


def mm_t(a, b):
    return lax.dot_general(a, b, (((1,), (1,)), ((), ())), preferred_element_type=F32)


def normalize(x):
    mean = jnp.mean(x, -1, keepdims=True)
    center = x - mean
    var = jnp.mean(center * center, -1, keepdims=True)
    inv = lax.rsqrt(var + EPS)
    return center * inv, inv


def norm_back(grad, xhat, inv, gain):
    d = grad * gain
    m1 = jnp.mean(d, -1, keepdims=True)
    m2 = jnp.mean(d * xhat, -1, keepdims=True)
    return inv * (d - m1 - xhat * m2)


def bit_reverse(index, bits):
    out = 0
    for b in range(bits):
        out = (out << 1) | ((index >> b) & 1)
    return out


def put_rows(ref, value, blocks):
    rows = value.shape[0] // blocks
    bits = blocks.bit_length() - 1
    if rows % 16:
        ref[...] = value
        return
    for b in range(blocks):
        d = bit_reverse(b, bits)
        ref[d * rows : (d + 1) * rows, :] = value[b * rows : (b + 1) * rows, :]


def order_rows(value, blocks):
    rows = value.shape[0] // blocks
    if rows % 16 == 0:
        return value
    bits = blocks.bit_length() - 1
    split = value.reshape((2,) * bits + (rows, value.shape[1]))
    split = split.transpose(tuple(reversed(range(bits))) + (bits, bits + 1))
    return split.reshape(value.shape)


def call(body, name, out_shape, args, flops, grid=None, in_specs=None, out_specs=None, scalars=None, scratch=(), aliases=None):
    nbytes = sum(a.size * a.dtype.itemsize for a in args)
    nbytes += sum(o.size * o.dtype.itemsize for o in out_shape)
    if in_specs is None:
        in_specs = [whole(a.shape) for a in args]
    if out_specs is None:
        out_specs = [whole(o.shape) for o in out_shape]
    return pl.pallas_call(
        body,
        name=name,
        out_shape=out_shape,
        grid_spec=pltpu.PrefetchScalarGridSpec(
            num_scalar_prefetch=1,
            grid=grid or (1,),
            in_specs=in_specs,
            out_specs=out_specs,
            scratch_shapes=list(scratch),
        ),
        input_output_aliases=aliases or {},
        compiler_params=pltpu.CompilerParams(vmem_limit_bytes=LIMIT),
        cost_estimate=pl.CostEstimate(flops=flops, bytes_accessed=nbytes, transcendentals=0),
    )(scalars, *args)


def whole(shape):
    return pl.BlockSpec(shape, lambda *_: (0,) * len(shape))


def sds(shape, dtype):
    return jax.ShapeDtypeStruct(shape, dtype)


def chip_spec(shape):
    return pl.BlockSpec((None,) + tuple(shape[1:]), lambda i, sc: (sc[0], 0, 0))


def attention_kernel(sc, tok, gain, shift, w_ref, att_ref, lse_ref, normed):
    @pl.when(pl.program_id(0) == 0)
    def _():
        xhat, _ = normalize(tok[...].astype(F32))
        normed[...] = (xhat * gain[...] + shift[...]).astype(BF)

    seq = normed.shape[0]
    w = jnp.concatenate([w_ref[0], w_ref[1], w_ref[2]], axis=1)
    qkv = mm(normed[...], w).astype(BF)
    scale = HEAD_DIM**-0.5
    q = qkv[:, :PAIR] * jnp.asarray(scale, BF)
    k = qkv[:, PAIR : 2 * PAIR]
    vt = qkv[:, 2 * PAIR :].T
    lane = lax.broadcasted_iota(jnp.int32, (seq, PAIR), 1)
    visible = lax.broadcasted_iota(jnp.int32, (seq, 1), 0) < sc[1]
    outs = []
    for h in range(2):
        mine = (lane >= h * HEAD_DIM) & (lane < (h + 1) * HEAD_DIM)
        kh = jnp.where(mine, k, jnp.zeros_like(k))
        s = jnp.where(visible, mm_t(kh, q), -1e30)
        top = jnp.max(s, 0, keepdims=True)
        e = jnp.exp(s - top)
        total = jnp.sum(e, 0, keepdims=True)
        lse_ref[h : h + 1, :] = top + jnp.log(total)
        o = mm(vt[h * HEAD_DIM : (h + 1) * HEAD_DIM], e.astype(BF))
        outs.append(o / total)
    att_ref[...] = jnp.concatenate(outs, 0).T.astype(BF)
    lse_ref[2:8, :] = jnp.zeros((6, seq), F32)


def prepare_kernel(blocks, sc, tok, cot, gain, shift, n1, n1t, gm, gmt, vec):
    xhat, _ = normalize(tok[...].astype(F32))
    normed = (xhat * gain[...] + shift[...]).astype(BF)
    n1[...] = normed
    put_rows(n1t, normed.T, blocks)
    seq = normed.shape[0]
    visible = lax.broadcasted_iota(jnp.int32, (seq, 1), 0) < sc[1]
    g = jnp.where(visible, cot[...].astype(F32), 0.0)
    gl = g.astype(BF)
    gm[...] = gl
    put_rows(gmt, gl.T, blocks)
    vec[...] = jnp.broadcast_to(jnp.sum(g, 0, keepdims=True), vec.shape)


def project_kernel(blocks, sc, tok, att_a, att_b, wo_a, wo_b, b_out, gain, shift, resid, n2, n2t):
    x = tok[...].astype(F32)
    r = x + mm(att_a[...], wo_a[...]) + mm(att_b[...], wo_b[...]) + b_out[...]
    resid[...] = r
    xhat, _ = normalize(r)
    normed = (xhat * gain[...] + shift[...]).astype(BF)
    n2[...] = normed
    put_rows(n2t, normed.T, blocks)


def gelu_pair(u):
    z = jnp.abs(u)
    t = 1.0 / (1.0 + TAIL_P * z)
    poly = TAIL_C[-1]
    for c in TAIL_C[-2::-1]:
        poly = poly * t + c
    e = jnp.exp(-0.5 * u * u)
    tail = e * (poly * t)
    cdf = jnp.where(u < 0, tail, 1.0 - tail)
    return u * cdf, cdf + u * e * 0.3989422804014327


def mlp_kernel(tiles, first, cross, sc, *refs):
    n2, n2t, gm, gmt = refs[:4]
    wu = refs[4 : 4 + tiles]
    wd = refs[4 + tiles : 4 + 2 * tiles]
    bu = refs[4 + 2 * tiles]
    at = 5 + 2 * tiles
    if not first:
        macc_in, gacc_in, db_in = refs[at : at + 3]
        at += 3
    keep, send, macc, gacc, db = refs[at:]
    width = wu[0].shape[1]
    half = keep.shape[1]
    core = sc[0]
    db[...] = jnp.zeros_like(db) if first else db_in[...]
    for t in range(tiles):
        wut, wdt = wu[t][...], wd[t][...]
        u = mm(n2[...], wut) + bu[pl.ds(sc[1 + 2 * t], 1), :]
        act, slope = gelu_pair(u)
        act = act.astype(BF)
        gp = (mm_t(gm[...], wdt) * slope).astype(BF)
        db[pl.ds(sc[2 + 2 * t], 1), :] = jnp.sum(gp.astype(F32), 0, keepdims=True)
        m, g = mm(act, wdt), mm_t(gp, wut)
        if t == 0 and first:
            macc[...], gacc[...] = m, g
        elif t == 0:
            macc[...], gacc[...] = macc_in[...] + m, gacc_in[...] + g
        else:
            macc[...] += m
            gacc[...] += g
        for which, (lhs, rhs) in enumerate(((n2t, gp), (gmt, act))):
            grad = mm(lhs[...], rhs).astype(BF)
            top, low = grad[:half], grad[half:]
            other = (t ^ 1) if cross else t
            keep[which, :, t * width : (t + 1) * width] = jnp.where(core == 0, top, low)
            send[which, :, other * width : (other + 1) * width] = jnp.where(core == 0, low, top)


def middle_kernel(blocks, sc, resid, macc, gacc, gm, b_down, gain, out, gres, rl, rlt, vec):
    r = resid[...]
    seq = r.shape[0]
    visible = lax.broadcasted_iota(jnp.int32, (seq, 1), 0) < sc[1]
    out[...] = jnp.where(visible, r + macc[...] + b_down[...], 0.0).astype(BF)
    xhat, inv = normalize(r)
    gs = gacc[...]
    gr = gm[...].astype(F32) + norm_back(gs, xhat, inv, gain[...])
    gres[...] = gr
    low = gr.astype(BF)
    rl[...] = low
    put_rows(rlt, low.T, blocks)
    vec[0:1, :] = jnp.sum(gs * xhat, 0, keepdims=True)
    vec[1:2, :] = jnp.sum(gs, 0, keepdims=True)
    vec[2:3, :] = jnp.sum(gr, 0, keepdims=True)
    vec[3:8, :] = jnp.zeros((5, vec.shape[1]), F32)


def attention_back_kernel(first, sc, *refs):
    n1, n1t, rl, rlt, att, lse, w_ref, wo = refs[:8]
    at = 8
    if not first:
        gf_in = refs[at]
        at += 1
    keep, send, gf = refs[at:]
    seq = n1.shape[0]
    half = keep.shape[1]
    scale = HEAD_DIM**-0.5
    w = jnp.concatenate([w_ref[0], w_ref[1], w_ref[2]], axis=1)
    qkv = mm(n1[...], w).astype(BF)
    q, k, v = qkv[:, :PAIR], qkv[:, PAIR : 2 * PAIR], qkv[:, 2 * PAIR :]
    qs = q * jnp.asarray(scale, BF)
    ga = mm_t(rl[...], wo[...]).astype(BF)
    kt = k.T
    lane = lax.broadcasted_iota(jnp.int32, (seq, PAIR), 1)
    visible = lax.broadcasted_iota(jnp.int32, (seq, 1), 0) < sc[1]
    zero = jnp.zeros_like(q)
    dqt = []
    dk = jnp.zeros((seq, PAIR), F32)
    dv = jnp.zeros((seq, PAIR), F32)
    for h in range(2):
        mine = (lane >= h * HEAD_DIM) & (lane < (h + 1) * HEAD_DIM)
        s = jnp.where(visible, mm_t(jnp.where(mine, k, zero), qs), -1e30)
        p = jnp.exp(s - lse[h : h + 1, :])
        dp = mm_t(jnp.where(mine, v, zero), ga)
        row = jnp.sum(p * dp, 0, keepdims=True)
        ds = (p * (dp - row) * scale).astype(BF)
        dk += mm(ds, jnp.where(mine, q, zero))
        dv += mm(p.astype(BF), jnp.where(mine, ga, zero))
        dqt.append(mm(kt[h * HEAD_DIM : (h + 1) * HEAD_DIM], ds))
    dq = jnp.concatenate(dqt, 0).T
    d = jnp.concatenate([dq.astype(BF), dk.astype(BF), dv.astype(BF)], axis=1)
    g = mm_t(d, w)
    begin = pl.program_id(0) == 0

    @pl.when(begin)
    def _():
        gf[...] = g if first else gf_in[...] + g

    @pl.when(jnp.logical_not(begin))
    def _():
        gf[...] += g

    core = sc[0]
    dw = mm(n1t[...], d).astype(BF)
    dwo = mm(rlt[...], att[...]).astype(BF)
    parts = [dw[:, c * PAIR : (c + 1) * PAIR] for c in range(3)] + [dwo]
    for c, part in enumerate(parts):
        top, low = part[:half], part[half:]
        keep[c] = jnp.where(core == 0, top, low)
        send[c] = jnp.where(core == 0, low, top)


def last_kernel(sc, tok, gres, gf, gain, gt, gtl, vec):
    xhat, inv = normalize(tok[...].astype(F32))
    g = gf[...]
    out = gres[...] + norm_back(g, xhat, inv, gain[...])
    gt[...] = out
    gtl[...] = out.astype(BF)
    vec[0:1, :] = jnp.sum(g * xhat, 0, keepdims=True)
    vec[1:2, :] = jnp.sum(g, 0, keepdims=True)
    vec[2:8, :] = jnp.zeros((6, vec.shape[1]), F32)


def on_device(
    dp_n,
    mp_n,
    tokens,
    lengths,
    ln1_gain,
    ln1_shift,
    w_qkv,
    w_out,
    b_out,
    ln2_gain,
    ln2_shift,
    w_up,
    b_up,
    w_down,
    b_down,
    cotangent,
):
    chips, seq, width = tokens.shape
    feat = w_qkv.shape[2]
    hidden = w_up.shape[1]
    tile = hidden // 4
    pairs = feat // PAIR
    bits = dp_n.bit_length() - 1
    half = width // 2
    mp = lax.axis_index("mp")
    dp = lax.axis_index("dp")
    core = dp & 1
    two = dp & 3
    quarter = ((two & 1) << 1) | (two >> 1)
    i32 = jnp.int32

    def swap_y(x):
        return lax.ppermute(x, "mp", [(i, i ^ 1) for i in range(mp_n)])

    def swap_d(x, bit):
        return lax.ppermute(x, "dp", [(i, i ^ (1 << bit)) for i in range(dp_n)])

    own_sc = jnp.stack([mp, lengths[mp]]).astype(i32)
    peer_sc = jnp.stack([1 - mp, lengths[1 - mp]]).astype(i32)
    row = lambda v: v.reshape(1, -1)
    g1, s1, g2, s2, bo, bd = map(row, (ln1_gain, ln1_shift, ln2_gain, ln2_shift, b_out, b_down))

    hw = feat // 2
    wo_r0 = swap_y(lax.dynamic_slice_in_dim(w_out, core * hw, hw, 0))
    wo_r1 = swap_d(wo_r0, 0)
    wo_oth = jnp.where(core == 0, jnp.concatenate([wo_r0, wo_r1], 0), jnp.concatenate([wo_r1, wo_r0], 0))
    bu_own = b_up.reshape(4, tile)
    bu_oth = swap_y(bu_own)

    def attention(sc):
        return call(
            attention_kernel,
            "attention_fwd",
            [sds((seq, feat), BF), sds((pairs, 8, seq), F32)],
            [tokens, g1, s1, w_qkv],
            2 * seq * width * 3 * feat + 4 * seq * seq * feat,
            grid=(pairs,),
            in_specs=[
                chip_spec(tokens.shape),
                whole(g1.shape),
                whole(s1.shape),
                pl.BlockSpec((3, width, PAIR), lambda i, sc: (0, 0, i)),
            ],
            out_specs=[
                pl.BlockSpec((seq, PAIR), lambda i, sc: (0, i)),
                pl.BlockSpec((None, 8, seq), lambda i, sc: (i, 0, 0)),
            ],
            scalars=sc,
            scratch=[pltpu.VMEM((seq, width), BF)],
        )

    att_peer, lse_peer = attention(peer_sc)
    att_oth, lse_oth = swap_y(att_peer), swap_y(lse_peer)

    wu_r, wd_r = [None] * 4, [None] * 4
    for name, store, axis, src in (("u", wu_r, 1, w_up), ("d", wd_r, 0, w_down)):
        store[0] = swap_y(lax.dynamic_slice_in_dim(src, quarter * tile, tile, axis))
        store[1] = swap_d(store[0], 0)
        store[2] = swap_d(store[0], 1)
        store[3] = swap_d(store[2], 0)

    att_own, lse_own = attention(own_sc)

    n1, n1t, gm, gmt, vec_g = call(
        functools.partial(prepare_kernel, dp_n),
        "prepare",
        [sds((seq, width), BF), sds((width, seq), BF), sds((seq, width), BF), sds((width, seq), BF), sds((8, width), F32)],
        [tokens, cotangent, g1, s1],
        20 * seq * width,
        in_specs=[chip_spec(tokens.shape), chip_spec(cotangent.shape), whole(g1.shape), whole(s1.shape)],
        scalars=own_sc,
    )
    resid, n2, n2t = call(
        functools.partial(project_kernel, dp_n),
        "project",
        [sds((seq, width), F32), sds((seq, width), BF), sds((width, seq), BF)],
        [tokens, att_own, att_oth, w_out, wo_oth, bo, g2, s2],
        4 * seq * width * feat,
        in_specs=[chip_spec(tokens.shape)] + [whole(a.shape) for a in (att_own, att_oth, w_out, wo_oth, bo, g2, s2)],
        scalars=own_sc,
    )
    n1t, gmt, n2t = (order_rows(t, dp_n) for t in (n1t, gmt, n2t))

    own_half, oth_half = mp * 4, (1 - mp) * 4

    def mlp(first, cross, wus, wds, bias, slots, base, accs, specs):
        sc = [core]
        for a in slots:
            sc += [a, base + a]
        outs = [
            sds((2, half, 2 * tile), BF),
            sds((2, half, 2 * tile), BF),
            sds((seq, width), F32),
            sds((seq, width), F32),
            sds((8, tile), F32),
        ]
        args = [n2, n2t, gm, gmt, *wus, *wds, bias, *accs]
        in_specs = [whole(a.shape) for a in args]
        if specs:
            in_specs[4:8] = specs
        return call(
            functools.partial(mlp_kernel, 2, first, cross),
            "mlp_tiles",
            outs,
            args,
            12 * seq * width * 2 * tile,
            in_specs=in_specs,
            scalars=jnp.stack(sc).astype(i32),
            aliases={} if first else {10: 2, 11: 3, 12: 4},
        )

    def own_specs(a):
        return [pl.BlockSpec((width, tile), lambda i, sc, t=t: (0, t)) for t in (a, a + 1)] + [
            pl.BlockSpec((tile, width), lambda i, sc, t=t: (t, 0)) for t in (a, a + 1)
        ]

    pieces = []
    accs = []
    const = lambda v: jnp.asarray(v, i32)
    for a in (0, 2):
        k, s, *accs = mlp(
            a == 0, False, [w_up] * 2, [w_down] * 2, bu_own, [const(a), const(a + 1)], own_half, accs, own_specs(a)
        )
        pieces.append((k, s))
    mine = [quarter, quarter ^ 2, quarter ^ 1, quarter ^ 3]
    for a in (0, 2):
        k, s, *accs = mlp(
            False, True, wu_r[a : a + 2], wd_r[a : a + 2], bu_oth, mine[a : a + 2], oth_half, accs, None
        )
        pieces.append((k, s))
    macc, gacc, db = accs

    out_own, gres, rl, rlt, vec_mid = call(
        functools.partial(middle_kernel, dp_n),
        "middle",
        [sds((seq, width), BF), sds((seq, width), F32), sds((seq, width), BF), sds((width, seq), BF), sds((8, width), F32)],
        [resid, macc, gacc, gm, bd, g2],
        40 * seq * width,
        scalars=own_sc,
    )
    out_oth = swap_y(out_own)
    rlt = order_rows(rlt, dp_n)

    hq = width // 4
    wq_r = [None] * 4
    wq_r[0] = swap_y(lax.dynamic_slice_in_dim(w_qkv, quarter * hq, hq, 1))
    wq_r[1] = swap_d(wq_r[0], 0)
    wq_r[2] = swap_d(wq_r[0], 1)
    wq_r[3] = swap_d(wq_r[2], 0)
    wq_oth = jnp.concatenate(wq_r, 1)
    for r in range(4):
        wq_oth = lax.dynamic_update_slice_in_dim(wq_oth, wq_r[r], mine[r] * hq, 1)

    def attention_back(first, wq, wo, att, lse, accs):
        args = [n1, n1t, rl, rlt, att, lse, wq, wo, *accs]
        in_specs = [whole(a.shape) for a in args]
        in_specs[4] = pl.BlockSpec((seq, PAIR), lambda i, sc: (0, i))
        in_specs[5] = pl.BlockSpec((None, 8, seq), lambda i, sc: (i, 0, 0))
        in_specs[6] = pl.BlockSpec((3, width, PAIR), lambda i, sc: (0, 0, i))
        in_specs[7] = pl.BlockSpec((PAIR, width), lambda i, sc: (i, 0))
        piece = pl.BlockSpec((4, half, PAIR), lambda i, sc: (0, 0, i))
        return call(
            functools.partial(attention_back_kernel, first),
            "attention_bwd",
            [sds((4, half, feat), BF), sds((4, half, feat), BF), sds((seq, width), F32)],
            args,
            2 * seq * width * feat * 11 + 10 * seq * seq * feat,
            grid=(pairs,),
            in_specs=in_specs,
            out_specs=[piece, piece, whole((seq, width))],
            scalars=jnp.stack([core, own_sc[1]]).astype(i32),
            aliases={} if first else {9: 2},
        )

    k, s, gf = attention_back(True, w_qkv, w_out, att_own, lse_own, [])
    pieces.append((k, s))
    k, s, gf = attention_back(False, wq_oth, wo_oth, att_oth, lse_oth, [gf])
    pieces.append((k, s))

    gt_own, gt_low, vec_last = call(
        last_kernel,
        "last",
        [sds((seq, width), F32), sds((seq, width), BF), sds((8, width), F32)],
        [tokens, gres, gf, g1],
        30 * seq * width,
        in_specs=[chip_spec(tokens.shape)] + [whole(a.shape) for a in (gres, gf, g1)],
        scalars=own_sc,
    )
    gt_oth = swap_y(gt_low).astype(F32)

    def add(a, b):
        return (a.astype(F32) + b.astype(F32)).astype(BF)

    def split(x, bit):
        n = x.shape[1] // 2
        b = (dp >> bit) & 1
        return (
            lax.dynamic_slice_in_dim(x, b * n, n, 1),
            lax.dynamic_slice_in_dim(x, (1 - b) * n, n, 1),
        )

    state = [add(k, swap_d(s, 0)) for k, s in pieces]
    for bit in range(1, bits):
        parts = [split(x, bit) for x in state]
        got = [swap_d(s, bit) for _, s in parts]
        if bit == 1:
            got[2], got[3] = got[3], got[2]
        state = [add(p[0], g) for p, g in zip(parts, got)]
    own1, own2, oth1, oth2, at_own, at_oth = state
    rows = own1.shape[1]
    got1, got2, got_at = swap_y(oth1), swap_y(oth2), swap_y(at_oth)

    slots = jnp.stack([got1[..., :tile], got1[..., tile:], got2[..., :tile], got2[..., tile:]])
    got = [lax.dynamic_index_in_dim(slots, slot_of(a, two), 0, keepdims=False) for a in range(4)]
    mine_mlp = [own1[..., :tile], own1[..., tile:], own2[..., :tile], own2[..., tile:]]
    total = jnp.concatenate([m.astype(F32) + g.astype(F32) for m, g in zip(mine_mlp, got)], -1)
    total_at = at_own.astype(F32) + got_at.astype(F32)

    vecs = jnp.concatenate([vec_g[:1], vec_mid[:3], vec_last[:2], db.reshape(-1, width)], 0)
    for bit in range(bits):
        vecs = vecs + swap_d(vecs, bit)
    vecs = vecs + swap_y(vecs)
    shard = lax.dynamic_slice_in_dim(vecs[:6], dp * rows, rows, 1)
    bias = vecs[6:].reshape(mp_n, hidden)
    cols = hidden // dp_n
    bias = lax.dynamic_slice(bias, (mp, dp * cols), (1, cols))

    def both(own, oth):
        return jnp.where(mp == 0, jnp.stack([own, oth]), jnp.stack([oth, own]))

    return (
        both(out_own, out_oth),
        both(gt_own, gt_oth),
        shard[4],
        shard[5],
        total_at[:3],
        total_at[3].T,
        shard[3],
        shard[1],
        shard[2],
        total[0],
        bias,
        total[1].T,
        shard[0],
    )


def slot_of(a, two):
    q = ((two & 1) << 1) | (two >> 1)
    d = q ^ a
    return ((d & 1) << 1) | (d >> 1)


def solution(mesh):
    return jax.shard_map(
        functools.partial(on_device, mesh.shape["dp"], mesh.shape["mp"]),
        mesh=mesh,
        in_specs=(
            P("dp", None, None),
            P("dp"),
            P(),
            P(),
            P(None, None, "mp"),
            P("mp", None),
            P(),
            P(),
            P(),
            P(None, "mp"),
            P("mp"),
            P("mp", None),
            P(),
            P("dp", None, None),
        ),
        out_specs=(
            P("dp", None, None),
            P("dp", None, None),
            P("dp"),
            P("dp"),
            P(None, "dp", "mp"),
            P("mp", "dp"),
            P("dp"),
            P("dp"),
            P("dp"),
            P("dp", "mp"),
            P("mp", "dp"),
            P("mp", "dp"),
            P("dp"),
        ),
        check_vma=False,
    )
```

```python
import functools

import jax
import jax.numpy as jnp
from jax import lax
from jax.experimental import pallas as pl
from jax.experimental.pallas import tpu as pltpu
from jax.sharding import PartitionSpec as P

HEAD_DIM = 64
PAIR = 2 * HEAD_DIM
BF = jnp.bfloat16
F32 = jnp.float32
EPS = 1e-05
LIMIT = 40 * 1024 * 1024

TAIL_P = 0.3
TAIL_C = (
    0.11962929256864907,
    0.12075406313917503,
    0.09991275007605285,
    0.12856432480895655,
    -0.05368921426491713,
    0.2063600527786208,
    -0.1572071533588575,
    0.03567581131365836,
)


def mm(a, b):
    return lax.dot_general(a, b, (((1,), (0,)), ((), ())), preferred_element_type=F32)


def mm_t(a, b):
    return lax.dot_general(a, b, (((1,), (1,)), ((), ())), preferred_element_type=F32)


def normalize(x):
    mean = jnp.mean(x, -1, keepdims=True)
    center = x - mean
    var = jnp.mean(center * center, -1, keepdims=True)
    inv = lax.rsqrt(var + EPS)
    return center * inv, inv


def norm_back(grad, xhat, inv, gain):
    d = grad * gain
    m1 = jnp.mean(d, -1, keepdims=True)
    m2 = jnp.mean(d * xhat, -1, keepdims=True)
    return inv * (d - m1 - xhat * m2)


def bit_reverse(index, bits):
    out = 0
    for b in range(bits):
        out = (out << 1) | ((index >> b) & 1)
    return out


def put_rows(ref, value, blocks):
    rows = value.shape[0] // blocks
    bits = blocks.bit_length() - 1
    if rows % 16:
        ref[...] = value
        return
    for b in range(blocks):
        d = bit_reverse(b, bits)
        ref[d * rows : (d + 1) * rows, :] = value[b * rows : (b + 1) * rows, :]


def order_rows(value, blocks):
    rows = value.shape[0] // blocks
    if rows % 16 == 0:
        return value
    bits = blocks.bit_length() - 1
    split = value.reshape((2,) * bits + (rows, value.shape[1]))
    split = split.transpose(tuple(reversed(range(bits))) + (bits, bits + 1))
    return split.reshape(value.shape)


def call(body, name, out_shape, args, flops, grid=None, in_specs=None, out_specs=None, scalars=None, scratch=(), aliases=None):
    nbytes = sum(a.size * a.dtype.itemsize for a in args)
    nbytes += sum(o.size * o.dtype.itemsize for o in out_shape)
    if in_specs is None:
        in_specs = [whole(a.shape) for a in args]
    if out_specs is None:
        out_specs = [whole(o.shape) for o in out_shape]
    return pl.pallas_call(
        body,
        name=name,
        out_shape=out_shape,
        grid_spec=pltpu.PrefetchScalarGridSpec(
            num_scalar_prefetch=1,
            grid=grid or (1,),
            in_specs=in_specs,
            out_specs=out_specs,
            scratch_shapes=list(scratch),
        ),
        input_output_aliases=aliases or {},
        compiler_params=pltpu.CompilerParams(vmem_limit_bytes=LIMIT),
        cost_estimate=pl.CostEstimate(flops=flops, bytes_accessed=nbytes, transcendentals=0),
    )(scalars, *args)


def whole(shape):
    return pl.BlockSpec(shape, lambda *_: (0,) * len(shape))


def sds(shape, dtype):
    return jax.ShapeDtypeStruct(shape, dtype)


def chip_spec(shape):
    return pl.BlockSpec((None,) + tuple(shape[1:]), lambda i, sc: (sc[0], 0, 0))


def attention_kernel(sc, tok, gain, shift, w_ref, att_ref, lse_ref, normed):
    @pl.when(pl.program_id(0) == 0)
    def _():
        xhat, _ = normalize(tok[...].astype(F32))
        normed[...] = (xhat * gain[...] + shift[...]).astype(BF)

    seq = normed.shape[0]
    w = jnp.concatenate([w_ref[0], w_ref[1], w_ref[2]], axis=1)
    qkv = mm(normed[...], w).astype(BF)
    scale = HEAD_DIM**-0.5
    q = qkv[:, :PAIR] * jnp.asarray(scale, BF)
    k = qkv[:, PAIR : 2 * PAIR]
    vt = qkv[:, 2 * PAIR :].T
    lane = lax.broadcasted_iota(jnp.int32, (seq, PAIR), 1)
    visible = lax.broadcasted_iota(jnp.int32, (seq, 1), 0) < sc[1]
    outs = []
    for h in range(2):
        mine = (lane >= h * HEAD_DIM) & (lane < (h + 1) * HEAD_DIM)
        kh = jnp.where(mine, k, jnp.zeros_like(k))
        s = jnp.where(visible, mm_t(kh, q), -1e30)
        top = jnp.max(s, 0, keepdims=True)
        e = jnp.exp(s - top)
        total = jnp.sum(e, 0, keepdims=True)
        lse_ref[h : h + 1, :] = top + jnp.log(total)
        o = mm(vt[h * HEAD_DIM : (h + 1) * HEAD_DIM], e.astype(BF))
        outs.append(o / total)
    att_ref[...] = jnp.concatenate(outs, 0).T.astype(BF)
    lse_ref[2:8, :] = jnp.zeros((6, seq), F32)


def prepare_kernel(blocks, sc, tok, cot, gain, shift, n1, n1t, gm, gmt, vec):
    xhat, _ = normalize(tok[...].astype(F32))
    normed = (xhat * gain[...] + shift[...]).astype(BF)
    n1[...] = normed
    put_rows(n1t, normed.T, blocks)
    seq = normed.shape[0]
    visible = lax.broadcasted_iota(jnp.int32, (seq, 1), 0) < sc[1]
    g = jnp.where(visible, cot[...].astype(F32), 0.0)
    gl = g.astype(BF)
    gm[...] = gl
    put_rows(gmt, gl.T, blocks)
    vec[...] = jnp.broadcast_to(jnp.sum(g, 0, keepdims=True), vec.shape)


def project_kernel(blocks, sc, tok, att_a, att_b, wo_a, wo_b, b_out, gain, shift, resid, n2, n2t):
    x = tok[...].astype(F32)
    r = x + mm(att_a[...], wo_a[...]) + mm(att_b[...], wo_b[...]) + b_out[...]
    resid[...] = r
    xhat, _ = normalize(r)
    normed = (xhat * gain[...] + shift[...]).astype(BF)
    n2[...] = normed
    put_rows(n2t, normed.T, blocks)


def gelu_pair(u):
    z = jnp.abs(u)
    t = 1.0 / (1.0 + TAIL_P * z)
    poly = TAIL_C[-1]
    for c in TAIL_C[-2::-1]:
        poly = poly * t + c
    e = jnp.exp(-0.5 * u * u)
    tail = e * (poly * t)
    cdf = jnp.where(u < 0, tail, 1.0 - tail)
    return u * cdf, cdf + u * e * 0.3989422804014327


def mlp_kernel(tiles, first, cross, sc, *refs):
    n2, n2t, gm, gmt = refs[:4]
    wu = refs[4 : 4 + tiles]
    wd = refs[4 + tiles : 4 + 2 * tiles]
    bu = refs[4 + 2 * tiles]
    at = 5 + 2 * tiles
    if not first:
        macc_in, gacc_in, db_in = refs[at : at + 3]
        at += 3
    keep, send, macc, gacc, db = refs[at:]
    width = wu[0].shape[1]
    half = keep.shape[1]
    core = sc[0]
    db[...] = jnp.zeros_like(db) if first else db_in[...]
    for t in range(tiles):
        wut, wdt = wu[t][...], wd[t][...]
        u = mm(n2[...], wut) + bu[pl.ds(sc[1 + 2 * t], 1), :]
        act, slope = gelu_pair(u)
        act = act.astype(BF)
        gp = (mm_t(gm[...], wdt) * slope).astype(BF)
        db[pl.ds(sc[2 + 2 * t], 1), :] = jnp.sum(gp.astype(F32), 0, keepdims=True)
        m, g = mm(act, wdt), mm_t(gp, wut)
        if t == 0 and first:
            macc[...], gacc[...] = m, g
        elif t == 0:
            macc[...], gacc[...] = macc_in[...] + m, gacc_in[...] + g
        else:
            macc[...] += m
            gacc[...] += g
        for which, (lhs, rhs) in enumerate(((n2t, gp), (gmt, act))):
            grad = mm(lhs[...], rhs).astype(BF)
            top, low = grad[:half], grad[half:]
            other = (t ^ 1) if cross else t
            keep[which, :, t * width : (t + 1) * width] = jnp.where(core == 0, top, low)
            send[which, :, other * width : (other + 1) * width] = jnp.where(core == 0, low, top)


def middle_kernel(blocks, sc, resid, macc, gacc, gm, b_down, gain, out, gres, rl, rlt, vec):
    r = resid[...]
    seq = r.shape[0]
    visible = lax.broadcasted_iota(jnp.int32, (seq, 1), 0) < sc[1]
    out[...] = jnp.where(visible, r + macc[...] + b_down[...], 0.0).astype(BF)
    xhat, inv = normalize(r)
    gs = gacc[...]
    gr = gm[...].astype(F32) + norm_back(gs, xhat, inv, gain[...])
    gres[...] = gr
    low = gr.astype(BF)
    rl[...] = low
    put_rows(rlt, low.T, blocks)
    vec[0:1, :] = jnp.sum(gs * xhat, 0, keepdims=True)
    vec[1:2, :] = jnp.sum(gs, 0, keepdims=True)
    vec[2:3, :] = jnp.sum(gr, 0, keepdims=True)
    vec[3:8, :] = jnp.zeros((5, vec.shape[1]), F32)


def attention_back_kernel(first, sc, *refs):
    n1, n1t, rl, rlt, att, lse, w_ref, wo = refs[:8]
    at = 8
    if not first:
        gf_in = refs[at]
        at += 1
    keep, send, gf = refs[at:]
    seq = n1.shape[0]
    half = keep.shape[1]
    scale = HEAD_DIM**-0.5
    w = jnp.concatenate([w_ref[0], w_ref[1], w_ref[2]], axis=1)
    qkv = mm(n1[...], w).astype(BF)
    q, k, v = qkv[:, :PAIR], qkv[:, PAIR : 2 * PAIR], qkv[:, 2 * PAIR :]
    qs = q * jnp.asarray(scale, BF)
    ga = mm_t(rl[...], wo[...]).astype(BF)
    kt = k.T
    lane = lax.broadcasted_iota(jnp.int32, (seq, PAIR), 1)
    visible = lax.broadcasted_iota(jnp.int32, (seq, 1), 0) < sc[1]
    zero = jnp.zeros_like(q)
    dqt = []
    dk = jnp.zeros((seq, PAIR), F32)
    dv = jnp.zeros((seq, PAIR), F32)
    for h in range(2):
        mine = (lane >= h * HEAD_DIM) & (lane < (h + 1) * HEAD_DIM)
        s = jnp.where(visible, mm_t(jnp.where(mine, k, zero), qs), -1e30)
        p = jnp.exp(s - lse[h : h + 1, :])
        dp = mm_t(jnp.where(mine, v, zero), ga)
        row = jnp.sum(p * dp, 0, keepdims=True)
        ds = (p * (dp - row) * scale).astype(BF)
        dk += mm(ds, jnp.where(mine, q, zero))
        dv += mm(p.astype(BF), jnp.where(mine, ga, zero))
        dqt.append(mm(kt[h * HEAD_DIM : (h + 1) * HEAD_DIM], ds))
    dq = jnp.concatenate(dqt, 0).T
    d = jnp.concatenate([dq.astype(BF), dk.astype(BF), dv.astype(BF)], axis=1)
    g = mm_t(d, w)
    begin = pl.program_id(0) == 0

    @pl.when(begin)
    def _():
        gf[...] = g if first else gf_in[...] + g

    @pl.when(jnp.logical_not(begin))
    def _():
        gf[...] += g

    core = sc[0]
    dw = mm(n1t[...], d).astype(BF)
    dwo = mm(rlt[...], att[...]).astype(BF)
    parts = [dw[:, c * PAIR : (c + 1) * PAIR] for c in range(3)] + [dwo]
    for c, part in enumerate(parts):
        top, low = part[:half], part[half:]
        keep[c] = jnp.where(core == 0, top, low)
        send[c] = jnp.where(core == 0, low, top)


def last_kernel(sc, tok, gres, gf, gain, gt, gtl, vec):
    xhat, inv = normalize(tok[...].astype(F32))
    g = gf[...]
    out = gres[...] + norm_back(g, xhat, inv, gain[...])
    gt[...] = out
    gtl[...] = out.astype(BF)
    vec[0:1, :] = jnp.sum(g * xhat, 0, keepdims=True)
    vec[1:2, :] = jnp.sum(g, 0, keepdims=True)
    vec[2:8, :] = jnp.zeros((6, vec.shape[1]), F32)


def permute_program(
    dp_n,
    mp_n,
    tokens,
    lengths,
    ln1_gain,
    ln1_shift,
    w_qkv,
    w_out,
    b_out,
    ln2_gain,
    ln2_shift,
    w_up,
    b_up,
    w_down,
    b_down,
    cotangent,
):
    chips, seq, width = tokens.shape
    feat = w_qkv.shape[2]
    hidden = w_up.shape[1]
    tile = hidden // 4
    pairs = feat // PAIR
    bits = dp_n.bit_length() - 1
    half = width // 2
    mp = lax.axis_index("mp")
    dp = lax.axis_index("dp")
    core = dp & 1
    two = dp & 3
    quarter = ((two & 1) << 1) | (two >> 1)
    i32 = jnp.int32

    def swap_y(x):
        return lax.ppermute(x, "mp", [(i, i ^ 1) for i in range(mp_n)])

    def swap_d(x, bit):
        return lax.ppermute(x, "dp", [(i, i ^ (1 << bit)) for i in range(dp_n)])

    own_sc = jnp.stack([mp, lengths[mp]]).astype(i32)
    peer_sc = jnp.stack([1 - mp, lengths[1 - mp]]).astype(i32)
    row = lambda v: v.reshape(1, -1)
    g1, s1, g2, s2, bo, bd = map(row, (ln1_gain, ln1_shift, ln2_gain, ln2_shift, b_out, b_down))

    hw = feat // 2
    wo_r0 = swap_y(lax.dynamic_slice_in_dim(w_out, core * hw, hw, 0))
    wo_r1 = swap_d(wo_r0, 0)
    wo_oth = jnp.where(core == 0, jnp.concatenate([wo_r0, wo_r1], 0), jnp.concatenate([wo_r1, wo_r0], 0))
    bu_own = b_up.reshape(4, tile)
    bu_oth = swap_y(bu_own)

    def attention(sc):
        return call(
            attention_kernel,
            "attention_fwd",
            [sds((seq, feat), BF), sds((pairs, 8, seq), F32)],
            [tokens, g1, s1, w_qkv],
            2 * seq * width * 3 * feat + 4 * seq * seq * feat,
            grid=(pairs,),
            in_specs=[
                chip_spec(tokens.shape),
                whole(g1.shape),
                whole(s1.shape),
                pl.BlockSpec((3, width, PAIR), lambda i, sc: (0, 0, i)),
            ],
            out_specs=[
                pl.BlockSpec((seq, PAIR), lambda i, sc: (0, i)),
                pl.BlockSpec((None, 8, seq), lambda i, sc: (i, 0, 0)),
            ],
            scalars=sc,
            scratch=[pltpu.VMEM((seq, width), BF)],
        )

    att_peer, lse_peer = attention(peer_sc)
    att_oth, lse_oth = swap_y(att_peer), swap_y(lse_peer)

    wu_r, wd_r = [None] * 4, [None] * 4
    for name, store, axis, src in (("u", wu_r, 1, w_up), ("d", wd_r, 0, w_down)):
        store[0] = swap_y(lax.dynamic_slice_in_dim(src, quarter * tile, tile, axis))
        store[1] = swap_d(store[0], 0)
        store[2] = swap_d(store[0], 1)
        store[3] = swap_d(store[2], 0)

    att_own, lse_own = attention(own_sc)

    n1, n1t, gm, gmt, vec_g = call(
        functools.partial(prepare_kernel, dp_n),
        "prepare",
        [sds((seq, width), BF), sds((width, seq), BF), sds((seq, width), BF), sds((width, seq), BF), sds((8, width), F32)],
        [tokens, cotangent, g1, s1],
        20 * seq * width,
        in_specs=[chip_spec(tokens.shape), chip_spec(cotangent.shape), whole(g1.shape), whole(s1.shape)],
        scalars=own_sc,
    )
    resid, n2, n2t = call(
        functools.partial(project_kernel, dp_n),
        "project",
        [sds((seq, width), F32), sds((seq, width), BF), sds((width, seq), BF)],
        [tokens, att_own, att_oth, w_out, wo_oth, bo, g2, s2],
        4 * seq * width * feat,
        in_specs=[chip_spec(tokens.shape)] + [whole(a.shape) for a in (att_own, att_oth, w_out, wo_oth, bo, g2, s2)],
        scalars=own_sc,
    )
    n1t, gmt, n2t = (order_rows(t, dp_n) for t in (n1t, gmt, n2t))

    own_half, oth_half = mp * 4, (1 - mp) * 4

    def mlp(first, cross, wus, wds, bias, slots, base, accs, specs):
        sc = [core]
        for a in slots:
            sc += [a, base + a]
        outs = [
            sds((2, half, 2 * tile), BF),
            sds((2, half, 2 * tile), BF),
            sds((seq, width), F32),
            sds((seq, width), F32),
            sds((8, tile), F32),
        ]
        args = [n2, n2t, gm, gmt, *wus, *wds, bias, *accs]
        in_specs = [whole(a.shape) for a in args]
        if specs:
            in_specs[4:8] = specs
        return call(
            functools.partial(mlp_kernel, 2, first, cross),
            "mlp_tiles",
            outs,
            args,
            12 * seq * width * 2 * tile,
            in_specs=in_specs,
            scalars=jnp.stack(sc).astype(i32),
            aliases={} if first else {10: 2, 11: 3, 12: 4},
        )

    def own_specs(a):
        return [pl.BlockSpec((width, tile), lambda i, sc, t=t: (0, t)) for t in (a, a + 1)] + [
            pl.BlockSpec((tile, width), lambda i, sc, t=t: (t, 0)) for t in (a, a + 1)
        ]

    pieces = []
    accs = []
    const = lambda v: jnp.asarray(v, i32)
    for a in (0, 2):
        k, s, *accs = mlp(
            a == 0, False, [w_up] * 2, [w_down] * 2, bu_own, [const(a), const(a + 1)], own_half, accs, own_specs(a)
        )
        pieces.append((k, s))
    mine = [quarter, quarter ^ 2, quarter ^ 1, quarter ^ 3]
    for a in (0, 2):
        k, s, *accs = mlp(
            False, True, wu_r[a : a + 2], wd_r[a : a + 2], bu_oth, mine[a : a + 2], oth_half, accs, None
        )
        pieces.append((k, s))
    macc, gacc, db = accs

    out_own, gres, rl, rlt, vec_mid = call(
        functools.partial(middle_kernel, dp_n),
        "middle",
        [sds((seq, width), BF), sds((seq, width), F32), sds((seq, width), BF), sds((width, seq), BF), sds((8, width), F32)],
        [resid, macc, gacc, gm, bd, g2],
        40 * seq * width,
        scalars=own_sc,
    )
    out_oth = swap_y(out_own)
    rlt = order_rows(rlt, dp_n)

    hq = width // 4
    wq_r = [None] * 4
    wq_r[0] = swap_y(lax.dynamic_slice_in_dim(w_qkv, quarter * hq, hq, 1))
    wq_r[1] = swap_d(wq_r[0], 0)
    wq_r[2] = swap_d(wq_r[0], 1)
    wq_r[3] = swap_d(wq_r[2], 0)
    wq_oth = jnp.concatenate(wq_r, 1)
    for r in range(4):
        wq_oth = lax.dynamic_update_slice_in_dim(wq_oth, wq_r[r], mine[r] * hq, 1)

    def attention_back(first, wq, wo, att, lse, accs):
        args = [n1, n1t, rl, rlt, att, lse, wq, wo, *accs]
        in_specs = [whole(a.shape) for a in args]
        in_specs[4] = pl.BlockSpec((seq, PAIR), lambda i, sc: (0, i))
        in_specs[5] = pl.BlockSpec((None, 8, seq), lambda i, sc: (i, 0, 0))
        in_specs[6] = pl.BlockSpec((3, width, PAIR), lambda i, sc: (0, 0, i))
        in_specs[7] = pl.BlockSpec((PAIR, width), lambda i, sc: (i, 0))
        piece = pl.BlockSpec((4, half, PAIR), lambda i, sc: (0, 0, i))
        return call(
            functools.partial(attention_back_kernel, first),
            "attention_bwd",
            [sds((4, half, feat), BF), sds((4, half, feat), BF), sds((seq, width), F32)],
            args,
            2 * seq * width * feat * 11 + 10 * seq * seq * feat,
            grid=(pairs,),
            in_specs=in_specs,
            out_specs=[piece, piece, whole((seq, width))],
            scalars=jnp.stack([core, own_sc[1]]).astype(i32),
            aliases={} if first else {9: 2},
        )

    k, s, gf = attention_back(True, w_qkv, w_out, att_own, lse_own, [])
    pieces.append((k, s))
    k, s, gf = attention_back(False, wq_oth, wo_oth, att_oth, lse_oth, [gf])
    pieces.append((k, s))

    gt_own, gt_low, vec_last = call(
        last_kernel,
        "last",
        [sds((seq, width), F32), sds((seq, width), BF), sds((8, width), F32)],
        [tokens, gres, gf, g1],
        30 * seq * width,
        in_specs=[chip_spec(tokens.shape)] + [whole(a.shape) for a in (gres, gf, g1)],
        scalars=own_sc,
    )
    gt_oth = swap_y(gt_low).astype(F32)

    def add(a, b):
        return (a.astype(F32) + b.astype(F32)).astype(BF)

    def split(x, bit):
        n = x.shape[1] // 2
        b = (dp >> bit) & 1
        return (
            lax.dynamic_slice_in_dim(x, b * n, n, 1),
            lax.dynamic_slice_in_dim(x, (1 - b) * n, n, 1),
        )

    state = [add(k, swap_d(s, 0)) for k, s in pieces]
    for bit in range(1, bits):
        parts = [split(x, bit) for x in state]
        got = [swap_d(s, bit) for _, s in parts]
        if bit == 1:
            got[2], got[3] = got[3], got[2]
        state = [add(p[0], g) for p, g in zip(parts, got)]
    own1, own2, oth1, oth2, at_own, at_oth = state
    rows = own1.shape[1]
    got1, got2, got_at = swap_y(oth1), swap_y(oth2), swap_y(at_oth)

    slots = jnp.stack([got1[..., :tile], got1[..., tile:], got2[..., :tile], got2[..., tile:]])
    got = [lax.dynamic_index_in_dim(slots, slot_of(a, two), 0, keepdims=False) for a in range(4)]
    mine_mlp = [own1[..., :tile], own1[..., tile:], own2[..., :tile], own2[..., tile:]]
    total = jnp.concatenate([m.astype(F32) + g.astype(F32) for m, g in zip(mine_mlp, got)], -1)
    total_at = at_own.astype(F32) + got_at.astype(F32)

    vecs = jnp.concatenate([vec_g[:1], vec_mid[:3], vec_last[:2], db.reshape(-1, width)], 0)
    for bit in range(bits):
        vecs = vecs + swap_d(vecs, bit)
    vecs = vecs + swap_y(vecs)
    shard = lax.dynamic_slice_in_dim(vecs[:6], dp * rows, rows, 1)
    bias = vecs[6:].reshape(mp_n, hidden)
    cols = hidden // dp_n
    bias = lax.dynamic_slice(bias, (mp, dp * cols), (1, cols))

    def both(own, oth):
        return jnp.where(mp == 0, jnp.stack([own, oth]), jnp.stack([oth, own]))

    return (
        both(out_own, out_oth),
        both(gt_own, gt_oth),
        shard[4],
        shard[5],
        total_at[:3],
        total_at[3].T,
        shard[3],
        shard[1],
        shard[2],
        total[0],
        bias,
        total[1].T,
        shard[0],
    )


def slot_of(a, two):
    q = ((two & 1) << 1) | (two >> 1)
    d = q ^ a
    return ((d & 1) << 1) | (d >> 1)


MESH = pl.DeviceIdType.MESH
ROWS = 48
VMEM_ALL = 67043328


def block_order(order):
    places = []
    for b in range(16):
        p = 0
        for bit in order:
            p = p * 2 + ((b >> bit) & 1)
        places.append(p)
    return places


MLP_ORDER = block_order((0, 1, 2, 3))
ATT_ORDER = block_order((0, 2, 3, 1))


def place_rows(ref, value, places):
    for b, p in enumerate(places):
        ref[p * ROWS : (p + 1) * ROWS, :] = value[b * ROWS : (b + 1) * ROWS, :]


def aligned(v, n):
    return pl.multiple_of(v, n)


def layer_kernel(
    lens, tok_h, cot_h, g1, s1, g2, s2, b_out, b_down, bu, wq_h, wo_h, wu_h, wd_h,
    out_h, gt_h, d_qkv, d_out, d_up, d_down, vec_out,
    tok, n1, n1t, gm, gmt, n2, n2t, resid, macc, gacc, att, lse, wq, wo, wu, wd, bu_oth,
    grad, rc, rx, rz, rw, ry, ac, az, aw, ax, ay, ob, gl, gr, vs, vr,
    loc, agl_s, agl_r, att_s, att_r, m_s, m_r, a_s, a_r, e_s, e_r, o_sem,
):
    dp, mp = lax.axis_index("dp"), lax.axis_index("mp")
    core, x, z0, z1 = dp % 2, (dp // 2) % 2, (dp // 4) % 2, dp // 8
    to_c = (dp + 1 - 2 * core, mp)
    to_x = (dp + 2 - 4 * x, mp)
    to_z = (dp + 4 - 8 * z0, mp)
    to_w = (dp + 8 - 16 * z1, mp)
    to_y = (dp, 1 - mp)
    quarter = core * 2 + z0
    seq, width = n1.shape

    def remote(src, dst, ss, rs, dev):
        return pltpu.make_async_remote_copy(
            src_ref=src, dst_ref=dst, send_sem=ss, recv_sem=rs, device_id=dev, device_id_type=MESH
        )

    def arrived(dst, rs, dev):
        remote(dst, dst, rs, rs, dev).wait_recv()

    def sent(src, ss, dev):
        remote(src, src, ss, ss, dev).wait_send()

    def local(src, dst, sem):
        return pltpu.make_async_copy(src, dst, sem)

    peer_tok = local(tok_h.at[1 - mp], tok.at[0], loc.at[0])
    own_tok = local(tok_h.at[mp], tok.at[1], loc.at[1])
    cot = local(cot_h.at[mp], gm, loc.at[2])
    wq_in = [local(wq_h.at[:, :, pl.ds(p * PAIR, PAIR)], wq.at[pl.ds(3 * p, 3)], loc.at[3 + p]) for p in range(3)]
    wo_in = local(wo_h, wo.at[pl.ds(0, 3)], loc.at[6])
    wu_in = [local(wu_h.at[:, pl.ds(j * PAIR, PAIR)], wu.at[j], loc.at[7 + j]) for j in range(12)]
    wd_in = local(wd_h, wd.at[pl.ds(0, 4)], loc.at[19])
    for c in [peer_tok, wq_in[0], wq_in[1], wq_in[2], own_tok, cot, wo_in] + wu_in + [wd_in]:
        c.start()

    barrier = pltpu.get_barrier_semaphore()
    for dev in (to_c, to_x, to_z, to_w, to_y):
        pl.semaphore_signal(barrier, inc=1, device_id=dev, device_id_type=MESH)
    pl.semaphore_wait(barrier, 5)

    qs = [quarter, (1 - core) * 2 + z0, core * 2 + 1 - z0, (1 - core) * 2 + 1 - z0]

    def item_at(i, r):
        if i == 0:
            return wo.at[pl.ds(3, 3), pl.ds(aligned(qs[r] * 32, 32), 32), :]
        if i < 4:
            return wu.at[12 + 3 * r + (i - 1)]
        if i < 7:
            return wd.at[4 + r, pl.ds((i - 4) * PAIR, PAIR), :]
        return wq.at[pl.ds(9 + 3 * (i - 7), 3), pl.ds(aligned(qs[r] * 192, 32), 192), :]

    def item_from(i):
        if i == 0:
            return wo_h.at[:, pl.ds(aligned(quarter * 32, 32), 32), :]
        if i < 4:
            return wu_h.at[:, pl.ds(aligned(quarter * 384 + (i - 1) * PAIR, PAIR), PAIR)]
        if i < 7:
            return wd_h.at[quarter, pl.ds((i - 4) * PAIR, PAIR), :]
        return wq_h.at[:, pl.ds(aligned(quarter * 192, 32), 192), pl.ds((i - 7) * PAIR, PAIR)]

    def item_into(i, r):
        if i == 0 or i >= 7:
            return item_at(i, {0: 0, 1: 0, 2: 0, 3: 2}[r])
        return item_at(i, r)

    def ask(i):
        remote(item_from(i), item_into(i, 0), agl_s.at[i, 0], agl_r.at[i, 0], to_y).start()

    def hand(i):
        arrived(item_at(i, 0), agl_r.at[i, 0], to_y)
        remote(item_at(i, 0), item_into(i, 1), agl_s.at[i, 1], agl_r.at[i, 1], to_c).start()
        remote(item_at(i, 0), item_into(i, 2), agl_s.at[i, 2], agl_r.at[i, 2], to_z).start()

    def hand_on(i):
        arrived(item_at(i, 2), agl_r.at[i, 2], to_z)
        remote(item_at(i, 2), item_into(i, 3), agl_s.at[i, 3], agl_r.at[i, 3], to_c).start()

    def have(i, r):
        arrived(item_at(i, r), agl_r.at[i, r], to_c)

    bu_copy = remote(bu, bu_oth, agl_s.at[10, 0], agl_r.at[10, 0], to_y)
    bu_copy.start()
    ask(0)
    ask(1)
    vs[0] = jnp.zeros_like(vs[0])

    lane = lax.broadcasted_iota(jnp.int32, (seq, PAIR), 1)
    place = lax.broadcasted_iota(jnp.int32, (seq, 1), 0)
    scale = HEAD_DIM**-0.5
    own_len = lens[mp]

    peer_tok.wait()
    for c in wq_in:
        c.wait()

    def att_copy(i):
        return (
            remote(att.at[i], att.at[6 + i], att_s.at[0, i], att_r.at[0, i], to_y),
            remote(lse.at[i], lse.at[6 + i], att_s.at[1, i], att_r.at[1, i], to_y),
        )

    def attend(i, _):
        chip, pair = i // 3, i % 3

        @pl.when(i == 3)
        def _():
            own_tok.wait()

        @pl.when(pair == 0)
        def _():
            xhat, _ = normalize(tok[chip].astype(F32))
            normed = (xhat * g1[...] + s1[...]).astype(BF)
            n1[...] = normed

            @pl.when(chip == 1)
            def _():
                place_rows(n1t, normed.T, ATT_ORDER)

        w = jnp.concatenate([wq[3 * pair], wq[3 * pair + 1], wq[3 * pair + 2]], axis=1)
        qkv = mm(n1[...], w).astype(BF)
        q = qkv[:, :PAIR] * jnp.asarray(scale, BF)
        k = qkv[:, PAIR : 2 * PAIR]
        vt = qkv[:, 2 * PAIR :].T
        visible = place < lens[(1 - mp) * (1 - chip) + mp * chip]
        outs = []
        for h in range(2):
            mine = (lane >= h * HEAD_DIM) & (lane < (h + 1) * HEAD_DIM)
            s = jnp.where(visible, mm_t(jnp.where(mine, k, jnp.zeros_like(k)), q), -1e30)
            top = jnp.max(s, 0, keepdims=True)
            e = jnp.exp(s - top)
            total = jnp.sum(e, 0, keepdims=True)
            lse[i, h : h + 1, :] = top + jnp.log(total)
            o = mm(vt[h * HEAD_DIM : (h + 1) * HEAD_DIM], e.astype(BF))
            outs.append(o / total)
        lse[i, 2:8, :] = jnp.zeros((6, seq), F32)
        att[i] = jnp.concatenate(outs, 0).T.astype(BF)

        @pl.when(chip == 0)
        def _():
            for c in att_copy(i):
                c.start()

        @pl.when(i == 2)
        def _():
            for n in range(2, 10):
                ask(n)
            hand(0)

        @pl.when(i == 4)
        def _():
            hand(1)
            hand_on(0)

        return 0

    lax.fori_loop(0, 6, attend, 0)

    cot.wait()
    visible = place < own_len
    g = jnp.where(visible, gm[...].astype(F32), 0.0)
    g_low = g.astype(BF)
    gm[...] = g_low
    place_rows(gmt, g_low.T, MLP_ORDER)
    vs[0, 0:1, :] = jnp.sum(g, 0, keepdims=True)
    wo_in.wait()
    have(0, 1)
    have(0, 3)
    for i in range(3):
        arrived(att.at[6 + i], att_r.at[0, i], to_y)
        arrived(lse.at[6 + i], att_r.at[1, i], to_y)
    blocks = jnp.concatenate([att[3 + p] for p in range(6)], axis=1)
    r = tok[1].astype(F32) + mm(blocks, wo[...].reshape(6 * PAIR, width)) + b_out[...]
    resid[...] = r
    xhat, _ = normalize(r)
    normed = (xhat * g2[...] + s2[...]).astype(BF)
    n2[...] = normed
    place_rows(n2t, normed.T, MLP_ORDER)
    macc[...] = jnp.zeros_like(macc)
    gacc[...] = jnp.zeros_like(gacc)

    half = 384

    def base(n):
        b = core * 384
        if n > 1:
            b = b + x * 192
        if n > 2:
            b = b + z0 * 96
        if n > 3:
            b = b + z1 * 48
        return b

    def send_part(n):
        return [(1 - core) * 384, base(1) + (1 - x) * 192, base(2) + (1 - z0) * 96, base(3) + (1 - z1) * 48][n]

    m_buf = [rc, rx, rz, rw]
    m_dev = [to_c, to_x, to_z, to_w]

    def cross(n, t):
        late = t // 4
        if n == 0:
            return t + late * (1 - 2 * (t % 2))
        if n == 2:
            return t + late * (2 - 4 * ((t // 2) % 2))
        return t

    def m_copy(n, t):
        rows = 384 >> n
        src = grad.at[t, :, pl.ds(aligned(send_part(n), 16), rows), :]
        to = cross(n, t)
        return remote(src, m_buf[n].at[to], m_s.at[n, t], m_r.at[n, to], m_dev[n])

    def m_add(n, t):
        rows = 384 >> n
        arrived(m_buf[n].at[t], m_r.at[n, t], m_dev[n])
        at = pl.ds(aligned(base(n + 1), 16), rows)
        for w in range(2):
            grad[t, w, at, :] = (grad[t, w, at, :].astype(F32) + m_buf[n][t, w].astype(F32)).astype(BF)

    def m_step(n, t):
        m_add(n, t)
        if n < 3:
            m_copy(n + 1, t).start()
            return

        @pl.when(t >= 4)
        def _():
            m_y(t).start()

    def unit_quarter(t):
        s = t - 4
        return ((core + s % 2) % 2) * 2 + (z0 + s // 2) % 2

    def m_y(t):
        src = grad.at[t, :, pl.ds(aligned(base(4), 16), ROWS), :]
        to = unit_quarter(t)
        return remote(src, ry.at[to], m_s.at[4, t], m_r.at[4, to], to_y)

    def tile(t, _):
        for j in range(4):

            @pl.when(t == j)
            def _(j=j):
                for c in wu_in[3 * j : 3 * j + 3]:
                    c.wait()
                if j == 0:
                    wd_in.wait()
                if j == 1:
                    hand(2)
                if j == 2:
                    hand(3)
                if j == 3:
                    hand(4)
                    hand_on(1)
                    hand_on(2)

        @pl.when(t == 4)
        def _():
            hand(5)
            hand(6)
            hand_on(3)

        @pl.when(t == 5)
        def _():
            for i in range(1, 7):
                have(i, 1)
            hand_on(4)
            for i in range(7, 10):
                hand(i)

        @pl.when(t == 6)
        def _():
            hand_on(5)
            hand_on(6)

        @pl.when(t == 7)
        def _():
            for i in range(1, 7):
                have(i, 3)
            for i in range(7, 10):
                hand_on(i)

        late = t // 4
        unit = unit_quarter(t + 4 * (1 - late)) * late + t * (1 - late)
        wut = jnp.concatenate([wu[3 * t], wu[3 * t + 1], wu[3 * t + 2]], axis=1)
        wdt = wd[t]
        bias = jnp.where(late == 0, bu[pl.ds(unit, 1), :], bu_oth[pl.ds(unit, 1), :])
        u = mm(n2[...], wut) + bias
        act, slope = gelu_pair(u)
        act = act.astype(BF)
        gp = (mm_t(gm[...], wdt) * slope).astype(BF)
        row = 8 + 4 * (mp + late - 2 * mp * late) + unit
        vs[0, pl.ds(row, 1), 0:384] = jnp.sum(gp.astype(F32), 0, keepdims=True)
        macc[...] += mm(act, wdt)
        gacc[...] += mm_t(gp, wut)
        grad[t, 0] = mm(n2t[...], gp).astype(BF)
        grad[t, 1] = mm(gmt[...], act).astype(BF)
        m_copy(0, t).start()

        @pl.when(t >= 1)
        def _():
            m_step(0, t - 1)

        @pl.when(t >= 5)
        def _():
            m_step(1, t - 5)

        return 0

    arrived(bu_oth, agl_r.at[10, 0], to_y)
    lax.fori_loop(0, 8, tile, 0)
    m_step(0, 7)

    r = resid[...]
    ob[...] = jnp.where(visible, r + macc[...] + b_down[...], 0.0).astype(BF)
    out_own = local(ob, out_h.at[mp], o_sem.at[0])
    out_far = remote(ob, out_h.at[mp], e_s.at[0], e_r.at[0], to_y)
    out_own.start()
    out_far.start()
    xhat, inv = normalize(r)
    gs = gacc[...]
    gres = gm[...].astype(F32) + norm_back(gs, xhat, inv, g2[...])
    low = gres.astype(BF)
    n2[...] = low
    place_rows(n2t, low.T, ATT_ORDER)
    vs[0, 1:2, :] = jnp.sum(gs * xhat, 0, keepdims=True)
    vs[0, 2:3, :] = jnp.sum(gs, 0, keepdims=True)
    vs[0, 3:4, :] = jnp.sum(gres, 0, keepdims=True)
    resid[...] = gres
    gacc[...] = jnp.zeros_like(gacc)
    for i in range(7, 10):
        have(i, 1)
        have(i, 3)
    for i in range(1, 4):
        sent(item_at(i, 0), agl_s.at[i, 1], to_c)
        sent(item_at(i, 0), agl_s.at[i, 2], to_z)
        sent(item_at(i, 2), agl_s.at[i, 3], to_c)

    a_buf = [ac, az, aw, ax]
    a_dev = [to_c, to_z, to_w, to_x]

    def a_base(n):
        b = core * 384
        if n > 1:
            b = b + z0 * 192
        if n > 2:
            b = b + z1 * 96
        if n > 3:
            b = b + x * 48
        return b

    def a_part(n):
        return [(1 - core) * 384, a_base(1) + (1 - z0) * 192, a_base(2) + (1 - z1) * 96, a_base(3) + (1 - x) * 48][n]

    def a_copy(n, p):
        rows = 384 >> n
        src = wu.at[pl.ds(4 * p, 4), pl.ds(aligned(a_part(n), 16), rows), :]
        return remote(src, a_buf[n].at[p], a_s.at[n, p], a_r.at[n, p], a_dev[n])

    def a_step(n, p):
        rows = 384 >> n
        arrived(a_buf[n].at[p], a_r.at[n, p], a_dev[n])
        at = pl.ds(aligned(a_base(n + 1), 16), rows)
        for w in range(4):
            wu[4 * p + w, at, :] = (wu[4 * p + w, at, :].astype(F32) + a_buf[n][p, w].astype(F32)).astype(BF)
        if n < 3:
            a_copy(n + 1, p).start()
            return

        @pl.when(p >= 3)
        def _():
            a_y(p).start()

    def a_y(p):
        src = wu.at[pl.ds(4 * p, 4), pl.ds(aligned(a_base(4), 16), ROWS), :]
        return remote(src, ay.at[p - 3], a_s.at[4, p], a_r.at[4, p], to_y)

    zero = jnp.zeros((seq, PAIR), BF)

    def back(p, _):
        w = jnp.concatenate([wq[3 * p], wq[3 * p + 1], wq[3 * p + 2]], axis=1)
        qkv = mm(n1[...], w).astype(BF)
        q, k, v = qkv[:, :PAIR], qkv[:, PAIR : 2 * PAIR], qkv[:, 2 * PAIR :]
        q_s = q * jnp.asarray(scale, BF)
        ga = mm_t(n2[...], wo[p]).astype(BF)
        kt = k.T
        dqt = []
        dk = jnp.zeros((seq, PAIR), F32)
        dv = jnp.zeros((seq, PAIR), F32)
        for h in range(2):
            mine = (lane >= h * HEAD_DIM) & (lane < (h + 1) * HEAD_DIM)
            s = jnp.where(visible, mm_t(jnp.where(mine, k, zero), q_s), -1e30)
            prob = jnp.exp(s - lse[3 + p, h : h + 1, :])
            d_prob = mm_t(jnp.where(mine, v, zero), ga)
            row = jnp.sum(prob * d_prob, 0, keepdims=True)
            ds = (prob * (d_prob - row) * scale).astype(BF)
            dk += mm(ds, jnp.where(mine, q, zero))
            dv += mm(prob.astype(BF), jnp.where(mine, ga, zero))
            dqt.append(mm(kt[h * HEAD_DIM : (h + 1) * HEAD_DIM], ds))
        dq = jnp.concatenate(dqt, 0).T
        d = jnp.concatenate([dq.astype(BF), dk.astype(BF), dv.astype(BF)], axis=1)
        gacc[...] += mm_t(d, w)
        dw = mm(n1t[...], d).astype(BF)
        for c in range(3):
            wu[4 * p + c] = dw[:, c * PAIR : (c + 1) * PAIR]
        wu[4 * p + 3] = mm(n2t[...], att[3 + p]).astype(BF)
        a_copy(0, p).start()

        @pl.when(p < 5)
        def _():
            m_step(1, p + 3)

        m_step(2, p)

        @pl.when(p >= 1)
        def _():
            m_step(3, p - 1)
            a_step(0, p - 1)

        @pl.when(p >= 2)
        def _():
            a_step(1, p - 2)

        @pl.when(p >= 3)
        def _():
            a_step(2, p - 3)

        return 0

    lax.fori_loop(0, 6, back, 0)

    chunk = seq // 4

    def gt_copy(j):
        rows = pl.ds(j * chunk, chunk)
        return remote(gl.at[rows, :], gr.at[rows, :], e_s.at[1 + j], e_r.at[1 + j], to_y)

    gain_sum = jnp.zeros((1, width), F32)
    shift_sum = jnp.zeros((1, width), F32)
    for j in range(4):
        rows = slice(j * chunk, (j + 1) * chunk)
        xhat, inv = normalize(tok[1, rows].astype(F32))
        gf = gacc[rows]
        gt = resid[rows] + norm_back(gf, xhat, inv, g1[...])
        resid[rows] = gt
        gl[rows] = gt.astype(BF)
        gt_copy(j).start()
        gain_sum += jnp.sum(gf * xhat, 0, keepdims=True)
        shift_sum += jnp.sum(gf, 0, keepdims=True)
        if j == 0:
            a_step(0, 5)
    gt_own = local(resid, gt_h.at[mp], o_sem.at[1])
    gt_own.start()
    vs[0, 4:5, :] = gain_sum
    vs[0, 5:6, :] = shift_sum
    v_dev = [to_c, to_z, to_w, to_x, to_y]

    def v_copy(n):
        return remote(vs.at[n], vr.at[n], e_s.at[5 + n], e_r.at[5 + n], v_dev[n])

    def v_step(n):
        arrived(vr.at[n], e_r.at[5 + n], v_dev[n])
        if n < 4:
            vs[n + 1] = vs[n] + vr[n]
            v_copy(n + 1).start()
        else:
            vec_out[...] = vs[4] + vr[4]

    v_copy(0).start()
    m_step(2, 6)
    m_step(3, 5)
    a_step(1, 4)
    a_step(2, 3)
    v_step(0)
    a_step(3, 0)
    a_step(3, 1)
    m_step(2, 7)
    m_step(3, 6)
    a_step(3, 2)
    a_step(1, 5)
    v_step(1)
    a_step(2, 4)
    a_step(3, 3)
    m_step(3, 7)
    v_step(2)
    a_step(2, 5)
    a_step(3, 4)
    v_step(3)
    a_step(3, 5)

    mine = pl.ds(aligned(base(4), 16), ROWS)
    for a in range(4):
        arrived(ry.at[a], m_r.at[4, a], to_y)
        cols = slice(a * 384, (a + 1) * 384)
        d_up[:, cols] = grad[a, 0, mine, :].astype(F32) + ry[a, 0].astype(F32)
        d_down[:, cols] = grad[a, 1, mine, :].astype(F32) + ry[a, 1].astype(F32)
    mine = pl.ds(aligned(a_base(4), 16), ROWS)
    for j in range(4):
        rows = slice(j * chunk, (j + 1) * chunk)
        arrived(gr.at[pl.ds(j * chunk, chunk), :], e_r.at[1 + j], to_y)
        macc[rows] = gr[rows].astype(F32)
        local(macc.at[pl.ds(j * chunk, chunk), :], gt_h.at[1 - mp, pl.ds(j * chunk, chunk), :], o_sem.at[2 + j]).start()
    for p in range(3):
        arrived(ay.at[p], a_r.at[4, 3 + p], to_y)
        cols = slice(p * PAIR, (p + 1) * PAIR)
        for c in range(3):
            d_qkv[c, :, cols] = wu[4 * p + c, mine, :].astype(F32) + ay[p, c].astype(F32)
        d_out[:, cols] = wu[4 * p + 3, mine, :].astype(F32) + ay[p, 3].astype(F32)
    v_step(4)

    bu_copy.wait_send()
    for i in range(10):
        sent(item_from(i), agl_s.at[i, 0], to_y)
        if not 1 <= i < 4:
            sent(item_at(i, 0), agl_s.at[i, 1], to_c)
            sent(item_at(i, 0), agl_s.at[i, 2], to_z)
            sent(item_at(i, 2), agl_s.at[i, 3], to_c)
    for i in range(3):
        for c in att_copy(i):
            c.wait_send()

    def drain_m(t, _):
        for n in range(4):
            m_copy(n, t).wait_send()

        @pl.when(t >= 4)
        def _():
            m_y(t).wait_send()

        return 0

    lax.fori_loop(0, 8, drain_m, 0)

    def drain_a(p, _):
        for n in range(4):
            a_copy(n, p).wait_send()

        @pl.when(p >= 3)
        def _():
            a_y(p).wait_send()

        return 0

    lax.fori_loop(0, 6, drain_a, 0)
    for j in range(4):
        gt_copy(j).wait_send()
        local(macc.at[pl.ds(j * chunk, chunk), :], gt_h.at[1 - mp, pl.ds(j * chunk, chunk), :], o_sem.at[2 + j]).wait()
    for n in range(5):
        v_copy(n).wait_send()
    out_own.wait()
    out_far.wait_send()
    arrived(out_h.at[1 - mp], e_r.at[0], to_y)
    gt_own.wait()


def kernel_program(
    mp_n, tokens, lengths, ln1_gain, ln1_shift, w_qkv, w_out, b_out, ln2_gain, ln2_shift, w_up, b_up, w_down, b_down, cotangent
):
    seq, width = tokens.shape[1:]
    feat, hidden = w_qkv.shape[2], w_up.shape[1]
    tile = hidden // 4
    row = lambda v: v.reshape(1, -1)
    rows8 = b_up.reshape(4, tile)
    args = [
        lengths, tokens, cotangent, row(ln1_gain), row(ln1_shift), row(ln2_gain), row(ln2_shift), row(b_out), row(b_down),
        jnp.concatenate([rows8, rows8], 0), w_qkv, w_out.reshape(3, PAIR, width), w_up, w_down.reshape(4, tile, width),
    ]
    hbm, vmem = pl.BlockSpec(memory_space=pl.ANY), pl.BlockSpec(memory_space=pltpu.VMEM)
    outs = [
        sds(tokens.shape, BF),
        sds(tokens.shape, F32),
        sds((3, ROWS, feat), F32),
        sds((ROWS, feat), F32),
        sds((ROWS, hidden), F32),
        sds((ROWS, hidden), F32),
        sds((16, width), F32),
    ]
    v = pltpu.VMEM
    act = v((seq, width), BF)
    act_t = v((width, seq), BF)
    wide = v((seq, width), F32)
    scratch = [
        v((2, seq, width), BF), act, act_t, act, act_t, act, act_t, wide, wide, wide,
        v((9, seq, PAIR), BF), v((9, 8, seq), F32),
        v((18, width, PAIR), BF), v((6, PAIR, width), BF), v((24, width, PAIR), BF), v((8, tile, width), BF), v((8, tile), F32),
        v((8, 2, width, tile), BF),
        v((8, 2, 384, tile), BF), v((8, 2, 192, tile), BF), v((8, 2, 96, tile), BF), v((8, 2, 48, tile), BF), v((4, 2, 48, tile), BF),
        v((6, 4, 384, PAIR), BF), v((6, 4, 192, PAIR), BF), v((6, 4, 96, PAIR), BF), v((6, 4, 48, PAIR), BF), v((3, 4, 48, PAIR), BF),
        act, act, act, v((5, 16, width), F32), v((5, 16, width), F32),
    ]
    dma = pltpu.SemaphoreType.DMA
    scratch += [
        dma((20,)), dma((11, 4)), dma((11, 4)), dma((2, 3)), dma((2, 3)), dma((5, 8)), dma((5, 8)), dma((5, 6)), dma((5, 6)),
        dma((10,)), dma((10,)), dma((6,)),
    ]
    out, gt, d_qkv, d_out, d_up, d_down, vec = pl.pallas_call(
        layer_kernel,
        name="layer",
        out_shape=outs,
        in_specs=[pl.BlockSpec(memory_space=pltpu.SMEM), hbm, hbm] + [vmem] * 7 + [hbm] * 4,
        out_specs=[hbm, hbm] + [vmem] * 5,
        scratch_shapes=scratch,
        compiler_params=pltpu.CompilerParams(collective_id=0, has_side_effects=True, vmem_limit_bytes=VMEM_ALL),
    )(*args)
    dp, mp = lax.axis_index("dp"), lax.axis_index("mp")
    shard = lax.dynamic_slice_in_dim(vec[:6], dp * ROWS, ROWS, 1)
    bias = vec[8:, :tile].reshape(mp_n, hidden)
    bias = lax.dynamic_slice(bias, (mp, dp * 2 * ROWS), (1, 2 * ROWS))
    return (
        out, gt, shard[4], shard[5], d_qkv, d_out.T, shard[3], shard[1], shard[2], d_up, bias, d_down.T, shard[0],
    )


def solution(mesh):
    dp_n, mp_n = mesh.shape["dp"], mesh.shape["mp"]
    body = functools.partial(kernel_program, mp_n) if dp_n == 16 else functools.partial(permute_program, dp_n, mp_n)
    return jax.shard_map(
        body,
        mesh=mesh,
        in_specs=(
            P("dp", None, None),
            P("dp"),
            P(),
            P(),
            P(None, None, "mp"),
            P("mp", None),
            P(),
            P(),
            P(),
            P(None, "mp"),
            P("mp"),
            P("mp", None),
            P(),
            P("dp", None, None),
        ),
        out_specs=(
            P("dp", None, None),
            P("dp", None, None),
            P("dp"),
            P("dp"),
            P(None, "dp", "mp"),
            P("mp", "dp"),
            P("dp"),
            P("dp"),
            P("dp"),
            P("dp", "mp"),
            P("mp", "dp"),
            P("mp", "dp"),
            P("dp"),
        ),
        check_vma=False,
    )
```

```python
import functools

import jax
import jax.numpy as jnp
from jax import lax
from jax.experimental import pallas as pl
from jax.experimental.pallas import tpu as pltpu
from jax.sharding import PartitionSpec as P

HEAD_DIM = 64
PAIR = 2 * HEAD_DIM
BF = jnp.bfloat16
F32 = jnp.float32
EPS = 1e-05
LIMIT = 40 * 1024 * 1024

TAIL_P = 0.3
TAIL_C = (
    0.11962929256864907,
    0.12075406313917503,
    0.09991275007605285,
    0.12856432480895655,
    -0.05368921426491713,
    0.2063600527786208,
    -0.1572071533588575,
    0.03567581131365836,
)


def mm(a, b):
    return lax.dot_general(a, b, (((1,), (0,)), ((), ())), preferred_element_type=F32)


def mm_t(a, b):
    return lax.dot_general(a, b, (((1,), (1,)), ((), ())), preferred_element_type=F32)


def normalize(x):
    mean = jnp.mean(x, -1, keepdims=True)
    center = x - mean
    var = jnp.mean(center * center, -1, keepdims=True)
    inv = lax.rsqrt(var + EPS)
    return center * inv, inv


def norm_back(grad, xhat, inv, gain):
    d = grad * gain
    m1 = jnp.mean(d, -1, keepdims=True)
    m2 = jnp.mean(d * xhat, -1, keepdims=True)
    return inv * (d - m1 - xhat * m2)


def bit_reverse(index, bits):
    out = 0
    for b in range(bits):
        out = (out << 1) | ((index >> b) & 1)
    return out


def put_rows(ref, value, blocks):
    rows = value.shape[0] // blocks
    bits = blocks.bit_length() - 1
    if rows % 16:
        ref[...] = value
        return
    for b in range(blocks):
        d = bit_reverse(b, bits)
        ref[d * rows : (d + 1) * rows, :] = value[b * rows : (b + 1) * rows, :]


def order_rows(value, blocks):
    rows = value.shape[0] // blocks
    if rows % 16 == 0:
        return value
    bits = blocks.bit_length() - 1
    split = value.reshape((2,) * bits + (rows, value.shape[1]))
    split = split.transpose(tuple(reversed(range(bits))) + (bits, bits + 1))
    return split.reshape(value.shape)


def call(body, name, out_shape, args, flops, grid=None, in_specs=None, out_specs=None, scalars=None, scratch=(), aliases=None):
    nbytes = sum(a.size * a.dtype.itemsize for a in args)
    nbytes += sum(o.size * o.dtype.itemsize for o in out_shape)
    if in_specs is None:
        in_specs = [whole(a.shape) for a in args]
    if out_specs is None:
        out_specs = [whole(o.shape) for o in out_shape]
    return pl.pallas_call(
        body,
        name=name,
        out_shape=out_shape,
        grid_spec=pltpu.PrefetchScalarGridSpec(
            num_scalar_prefetch=1,
            grid=grid or (1,),
            in_specs=in_specs,
            out_specs=out_specs,
            scratch_shapes=list(scratch),
        ),
        input_output_aliases=aliases or {},
        compiler_params=pltpu.CompilerParams(vmem_limit_bytes=LIMIT),
        cost_estimate=pl.CostEstimate(flops=flops, bytes_accessed=nbytes, transcendentals=0),
    )(scalars, *args)


def whole(shape):
    return pl.BlockSpec(shape, lambda *_: (0,) * len(shape))


def sds(shape, dtype):
    return jax.ShapeDtypeStruct(shape, dtype)


def chip_spec(shape):
    return pl.BlockSpec((None,) + tuple(shape[1:]), lambda i, sc: (sc[0], 0, 0))


def attention_kernel(sc, tok, gain, shift, w_ref, att_ref, lse_ref, normed):
    @pl.when(pl.program_id(0) == 0)
    def _():
        xhat, _ = normalize(tok[...].astype(F32))
        normed[...] = (xhat * gain[...] + shift[...]).astype(BF)

    seq = normed.shape[0]
    w = jnp.concatenate([w_ref[0], w_ref[1], w_ref[2]], axis=1)
    qkv = mm(normed[...], w).astype(BF)
    scale = HEAD_DIM**-0.5
    q = qkv[:, :PAIR] * jnp.asarray(scale, BF)
    k = qkv[:, PAIR : 2 * PAIR]
    vt = qkv[:, 2 * PAIR :].T
    lane = lax.broadcasted_iota(jnp.int32, (seq, PAIR), 1)
    visible = lax.broadcasted_iota(jnp.int32, (seq, 1), 0) < sc[1]
    outs = []
    for h in range(2):
        mine = (lane >= h * HEAD_DIM) & (lane < (h + 1) * HEAD_DIM)
        kh = jnp.where(mine, k, jnp.zeros_like(k))
        s = jnp.where(visible, mm_t(kh, q), -1e30)
        top = jnp.max(s, 0, keepdims=True)
        e = jnp.exp(s - top)
        total = jnp.sum(e, 0, keepdims=True)
        lse_ref[h : h + 1, :] = top + jnp.log(total)
        o = mm(vt[h * HEAD_DIM : (h + 1) * HEAD_DIM], e.astype(BF))
        outs.append(o / total)
    att_ref[...] = jnp.concatenate(outs, 0).T.astype(BF)
    lse_ref[2:8, :] = jnp.zeros((6, seq), F32)


def prepare_kernel(blocks, sc, tok, cot, gain, shift, n1, n1t, gm, gmt, vec):
    xhat, _ = normalize(tok[...].astype(F32))
    normed = (xhat * gain[...] + shift[...]).astype(BF)
    n1[...] = normed
    put_rows(n1t, normed.T, blocks)
    seq = normed.shape[0]
    visible = lax.broadcasted_iota(jnp.int32, (seq, 1), 0) < sc[1]
    g = jnp.where(visible, cot[...].astype(F32), 0.0)
    gl = g.astype(BF)
    gm[...] = gl
    put_rows(gmt, gl.T, blocks)
    vec[...] = jnp.broadcast_to(jnp.sum(g, 0, keepdims=True), vec.shape)


def project_kernel(blocks, sc, tok, att_a, att_b, wo_a, wo_b, b_out, gain, shift, resid, n2, n2t):
    x = tok[...].astype(F32)
    r = x + mm(att_a[...], wo_a[...]) + mm(att_b[...], wo_b[...]) + b_out[...]
    resid[...] = r
    xhat, _ = normalize(r)
    normed = (xhat * gain[...] + shift[...]).astype(BF)
    n2[...] = normed
    put_rows(n2t, normed.T, blocks)


def gelu_pair(u):
    z = jnp.abs(u)
    t = 1.0 / (1.0 + TAIL_P * z)
    poly = TAIL_C[-1]
    for c in TAIL_C[-2::-1]:
        poly = poly * t + c
    e = jnp.exp(-0.5 * u * u)
    tail = e * (poly * t)
    cdf = jnp.where(u < 0, tail, 1.0 - tail)
    return u * cdf, cdf + u * e * 0.3989422804014327


def mlp_kernel(tiles, first, cross, sc, *refs):
    n2, n2t, gm, gmt = refs[:4]
    wu = refs[4 : 4 + tiles]
    wd = refs[4 + tiles : 4 + 2 * tiles]
    bu = refs[4 + 2 * tiles]
    at = 5 + 2 * tiles
    if not first:
        macc_in, gacc_in, db_in = refs[at : at + 3]
        at += 3
    keep, send, macc, gacc, db = refs[at:]
    width = wu[0].shape[1]
    half = keep.shape[1]
    core = sc[0]
    db[...] = jnp.zeros_like(db) if first else db_in[...]
    for t in range(tiles):
        wut, wdt = wu[t][...], wd[t][...]
        u = mm(n2[...], wut) + bu[pl.ds(sc[1 + 2 * t], 1), :]
        act, slope = gelu_pair(u)
        act = act.astype(BF)
        gp = (mm_t(gm[...], wdt) * slope).astype(BF)
        db[pl.ds(sc[2 + 2 * t], 1), :] = jnp.sum(gp.astype(F32), 0, keepdims=True)
        m, g = mm(act, wdt), mm_t(gp, wut)
        if t == 0 and first:
            macc[...], gacc[...] = m, g
        elif t == 0:
            macc[...], gacc[...] = macc_in[...] + m, gacc_in[...] + g
        else:
            macc[...] += m
            gacc[...] += g
        for which, (lhs, rhs) in enumerate(((n2t, gp), (gmt, act))):
            grad = mm(lhs[...], rhs).astype(BF)
            top, low = grad[:half], grad[half:]
            other = (t ^ 1) if cross else t
            keep[which, :, t * width : (t + 1) * width] = jnp.where(core == 0, top, low)
            send[which, :, other * width : (other + 1) * width] = jnp.where(core == 0, low, top)


def middle_kernel(blocks, sc, resid, macc, gacc, gm, b_down, gain, out, gres, rl, rlt, vec):
    r = resid[...]
    seq = r.shape[0]
    visible = lax.broadcasted_iota(jnp.int32, (seq, 1), 0) < sc[1]
    out[...] = jnp.where(visible, r + macc[...] + b_down[...], 0.0).astype(BF)
    xhat, inv = normalize(r)
    gs = gacc[...]
    gr = gm[...].astype(F32) + norm_back(gs, xhat, inv, gain[...])
    gres[...] = gr
    low = gr.astype(BF)
    rl[...] = low
    put_rows(rlt, low.T, blocks)
    vec[0:1, :] = jnp.sum(gs * xhat, 0, keepdims=True)
    vec[1:2, :] = jnp.sum(gs, 0, keepdims=True)
    vec[2:3, :] = jnp.sum(gr, 0, keepdims=True)
    vec[3:8, :] = jnp.zeros((5, vec.shape[1]), F32)


def attention_back_kernel(first, sc, *refs):
    n1, n1t, rl, rlt, att, lse, w_ref, wo = refs[:8]
    at = 8
    if not first:
        gf_in = refs[at]
        at += 1
    keep, send, gf = refs[at:]
    seq = n1.shape[0]
    half = keep.shape[1]
    scale = HEAD_DIM**-0.5
    w = jnp.concatenate([w_ref[0], w_ref[1], w_ref[2]], axis=1)
    qkv = mm(n1[...], w).astype(BF)
    q, k, v = qkv[:, :PAIR], qkv[:, PAIR : 2 * PAIR], qkv[:, 2 * PAIR :]
    qs = q * jnp.asarray(scale, BF)
    ga = mm_t(rl[...], wo[...]).astype(BF)
    kt = k.T
    lane = lax.broadcasted_iota(jnp.int32, (seq, PAIR), 1)
    visible = lax.broadcasted_iota(jnp.int32, (seq, 1), 0) < sc[1]
    zero = jnp.zeros_like(q)
    dqt = []
    dk = jnp.zeros((seq, PAIR), F32)
    dv = jnp.zeros((seq, PAIR), F32)
    for h in range(2):
        mine = (lane >= h * HEAD_DIM) & (lane < (h + 1) * HEAD_DIM)
        s = jnp.where(visible, mm_t(jnp.where(mine, k, zero), qs), -1e30)
        p = jnp.exp(s - lse[h : h + 1, :])
        dp = mm_t(jnp.where(mine, v, zero), ga)
        row = jnp.sum(p * dp, 0, keepdims=True)
        ds = (p * (dp - row) * scale).astype(BF)
        dk += mm(ds, jnp.where(mine, q, zero))
        dv += mm(p.astype(BF), jnp.where(mine, ga, zero))
        dqt.append(mm(kt[h * HEAD_DIM : (h + 1) * HEAD_DIM], ds))
    dq = jnp.concatenate(dqt, 0).T
    d = jnp.concatenate([dq.astype(BF), dk.astype(BF), dv.astype(BF)], axis=1)
    g = mm_t(d, w)
    begin = pl.program_id(0) == 0

    @pl.when(begin)
    def _():
        gf[...] = g if first else gf_in[...] + g

    @pl.when(jnp.logical_not(begin))
    def _():
        gf[...] += g

    core = sc[0]
    dw = mm(n1t[...], d).astype(BF)
    dwo = mm(rlt[...], att[...]).astype(BF)
    parts = [dw[:, c * PAIR : (c + 1) * PAIR] for c in range(3)] + [dwo]
    for c, part in enumerate(parts):
        top, low = part[:half], part[half:]
        keep[c] = jnp.where(core == 0, top, low)
        send[c] = jnp.where(core == 0, low, top)


def last_kernel(sc, tok, gres, gf, gain, gt, gtl, vec):
    xhat, inv = normalize(tok[...].astype(F32))
    g = gf[...]
    out = gres[...] + norm_back(g, xhat, inv, gain[...])
    gt[...] = out
    gtl[...] = out.astype(BF)
    vec[0:1, :] = jnp.sum(g * xhat, 0, keepdims=True)
    vec[1:2, :] = jnp.sum(g, 0, keepdims=True)
    vec[2:8, :] = jnp.zeros((6, vec.shape[1]), F32)


def permute_program(
    dp_n,
    mp_n,
    tokens,
    lengths,
    ln1_gain,
    ln1_shift,
    w_qkv,
    w_out,
    b_out,
    ln2_gain,
    ln2_shift,
    w_up,
    b_up,
    w_down,
    b_down,
    cotangent,
):
    chips, seq, width = tokens.shape
    feat = w_qkv.shape[2]
    hidden = w_up.shape[1]
    tile = hidden // 4
    pairs = feat // PAIR
    bits = dp_n.bit_length() - 1
    half = width // 2
    mp = lax.axis_index("mp")
    dp = lax.axis_index("dp")
    core = dp & 1
    two = dp & 3
    quarter = ((two & 1) << 1) | (two >> 1)
    i32 = jnp.int32

    def swap_y(x):
        return lax.ppermute(x, "mp", [(i, i ^ 1) for i in range(mp_n)])

    def swap_d(x, bit):
        return lax.ppermute(x, "dp", [(i, i ^ (1 << bit)) for i in range(dp_n)])

    own_sc = jnp.stack([mp, lengths[mp]]).astype(i32)
    peer_sc = jnp.stack([1 - mp, lengths[1 - mp]]).astype(i32)
    row = lambda v: v.reshape(1, -1)
    g1, s1, g2, s2, bo, bd = map(row, (ln1_gain, ln1_shift, ln2_gain, ln2_shift, b_out, b_down))

    hw = feat // 2
    wo_r0 = swap_y(lax.dynamic_slice_in_dim(w_out, core * hw, hw, 0))
    wo_r1 = swap_d(wo_r0, 0)
    wo_oth = jnp.where(core == 0, jnp.concatenate([wo_r0, wo_r1], 0), jnp.concatenate([wo_r1, wo_r0], 0))
    bu_own = b_up.reshape(4, tile)
    bu_oth = swap_y(bu_own)

    def attention(sc):
        return call(
            attention_kernel,
            "attention_fwd",
            [sds((seq, feat), BF), sds((pairs, 8, seq), F32)],
            [tokens, g1, s1, w_qkv],
            2 * seq * width * 3 * feat + 4 * seq * seq * feat,
            grid=(pairs,),
            in_specs=[
                chip_spec(tokens.shape),
                whole(g1.shape),
                whole(s1.shape),
                pl.BlockSpec((3, width, PAIR), lambda i, sc: (0, 0, i)),
            ],
            out_specs=[
                pl.BlockSpec((seq, PAIR), lambda i, sc: (0, i)),
                pl.BlockSpec((None, 8, seq), lambda i, sc: (i, 0, 0)),
            ],
            scalars=sc,
            scratch=[pltpu.VMEM((seq, width), BF)],
        )

    att_peer, lse_peer = attention(peer_sc)
    att_oth, lse_oth = swap_y(att_peer), swap_y(lse_peer)

    wu_r, wd_r = [None] * 4, [None] * 4
    for name, store, axis, src in (("u", wu_r, 1, w_up), ("d", wd_r, 0, w_down)):
        store[0] = swap_y(lax.dynamic_slice_in_dim(src, quarter * tile, tile, axis))
        store[1] = swap_d(store[0], 0)
        store[2] = swap_d(store[0], 1)
        store[3] = swap_d(store[2], 0)

    att_own, lse_own = attention(own_sc)

    n1, n1t, gm, gmt, vec_g = call(
        functools.partial(prepare_kernel, dp_n),
        "prepare",
        [sds((seq, width), BF), sds((width, seq), BF), sds((seq, width), BF), sds((width, seq), BF), sds((8, width), F32)],
        [tokens, cotangent, g1, s1],
        20 * seq * width,
        in_specs=[chip_spec(tokens.shape), chip_spec(cotangent.shape), whole(g1.shape), whole(s1.shape)],
        scalars=own_sc,
    )
    resid, n2, n2t = call(
        functools.partial(project_kernel, dp_n),
        "project",
        [sds((seq, width), F32), sds((seq, width), BF), sds((width, seq), BF)],
        [tokens, att_own, att_oth, w_out, wo_oth, bo, g2, s2],
        4 * seq * width * feat,
        in_specs=[chip_spec(tokens.shape)] + [whole(a.shape) for a in (att_own, att_oth, w_out, wo_oth, bo, g2, s2)],
        scalars=own_sc,
    )
    n1t, gmt, n2t = (order_rows(t, dp_n) for t in (n1t, gmt, n2t))

    own_half, oth_half = mp * 4, (1 - mp) * 4

    def mlp(first, cross, wus, wds, bias, slots, base, accs, specs):
        sc = [core]
        for a in slots:
            sc += [a, base + a]
        outs = [
            sds((2, half, 2 * tile), BF),
            sds((2, half, 2 * tile), BF),
            sds((seq, width), F32),
            sds((seq, width), F32),
            sds((8, tile), F32),
        ]
        args = [n2, n2t, gm, gmt, *wus, *wds, bias, *accs]
        in_specs = [whole(a.shape) for a in args]
        if specs:
            in_specs[4:8] = specs
        return call(
            functools.partial(mlp_kernel, 2, first, cross),
            "mlp_tiles",
            outs,
            args,
            12 * seq * width * 2 * tile,
            in_specs=in_specs,
            scalars=jnp.stack(sc).astype(i32),
            aliases={} if first else {10: 2, 11: 3, 12: 4},
        )

    def own_specs(a):
        return [pl.BlockSpec((width, tile), lambda i, sc, t=t: (0, t)) for t in (a, a + 1)] + [
            pl.BlockSpec((tile, width), lambda i, sc, t=t: (t, 0)) for t in (a, a + 1)
        ]

    pieces = []
    accs = []
    const = lambda v: jnp.asarray(v, i32)
    for a in (0, 2):
        k, s, *accs = mlp(
            a == 0, False, [w_up] * 2, [w_down] * 2, bu_own, [const(a), const(a + 1)], own_half, accs, own_specs(a)
        )
        pieces.append((k, s))
    mine = [quarter, quarter ^ 2, quarter ^ 1, quarter ^ 3]
    for a in (0, 2):
        k, s, *accs = mlp(
            False, True, wu_r[a : a + 2], wd_r[a : a + 2], bu_oth, mine[a : a + 2], oth_half, accs, None
        )
        pieces.append((k, s))
    macc, gacc, db = accs

    out_own, gres, rl, rlt, vec_mid = call(
        functools.partial(middle_kernel, dp_n),
        "middle",
        [sds((seq, width), BF), sds((seq, width), F32), sds((seq, width), BF), sds((width, seq), BF), sds((8, width), F32)],
        [resid, macc, gacc, gm, bd, g2],
        40 * seq * width,
        scalars=own_sc,
    )
    out_oth = swap_y(out_own)
    rlt = order_rows(rlt, dp_n)

    hq = width // 4
    wq_r = [None] * 4
    wq_r[0] = swap_y(lax.dynamic_slice_in_dim(w_qkv, quarter * hq, hq, 1))
    wq_r[1] = swap_d(wq_r[0], 0)
    wq_r[2] = swap_d(wq_r[0], 1)
    wq_r[3] = swap_d(wq_r[2], 0)
    wq_oth = jnp.concatenate(wq_r, 1)
    for r in range(4):
        wq_oth = lax.dynamic_update_slice_in_dim(wq_oth, wq_r[r], mine[r] * hq, 1)

    def attention_back(first, wq, wo, att, lse, accs):
        args = [n1, n1t, rl, rlt, att, lse, wq, wo, *accs]
        in_specs = [whole(a.shape) for a in args]
        in_specs[4] = pl.BlockSpec((seq, PAIR), lambda i, sc: (0, i))
        in_specs[5] = pl.BlockSpec((None, 8, seq), lambda i, sc: (i, 0, 0))
        in_specs[6] = pl.BlockSpec((3, width, PAIR), lambda i, sc: (0, 0, i))
        in_specs[7] = pl.BlockSpec((PAIR, width), lambda i, sc: (i, 0))
        piece = pl.BlockSpec((4, half, PAIR), lambda i, sc: (0, 0, i))
        return call(
            functools.partial(attention_back_kernel, first),
            "attention_bwd",
            [sds((4, half, feat), BF), sds((4, half, feat), BF), sds((seq, width), F32)],
            args,
            2 * seq * width * feat * 11 + 10 * seq * seq * feat,
            grid=(pairs,),
            in_specs=in_specs,
            out_specs=[piece, piece, whole((seq, width))],
            scalars=jnp.stack([core, own_sc[1]]).astype(i32),
            aliases={} if first else {9: 2},
        )

    k, s, gf = attention_back(True, w_qkv, w_out, att_own, lse_own, [])
    pieces.append((k, s))
    k, s, gf = attention_back(False, wq_oth, wo_oth, att_oth, lse_oth, [gf])
    pieces.append((k, s))

    gt_own, gt_low, vec_last = call(
        last_kernel,
        "last",
        [sds((seq, width), F32), sds((seq, width), BF), sds((8, width), F32)],
        [tokens, gres, gf, g1],
        30 * seq * width,
        in_specs=[chip_spec(tokens.shape)] + [whole(a.shape) for a in (gres, gf, g1)],
        scalars=own_sc,
    )
    gt_oth = swap_y(gt_low).astype(F32)

    def add(a, b):
        return (a.astype(F32) + b.astype(F32)).astype(BF)

    def split(x, bit):
        n = x.shape[1] // 2
        b = (dp >> bit) & 1
        return (
            lax.dynamic_slice_in_dim(x, b * n, n, 1),
            lax.dynamic_slice_in_dim(x, (1 - b) * n, n, 1),
        )

    state = [add(k, swap_d(s, 0)) for k, s in pieces]
    for bit in range(1, bits):
        parts = [split(x, bit) for x in state]
        got = [swap_d(s, bit) for _, s in parts]
        if bit == 1:
            got[2], got[3] = got[3], got[2]
        state = [add(p[0], g) for p, g in zip(parts, got)]
    own1, own2, oth1, oth2, at_own, at_oth = state
    rows = own1.shape[1]
    got1, got2, got_at = swap_y(oth1), swap_y(oth2), swap_y(at_oth)

    slots = jnp.stack([got1[..., :tile], got1[..., tile:], got2[..., :tile], got2[..., tile:]])
    got = [lax.dynamic_index_in_dim(slots, slot_of(a, two), 0, keepdims=False) for a in range(4)]
    mine_mlp = [own1[..., :tile], own1[..., tile:], own2[..., :tile], own2[..., tile:]]
    total = jnp.concatenate([m.astype(F32) + g.astype(F32) for m, g in zip(mine_mlp, got)], -1)
    total_at = at_own.astype(F32) + got_at.astype(F32)

    vecs = jnp.concatenate([vec_g[:1], vec_mid[:3], vec_last[:2], db.reshape(-1, width)], 0)
    for bit in range(bits):
        vecs = vecs + swap_d(vecs, bit)
    vecs = vecs + swap_y(vecs)
    shard = lax.dynamic_slice_in_dim(vecs[:6], dp * rows, rows, 1)
    bias = vecs[6:].reshape(mp_n, hidden)
    cols = hidden // dp_n
    bias = lax.dynamic_slice(bias, (mp, dp * cols), (1, cols))

    def both(own, oth):
        return jnp.where(mp == 0, jnp.stack([own, oth]), jnp.stack([oth, own]))

    return (
        both(out_own, out_oth),
        both(gt_own, gt_oth),
        shard[4],
        shard[5],
        total_at[:3],
        total_at[3].T,
        shard[3],
        shard[1],
        shard[2],
        total[0],
        bias,
        total[1].T,
        shard[0],
    )


def slot_of(a, two):
    q = ((two & 1) << 1) | (two >> 1)
    d = q ^ a
    return ((d & 1) << 1) | (d >> 1)


MESH = pl.DeviceIdType.MESH
ROWS = 48
VMEM_ALL = 67043328


def place_rows(ref, value):
    for b in range(16):
        p = bit_reverse(b, 4)
        ref[p * ROWS : (p + 1) * ROWS, :] = value[b * ROWS : (b + 1) * ROWS, :]


def store_rows(ref, index, value, turn):
    rows = value.shape[0] // 8
    for b in range(8):
        c, i, j = b // 4, (b // 2) % 2, b % 2
        if i == j:
            at = pl.ds(b * rows, rows)
        else:
            at = pl.ds(aligned((4 * c + 1) * rows + (i * turn + j * (1 - turn)) * rows, 16), rows)
        ref[(*index, at, slice(None))] = value[b * rows : (b + 1) * rows]


def aligned(v, n):
    return pl.multiple_of(v, n)


def layer_kernel(
    lens, tok_h, cot_h, g1_v, s1_v, g2_v, s2_v, b_out_v, b_down_v, bu, wq_h, wo_h, wu_h, wd_h,
    out_h, gt_h, d_qkv, d_out, d_up, d_down, vec_out,
    tok, n1, n1t, gm, gmt, n2, n2t, resid, macc, gacc, att, lse, wq, wo, wu, wd, bu_oth, bias_rows,
    grad, rc, rx, rz, rw, ry, ac, ax, az, aw, ay, ob, gl, gr, vs, vr,
    loc, agl_s, agl_r, att_s, att_r, m_s, m_r, a_s, a_r, e_s, e_r, o_sem,
):
    dp, mp = lax.axis_index("dp"), lax.axis_index("mp")
    core, x, z0, z1 = dp % 2, (dp // 2) % 2, (dp // 4) % 2, dp // 8
    to_c = (dp + 1 - 2 * core, mp)
    to_x = (dp + 2 - 4 * x, mp)
    to_z = (dp + 4 - 8 * z0, mp)
    to_w = (dp + 8 - 16 * z1, mp)
    to_y = (dp, 1 - mp)
    seq, width = n1.shape
    g1, s1, g2, s2, b_out, b_down = (v[...].reshape(1, width) for v in (g1_v, s1_v, g2_v, s2_v, b_out_v, b_down_v))

    def remote(src, dst, ss, rs, dev):
        return pltpu.make_async_remote_copy(
            src_ref=src, dst_ref=dst, send_sem=ss, recv_sem=rs, device_id=dev, device_id_type=MESH
        )

    def arrived(dst, rs, dev):
        remote(dst, dst, rs, rs, dev).wait_recv()

    def sent(src, ss, dev):
        remote(src, src, ss, ss, dev).wait_send()

    def local(src, dst, sem):
        return pltpu.make_async_copy(src, dst, sem)

    peer_tok = local(tok_h.at[1 - mp], tok.at[0], loc.at[0])
    own_tok = local(tok_h.at[mp], tok.at[1], loc.at[1])
    cot = local(cot_h.at[mp], gm, loc.at[2])
    wq_in = [local(wq_h.at[:, :, pl.ds(p * PAIR, PAIR)], wq.at[pl.ds(3 * p, 3)], loc.at[3 + p]) for p in range(3)]
    wo_in = local(wo_h, wo.at[pl.ds(0, 3)], loc.at[6])
    wu_in = [local(wu_h.at[:, pl.ds(j * PAIR, PAIR)], wu.at[j], loc.at[7 + j]) for j in range(12)]
    wd_in = local(wd_h, wd.at[pl.ds(0, 4)], loc.at[19])
    for c in [peer_tok] + wq_in + wu_in[:6] + [own_tok, cot, wo_in] + wu_in[6:] + [wd_in]:
        c.start()

    barrier = pltpu.get_barrier_semaphore()
    for dev in (to_c, to_x, to_z, to_w, to_y):
        pl.semaphore_signal(barrier, inc=1, device_id=dev, device_id_type=MESH)
    pl.semaphore_wait(barrier, 5)

    def span(i, other, at, n):
        unit = 16 if i == 0 else 96 if i < 5 else 48
        rows = pl.ds(aligned(at * unit, 16), n * unit)
        if i == 0:
            return wo.at[pl.ds(3 * other, 3), rows, :]
        if i < 5:
            return wu.at[pl.ds(12 * other + 3 * (i - 1), 3), rows, :]
        return wd.at[4 * other + i - 5, rows, :]

    def half_rows(other, c):
        return wq.at[pl.ds(9 * other, 9), pl.ds(aligned(c * 384, 384), 384), :]

    def axes_of(i):
        return (z0, x, to_z, to_x) if i >= 5 else (x, z0, to_x, to_z)

    def spot(i, r):
        if i == 9:
            return half_rows(1, core if r == 0 else 1 - core)
        first, second = axes_of(i)[:2]
        own = core * 4 + second * 2
        return [(own + first, 1), (own + 1 - first, 1), (core * 4 + (1 - second) * 2, 2), ((1 - core) * 4, 4)][r]

    def landed(i, r):
        return spot(i, r) if i == 9 else span(i, 1, *spot(i, r))

    def passed(i, r):
        if i == 9:
            return half_rows(int(r > 0), core)
        first, second = axes_of(i)[:2]
        own = core * 4 + second * 2
        if r == 0:
            return wo_h.at[:, pl.ds(aligned((own + first) * 16, 16), 16), :] if i == 0 else (
                wd_h.at[i - 5, pl.ds(aligned((own + first) * 48, 16), 48), :] if i >= 5 else span(i, 0, own + first, 1)
            )
        return span(i, 1, *[(own + first, 1), (own, 2), (core * 4, 4)][r - 1])

    def toward(i, r):
        return to_c if r == 3 else to_y if r == 0 else axes_of(i)[1 + r]

    def pass_on(i, r):
        if r > 0:
            before = 0 if i == 9 else r - 1
            arrived(landed(i, before), agl_r.at[i, before], to_y)
        into = landed(i, 0) if r == 0 else passed(i, r)
        remote(passed(i, r), into, agl_s.at[i, r], agl_r.at[i, r], toward(i, r)).start()

    def have(i):
        arrived(landed(i, 3), agl_r.at[i, 3], to_c)

    bu_copy = remote(bu, bu_oth, agl_s.at[10, 0], agl_r.at[10, 0], to_y)
    bu_copy.start()
    for i in (0, 5, 6):
        pass_on(i, 0)
    vs[0] = jnp.zeros_like(vs[0])

    lane = lax.broadcasted_iota(jnp.int32, (seq, PAIR), 1)
    place = lax.broadcasted_iota(jnp.int32, (seq, 1), 0)
    scale = HEAD_DIM**-0.5
    own_len = lens[mp]

    peer_tok.wait()
    for c in wq_in + wu_in[:6]:
        c.wait()
    for i in (1, 2):
        pass_on(i, 0)

    def att_copy(i):
        return (
            remote(att.at[i], att.at[6 + i], att_s.at[0, i], att_r.at[0, i], to_y),
            remote(lse.at[i], lse.at[6 + i], att_s.at[1, i], att_r.at[1, i], to_y),
        )

    def attend(i, _):
        chip, pair = i // 3, i % 3

        @pl.when(i == 3)
        def _():
            own_tok.wait()

        @pl.when(pair == 0)
        def _():
            xhat, _ = normalize(tok[chip].astype(F32))
            normed = (xhat * g1 + s1).astype(BF)
            n1[...] = normed

            @pl.when(chip == 1)
            def _():
                place_rows(n1t, normed.T)

        w = jnp.concatenate([wq[3 * pair], wq[3 * pair + 1], wq[3 * pair + 2]], axis=1)
        qkv = mm(n1[...], w).astype(BF)
        q = qkv[:, :PAIR] * jnp.asarray(scale, BF)
        k = qkv[:, PAIR : 2 * PAIR]
        vt = qkv[:, 2 * PAIR :].T
        visible = place < lens[(1 - mp) * (1 - chip) + mp * chip]
        outs = []
        for h in range(2):
            mine = (lane >= h * HEAD_DIM) & (lane < (h + 1) * HEAD_DIM)
            s = jnp.where(visible, mm_t(jnp.where(mine, k, jnp.zeros_like(k)), q), -1e30)
            top = jnp.max(s, 0, keepdims=True)
            e = jnp.exp(s - top)
            total = jnp.sum(e, 0, keepdims=True)
            lse[i, h : h + 1, :] = top + jnp.log(total)
            o = mm(vt[h * HEAD_DIM : (h + 1) * HEAD_DIM], e.astype(BF))
            outs.append(o / total)
        lse[i, 2:8, :] = jnp.zeros((6, seq), F32)
        att[i] = jnp.concatenate(outs, 0).T.astype(BF)

        @pl.when(chip == 0)
        def _():
            for c in att_copy(i):
                c.start()

        for when, steps in (
            (1, [(0, 1)]),
            (2, [(3, 0), (7, 0), (4, 0), (8, 0), (9, 0), (0, 2), (5, 1), (1, 1)]),
            (3, [(0, 3), (6, 1), (2, 1), (5, 2)]),
            (4, [(1, 2), (6, 2), (5, 3)]),
            (5, [(2, 2), (1, 3)]),
        ):

            @pl.when(i == when)
            def _(when=when, steps=steps):
                if when == 2:
                    for c in wu_in[6:]:
                        c.wait()
                for step in steps:
                    pass_on(*step)

        return 0

    lax.fori_loop(0, 6, attend, 0)

    cot.wait()
    visible = place < own_len
    g = jnp.where(visible, gm[...].astype(F32), 0.0)
    g_low = g.astype(BF)
    gm[...] = g_low
    place_rows(gmt, g_low.T)
    vs[0, 0:1, :] = jnp.sum(g, 0, keepdims=True)
    wo_in.wait()
    have(0)
    for i in range(3):
        arrived(att.at[6 + i], att_r.at[0, i], to_y)
        arrived(lse.at[6 + i], att_r.at[1, i], to_y)
    blocks = jnp.concatenate([att[3 + p] for p in range(6)], axis=1)
    r = tok[1].astype(F32) + mm(blocks, wo[...].reshape(6 * PAIR, width)) + b_out
    resid[...] = r
    xhat, _ = normalize(r)
    normed = (xhat * g2 + s2).astype(BF)
    n2[...] = normed
    place_rows(n2t, normed.T)
    macc[...] = jnp.zeros_like(macc)
    gacc[...] = jnp.zeros_like(gacc)

    half = 384

    def halved(n, turn):
        first, second = turn * x + (1 - turn) * z0, turn * z0 + (1 - turn) * x
        return sum(b * (384 >> k) for k, b in enumerate((core, first, second, z1)[:n]))

    def given(n, turn):
        first, second = turn * x + (1 - turn) * z0, turn * z0 + (1 - turn) * x
        return halved(n, turn) + (1 - (core, first, second, z1)[n]) * (384 >> n)

    def partner(n, turn):
        if n == 0:
            return to_c
        if n == 3:
            return to_w
        by_x = turn if n == 1 else 1 - turn
        return (dp + by_x * (2 - 4 * x) + (1 - by_x) * (4 - 8 * z0), mp)

    m_buf = [rc, rx, rz, rw]

    def m_copy(n, t):
        rows = 384 >> n
        turn = t % 2
        src = grad.at[t, :, pl.ds(aligned(given(n, turn), 16), rows), :]
        return remote(src, m_buf[n].at[t], m_s.at[n, t], m_r.at[n, t], partner(n, turn))

    def m_step(n, t):
        rows = 384 >> n
        turn = t % 2
        at = pl.ds(aligned(halved(n + 1, turn), 16), rows)
        arrived(m_buf[n].at[t], m_r.at[n, t], to_c)
        merge = n == 2 and t < 4
        if merge:
            arrived(ry.at[t], m_r.at[4, t], to_y)
        for w in range(2):
            total = grad[t, w, at, :].astype(F32) + m_buf[n][t, w].astype(F32)
            if n == 3:
                (d_up, d_down)[w][:, t * 384 : (t + 1) * 384] = total
                continue
            if merge:
                total += ry[t, w].astype(F32)
            grad[t, w, at, :] = total.astype(BF)
        if n < 2 or merge:
            m_copy(n + 1, t).start()
        elif n == 2:
            m_y(t).start()

    def m_step0(t):
        arrived(rc.at[t], m_r.at[0, t], to_c)
        at = pl.ds(aligned(core * 384, 384), 384)
        for w in range(2):
            grad[t, w, at, :] = (grad[t, w, at, :].astype(F32) + rc[t, w].astype(F32)).astype(BF)
        m_copy(1, t).start()

    def m_y(t):
        src = grad.at[t, :, pl.ds(aligned(halved(3, t % 2), 16), 2 * ROWS), :]
        return remote(src, ry.at[t - 4], m_s.at[4, t], m_r.at[4, t - 4], to_y)

    def tile(t, _):
        for when, steps, ready in (
            (0, [(6, 3), (2, 3)], []),
            (1, [(3, 1), (7, 1)], []),
            (2, [(4, 1), (8, 1), (3, 2), (7, 2)], []),
            (3, [(4, 2), (8, 2), (3, 3), (7, 3)], []),
            (4, [], [1, 5]),
            (5, [(4, 3), (8, 3)], [2, 6]),
            (6, [], [3, 7]),
            (7, [(9, 3)], [4, 8]),
        ):

            @pl.when(t == when)
            def _(when=when, steps=steps, ready=ready):
                if when == 0:
                    wd_in.wait()
                for i in ready:
                    have(i)
                for step in steps:
                    pass_on(*step)

        late = t // 4
        unit = t % 4
        wut = jnp.concatenate([wu[3 * t], wu[3 * t + 1], wu[3 * t + 2]], axis=1)
        wdt = wd[t]
        u = mm(n2[...], wut) + bias_rows[pl.ds(t, 1), :]
        act, slope = gelu_pair(u)
        act = act.astype(BF)
        gp = (mm_t(gm[...], wdt) * slope).astype(BF)
        row = 8 + 4 * (mp + late - 2 * mp * late) + unit
        vs[0, pl.ds(row, 1), 0:384] = jnp.sum(gp.astype(F32), 0, keepdims=True)
        macc[...] += mm(act, wdt)
        gacc[...] += mm_t(gp, wut)
        turn = t % 2
        store_rows(grad, (t, 0), mm(n2t[...], gp).astype(BF), turn)
        store_rows(grad, (t, 1), mm(gmt[...], act).astype(BF), turn)
        m_copy(0, t).start()

        @pl.when(t >= 1)
        def _():
            m_step0(t - 1)

        for j in range(3):

            @pl.when(t == 5 + j)
            def _(j=j):
                m_step(1, j)

        return 0

    arrived(bu_oth, agl_r.at[10, 0], to_y)
    for j in range(4):
        bias_rows[j : j + 1, :] = bu[j * 384 : (j + 1) * 384].reshape(1, 384)
        bias_rows[4 + j : 5 + j, :] = bu_oth[j * 384 : (j + 1) * 384].reshape(1, 384)
    lax.fori_loop(0, 8, tile, 0)

    r = resid[...]
    ob[...] = jnp.where(visible, r + macc[...] + b_down, 0.0).astype(BF)
    out_own = local(ob, out_h.at[mp], o_sem.at[0])
    out_far = remote(ob, out_h.at[mp], e_s.at[0], e_r.at[0], to_y)
    out_own.start()
    out_far.start()
    xhat, inv = normalize(r)
    gs = gacc[...]
    gres = gm[...].astype(F32) + norm_back(gs, xhat, inv, g2)
    low = gres.astype(BF)
    n2[...] = low
    place_rows(n2t, low.T)
    vs[0, 1:2, :] = jnp.sum(gs * xhat, 0, keepdims=True)
    vs[0, 2:3, :] = jnp.sum(gs, 0, keepdims=True)
    vs[0, 3:4, :] = jnp.sum(gres, 0, keepdims=True)
    resid[...] = gres
    gacc[...] = jnp.zeros_like(gacc)
    m_step0(7)
    m_step(1, 3)
    have(9)
    for i in range(1, 5):
        for r in range(4):
            sent(passed(i, r), agl_s.at[i, r], to_c)

    a_buf = [ac, ax, az, aw]

    def a_turn(p):
        return 1 - p % 3 % 2

    def a_copy(n, p):
        rows = 384 >> n
        turn = a_turn(p)
        src = wu.at[pl.ds(4 * p, 4), pl.ds(aligned(given(n, turn), 16), rows), :]
        return remote(src, a_buf[n].at[p], a_s.at[n, p], a_r.at[n, p], partner(n, turn))

    def a_step(n, p):
        rows = 384 >> n
        arrived(a_buf[n].at[p], a_r.at[n, p], to_c)
        merge = n == 2 and p < 3
        if merge:
            arrived(ay.at[p], a_r.at[4, p], to_y)
        at = pl.ds(aligned(halved(n + 1, a_turn(p)), 16), rows)
        for w in range(4):
            total = wu[4 * p + w, at, :].astype(F32) + a_buf[n][p, w].astype(F32)
            if n == 3:
                cols = slice(p * PAIR, (p + 1) * PAIR)
                if w < 3:
                    d_qkv[w, :, cols] = total
                else:
                    d_out[:, cols] = total
                continue
            if merge:
                total += ay[p, w].astype(F32)
            wu[4 * p + w, at, :] = total.astype(BF)
        if n < 2 or merge:
            a_copy(n + 1, p).start()
        elif n == 2:
            a_y(p).start()

    def a_y(p):
        src = wu.at[pl.ds(4 * p, 4), pl.ds(aligned(halved(3, a_turn(p)), 16), 2 * ROWS), :]
        return remote(src, ay.at[p - 3], a_s.at[4, p], a_r.at[4, p - 3], to_y)

    zero = jnp.zeros((seq, PAIR), BF)

    def back(k, _):
        p = (k + 3) % 6
        w = jnp.concatenate([wq[3 * p], wq[3 * p + 1], wq[3 * p + 2]], axis=1)
        qkv = mm(n1[...], w).astype(BF)
        q, key, v = qkv[:, :PAIR], qkv[:, PAIR : 2 * PAIR], qkv[:, 2 * PAIR :]
        q_s = q * jnp.asarray(scale, BF)
        ga = mm_t(n2[...], wo[p]).astype(BF)
        kt = key.T
        dqt = []
        dk = jnp.zeros((seq, PAIR), F32)
        dv = jnp.zeros((seq, PAIR), F32)
        for h in range(2):
            mine = (lane >= h * HEAD_DIM) & (lane < (h + 1) * HEAD_DIM)
            s = jnp.where(visible, mm_t(jnp.where(mine, key, zero), q_s), -1e30)
            prob = jnp.exp(s - lse[3 + p, h : h + 1, :])
            d_prob = mm_t(jnp.where(mine, v, zero), ga)
            row = jnp.sum(prob * d_prob, 0, keepdims=True)
            ds = (prob * (d_prob - row) * scale).astype(BF)
            dk += mm(ds, jnp.where(mine, q, zero))
            dv += mm(prob.astype(BF), jnp.where(mine, ga, zero))
            dqt.append(mm(kt[h * HEAD_DIM : (h + 1) * HEAD_DIM], ds))
        dq = jnp.concatenate(dqt, 0).T
        d = jnp.concatenate([dq.astype(BF), dk.astype(BF), dv.astype(BF)], axis=1)
        gacc[...] += mm_t(d, w)
        dw = mm(n1t[...], d).astype(BF)
        turn = a_turn(p)
        for c in range(3):
            store_rows(wu, (4 * p + c,), dw[:, c * PAIR : (c + 1) * PAIR], turn)
        store_rows(wu, (4 * p + 3,), mm(n2t[...], att[3 + p]).astype(BF), turn)
        a_copy(0, p).start()
        for when, m_steps, a_steps in (
            (0, [(1, 4)], []),
            (1, [(1, 5)], [(0, 3)]),
            (2, [(1, 6)], [(0, 4)]),
            (3, [(1, 7), (2, 4)], [(0, 5)]),
            (4, [(2, 5)], [(0, 0), (1, 3)]),
            (5, [(2, 6), (2, 0)], [(0, 1), (1, 4)]),
        ):

            @pl.when(k == when)
            def _(m_steps=m_steps, a_steps=a_steps):
                for step in a_steps:
                    a_step(*step)
                for step in m_steps:
                    m_step(*step)

        return 0

    lax.fori_loop(0, 6, back, 0)

    chunk = seq // 4

    def gt_copy(j):
        rows = pl.ds(j * chunk, chunk)
        return remote(gl.at[rows, :], gr.at[rows, :], e_s.at[1 + j], e_r.at[1 + j], to_y)

    gain_sum = jnp.zeros((1, width), F32)
    shift_sum = jnp.zeros((1, width), F32)
    for j in range(4):
        rows = slice(j * chunk, (j + 1) * chunk)
        xhat, inv = normalize(tok[1, rows].astype(F32))
        gf = gacc[rows]
        gt = resid[rows] + norm_back(gf, xhat, inv, g1)
        resid[rows] = gt
        gl[rows] = gt.astype(BF)
        gt_copy(j).start()
        gain_sum += jnp.sum(gf * xhat, 0, keepdims=True)
        shift_sum += jnp.sum(gf, 0, keepdims=True)
        if j == 0:
            a_step(0, 2)
    gt_own = local(resid, gt_h.at[mp], o_sem.at[1])
    gt_own.start()
    vs[0, 4:5, :] = gain_sum
    vs[0, 5:6, :] = shift_sum
    v_dev = [to_c, to_z, to_w, to_x, to_y]

    def v_copy(n):
        return remote(vs.at[n], vr.at[n], e_s.at[5 + n], e_r.at[5 + n], v_dev[n])

    def v_step(n):
        arrived(vr.at[n], e_r.at[5 + n], v_dev[n])
        if n < 4:
            vs[n + 1] = vs[n] + vr[n]
            v_copy(n + 1).start()
        else:
            vec_out[...] = vs[4] + vr[4]

    v_copy(0).start()
    for step in (
        (m_step, 2, 7), (m_step, 2, 1), (a_step, 1, 5), (a_step, 2, 3), (a_step, 2, 4), (v_step, 0),
        (m_step, 2, 2), (a_step, 1, 0), (a_step, 2, 5), (m_step, 2, 3), (m_step, 3, 0), (v_step, 1),
        (a_step, 1, 1), (m_step, 3, 1), (a_step, 2, 0), (v_step, 2),
        (a_step, 1, 2), (m_step, 3, 2), (a_step, 2, 1), (m_step, 3, 3), (v_step, 3),
        (a_step, 3, 0), (a_step, 2, 2), (a_step, 3, 1), (a_step, 3, 2),
    ):
        step[0](*step[1:])

    for j in range(4):
        rows = slice(j * chunk, (j + 1) * chunk)
        arrived(gr.at[pl.ds(j * chunk, chunk), :], e_r.at[1 + j], to_y)
        macc[rows] = gr[rows].astype(F32)
        local(macc.at[pl.ds(j * chunk, chunk), :], gt_h.at[1 - mp, pl.ds(j * chunk, chunk), :], o_sem.at[2 + j]).start()
    v_step(4)

    bu_copy.wait_send()
    for i in (0, 5, 6, 7, 8, 9):
        for r in (0, 3) if i == 9 else range(4):
            sent(passed(i, r), agl_s.at[i, r], to_c)
    for i in range(3):
        for c in att_copy(i):
            c.wait_send()

    def drain_m(t, _):
        for n in range(3):
            m_copy(n, t).wait_send()

        @pl.when(t < 4)
        def _():
            m_copy(3, t).wait_send()

        @pl.when(t >= 4)
        def _():
            m_y(t).wait_send()

        return 0

    lax.fori_loop(0, 8, drain_m, 0)

    def drain_a(p, _):
        for n in range(3):
            a_copy(n, p).wait_send()

        @pl.when(p < 3)
        def _():
            a_copy(3, p).wait_send()

        @pl.when(p >= 3)
        def _():
            a_y(p).wait_send()

        return 0

    lax.fori_loop(0, 6, drain_a, 0)
    for j in range(4):
        gt_copy(j).wait_send()
        local(macc.at[pl.ds(j * chunk, chunk), :], gt_h.at[1 - mp, pl.ds(j * chunk, chunk), :], o_sem.at[2 + j]).wait()
    for n in range(5):
        v_copy(n).wait_send()
    out_own.wait()
    out_far.wait_send()
    arrived(out_h.at[1 - mp], e_r.at[0], to_y)
    gt_own.wait()


def kernel_program(
    mp_n, tokens, lengths, ln1_gain, ln1_shift, w_qkv, w_out, b_out, ln2_gain, ln2_shift, w_up, b_up, w_down, b_down, cotangent
):
    seq, width = tokens.shape[1:]
    feat, hidden = w_qkv.shape[2], w_up.shape[1]
    tile = hidden // 4
    args = [
        lengths, tokens, cotangent, ln1_gain, ln1_shift, ln2_gain, ln2_shift, b_out, b_down,
        b_up, w_qkv, w_out.reshape(3, PAIR, width), w_up, w_down.reshape(4, tile, width),
    ]
    hbm, vmem = pl.BlockSpec(memory_space=pl.ANY), pl.BlockSpec(memory_space=pltpu.VMEM)
    outs = [
        sds(tokens.shape, BF),
        sds(tokens.shape, F32),
        sds((3, ROWS, feat), F32),
        sds((ROWS, feat), F32),
        sds((ROWS, hidden), F32),
        sds((ROWS, hidden), F32),
        sds((16, width), F32),
    ]
    v = pltpu.VMEM
    act = v((seq, width), BF)
    act_t = v((width, seq), BF)
    wide = v((seq, width), F32)
    scratch = [
        v((2, seq, width), BF), act, act_t, act, act_t, act, act_t, wide, wide, wide,
        v((9, seq, PAIR), BF), v((9, 8, seq), F32),
        v((18, width, PAIR), BF), v((6, PAIR, width), BF), v((24, width, PAIR), BF), v((8, tile, width), BF), v((hidden,), F32), v((8, tile), F32),
        v((8, 2, width, tile), BF),
        v((8, 2, 384, tile), BF), v((8, 2, 192, tile), BF), v((8, 2, 96, tile), BF), v((4, 2, 48, tile), BF), v((4, 2, 96, tile), BF),
        v((6, 4, 384, PAIR), BF), v((6, 4, 192, PAIR), BF), v((6, 4, 96, PAIR), BF), v((3, 4, 48, PAIR), BF), v((3, 4, 96, PAIR), BF),
        act, act, act, v((5, 16, width), F32), v((5, 16, width), F32),
    ]
    dma = pltpu.SemaphoreType.DMA
    scratch += [
        dma((20,)), dma((11, 4)), dma((11, 4)), dma((2, 3)), dma((2, 3)), dma((5, 8)), dma((5, 8)), dma((5, 6)), dma((5, 6)),
        dma((10,)), dma((10,)), dma((6,)),
    ]
    out, gt, d_qkv, d_out, d_up, d_down, vec = pl.pallas_call(
        layer_kernel,
        name="layer",
        out_shape=outs,
        in_specs=[pl.BlockSpec(memory_space=pltpu.SMEM), hbm, hbm] + [vmem] * 7 + [hbm] * 4,
        out_specs=[hbm, hbm] + [vmem] * 5,
        scratch_shapes=scratch,
        compiler_params=pltpu.CompilerParams(collective_id=0, has_side_effects=True, vmem_limit_bytes=VMEM_ALL),
    )(*args)
    dp, mp = lax.axis_index("dp"), lax.axis_index("mp")
    shard = lax.dynamic_slice_in_dim(vec[:6], dp * ROWS, ROWS, 1)
    bias = vec[8:, :tile].reshape(mp_n, hidden)
    bias = lax.dynamic_slice(bias, (mp, dp * 2 * ROWS), (1, 2 * ROWS))
    return (
        out, gt, shard[4], shard[5], d_qkv, d_out.T, shard[3], shard[1], shard[2], d_up, bias, d_down.T, shard[0],
    )


def solution(mesh):
    dp_n, mp_n = mesh.shape["dp"], mesh.shape["mp"]
    body = functools.partial(kernel_program, mp_n) if dp_n == 16 else functools.partial(permute_program, dp_n, mp_n)
    return jax.shard_map(
        body,
        mesh=mesh,
        in_specs=(
            P("dp", None, None),
            P("dp"),
            P(),
            P(),
            P(None, None, "mp"),
            P("mp", None),
            P(),
            P(),
            P(),
            P(None, "mp"),
            P("mp"),
            P("mp", None),
            P(),
            P("dp", None, None),
        ),
        out_specs=(
            P("dp", None, None),
            P("dp", None, None),
            P("dp"),
            P("dp"),
            P(None, "dp", "mp"),
            P("mp", "dp"),
            P("dp"),
            P("dp"),
            P("dp"),
            P("dp", "mp"),
            P("mp", "dp"),
            P("mp", "dp"),
            P("dp"),
        ),
        check_vma=False,
    )
```

```python
import functools

import jax
import jax.numpy as jnp
from jax import lax
from jax.experimental import pallas as pl
from jax.experimental.pallas import tpu as pltpu
from jax.sharding import PartitionSpec as P

HEAD_DIM = 64
PAIR = 2 * HEAD_DIM
BF = jnp.bfloat16
F32 = jnp.float32
EPS = 1e-05
LIMIT = 40 * 1024 * 1024

TAIL_P = 0.3
TAIL_C = (
    0.11962929256864907,
    0.12075406313917503,
    0.09991275007605285,
    0.12856432480895655,
    -0.05368921426491713,
    0.2063600527786208,
    -0.1572071533588575,
    0.03567581131365836,
)


def mm(a, b):
    return lax.dot_general(a, b, (((1,), (0,)), ((), ())), preferred_element_type=F32)


def mm_t(a, b):
    return lax.dot_general(a, b, (((1,), (1,)), ((), ())), preferred_element_type=F32)


def normalize(x):
    mean = jnp.mean(x, -1, keepdims=True)
    center = x - mean
    var = jnp.mean(center * center, -1, keepdims=True)
    inv = lax.rsqrt(var + EPS)
    return center * inv, inv


def norm_back(grad, xhat, inv, gain):
    d = grad * gain
    m1 = jnp.mean(d, -1, keepdims=True)
    m2 = jnp.mean(d * xhat, -1, keepdims=True)
    return inv * (d - m1 - xhat * m2)


def bit_reverse(index, bits):
    out = 0
    for b in range(bits):
        out = (out << 1) | ((index >> b) & 1)
    return out


def put_rows(ref, value, blocks):
    rows = value.shape[0] // blocks
    bits = blocks.bit_length() - 1
    if rows % 16:
        ref[...] = value
        return
    for b in range(blocks):
        d = bit_reverse(b, bits)
        ref[d * rows : (d + 1) * rows, :] = value[b * rows : (b + 1) * rows, :]


def order_rows(value, blocks):
    rows = value.shape[0] // blocks
    if rows % 16 == 0:
        return value
    bits = blocks.bit_length() - 1
    split = value.reshape((2,) * bits + (rows, value.shape[1]))
    split = split.transpose(tuple(reversed(range(bits))) + (bits, bits + 1))
    return split.reshape(value.shape)


def call(body, name, out_shape, args, flops, grid=None, in_specs=None, out_specs=None, scalars=None, scratch=(), aliases=None):
    nbytes = sum(a.size * a.dtype.itemsize for a in args)
    nbytes += sum(o.size * o.dtype.itemsize for o in out_shape)
    if in_specs is None:
        in_specs = [whole(a.shape) for a in args]
    if out_specs is None:
        out_specs = [whole(o.shape) for o in out_shape]
    return pl.pallas_call(
        body,
        name=name,
        out_shape=out_shape,
        grid_spec=pltpu.PrefetchScalarGridSpec(
            num_scalar_prefetch=1,
            grid=grid or (1,),
            in_specs=in_specs,
            out_specs=out_specs,
            scratch_shapes=list(scratch),
        ),
        input_output_aliases=aliases or {},
        compiler_params=pltpu.CompilerParams(vmem_limit_bytes=LIMIT),
        cost_estimate=pl.CostEstimate(flops=flops, bytes_accessed=nbytes, transcendentals=0),
    )(scalars, *args)


def whole(shape):
    return pl.BlockSpec(shape, lambda *_: (0,) * len(shape))


def sds(shape, dtype):
    return jax.ShapeDtypeStruct(shape, dtype)


def chip_spec(shape):
    return pl.BlockSpec((None,) + tuple(shape[1:]), lambda i, sc: (sc[0], 0, 0))


def attention_kernel(sc, tok, gain, shift, w_ref, att_ref, lse_ref, normed):
    @pl.when(pl.program_id(0) == 0)
    def _():
        xhat, _ = normalize(tok[...].astype(F32))
        normed[...] = (xhat * gain[...] + shift[...]).astype(BF)

    seq = normed.shape[0]
    w = jnp.concatenate([w_ref[0], w_ref[1], w_ref[2]], axis=1)
    qkv = mm(normed[...], w).astype(BF)
    scale = HEAD_DIM**-0.5
    q = qkv[:, :PAIR] * jnp.asarray(scale, BF)
    k = qkv[:, PAIR : 2 * PAIR]
    vt = qkv[:, 2 * PAIR :].T
    lane = lax.broadcasted_iota(jnp.int32, (seq, PAIR), 1)
    visible = lax.broadcasted_iota(jnp.int32, (seq, 1), 0) < sc[1]
    outs = []
    for h in range(2):
        mine = (lane >= h * HEAD_DIM) & (lane < (h + 1) * HEAD_DIM)
        kh = jnp.where(mine, k, jnp.zeros_like(k))
        s = jnp.where(visible, mm_t(kh, q), -1e30)
        top = jnp.max(s, 0, keepdims=True)
        e = jnp.exp(s - top)
        total = jnp.sum(e, 0, keepdims=True)
        lse_ref[h : h + 1, :] = top + jnp.log(total)
        o = mm(vt[h * HEAD_DIM : (h + 1) * HEAD_DIM], e.astype(BF))
        outs.append(o / total)
    att_ref[...] = jnp.concatenate(outs, 0).T.astype(BF)
    lse_ref[2:8, :] = jnp.zeros((6, seq), F32)


def prepare_kernel(blocks, sc, tok, cot, gain, shift, n1, n1t, gm, gmt, vec):
    xhat, _ = normalize(tok[...].astype(F32))
    normed = (xhat * gain[...] + shift[...]).astype(BF)
    n1[...] = normed
    put_rows(n1t, normed.T, blocks)
    seq = normed.shape[0]
    visible = lax.broadcasted_iota(jnp.int32, (seq, 1), 0) < sc[1]
    g = jnp.where(visible, cot[...].astype(F32), 0.0)
    gl = g.astype(BF)
    gm[...] = gl
    put_rows(gmt, gl.T, blocks)
    vec[...] = jnp.broadcast_to(jnp.sum(g, 0, keepdims=True), vec.shape)


def project_kernel(blocks, sc, tok, att_a, att_b, wo_a, wo_b, b_out, gain, shift, resid, n2, n2t):
    x = tok[...].astype(F32)
    r = x + mm(att_a[...], wo_a[...]) + mm(att_b[...], wo_b[...]) + b_out[...]
    resid[...] = r
    xhat, _ = normalize(r)
    normed = (xhat * gain[...] + shift[...]).astype(BF)
    n2[...] = normed
    put_rows(n2t, normed.T, blocks)


def gelu_pair(u):
    z = jnp.abs(u)
    t = 1.0 / (1.0 + TAIL_P * z)
    poly = TAIL_C[-1]
    for c in TAIL_C[-2::-1]:
        poly = poly * t + c
    e = jnp.exp(-0.5 * u * u)
    tail = e * (poly * t)
    cdf = jnp.where(u < 0, tail, 1.0 - tail)
    return u * cdf, cdf + u * e * 0.3989422804014327


def mlp_kernel(tiles, first, cross, sc, *refs):
    n2, n2t, gm, gmt = refs[:4]
    wu = refs[4 : 4 + tiles]
    wd = refs[4 + tiles : 4 + 2 * tiles]
    bu = refs[4 + 2 * tiles]
    at = 5 + 2 * tiles
    if not first:
        macc_in, gacc_in, db_in = refs[at : at + 3]
        at += 3
    keep, send, macc, gacc, db = refs[at:]
    width = wu[0].shape[1]
    half = keep.shape[1]
    core = sc[0]
    db[...] = jnp.zeros_like(db) if first else db_in[...]
    for t in range(tiles):
        wut, wdt = wu[t][...], wd[t][...]
        u = mm(n2[...], wut) + bu[pl.ds(sc[1 + 2 * t], 1), :]
        act, slope = gelu_pair(u)
        act = act.astype(BF)
        gp = (mm_t(gm[...], wdt) * slope).astype(BF)
        db[pl.ds(sc[2 + 2 * t], 1), :] = jnp.sum(gp.astype(F32), 0, keepdims=True)
        m, g = mm(act, wdt), mm_t(gp, wut)
        if t == 0 and first:
            macc[...], gacc[...] = m, g
        elif t == 0:
            macc[...], gacc[...] = macc_in[...] + m, gacc_in[...] + g
        else:
            macc[...] += m
            gacc[...] += g
        for which, (lhs, rhs) in enumerate(((n2t, gp), (gmt, act))):
            grad = mm(lhs[...], rhs).astype(BF)
            top, low = grad[:half], grad[half:]
            other = (t ^ 1) if cross else t
            keep[which, :, t * width : (t + 1) * width] = jnp.where(core == 0, top, low)
            send[which, :, other * width : (other + 1) * width] = jnp.where(core == 0, low, top)


def middle_kernel(blocks, sc, resid, macc, gacc, gm, b_down, gain, out, gres, rl, rlt, vec):
    r = resid[...]
    seq = r.shape[0]
    visible = lax.broadcasted_iota(jnp.int32, (seq, 1), 0) < sc[1]
    out[...] = jnp.where(visible, r + macc[...] + b_down[...], 0.0).astype(BF)
    xhat, inv = normalize(r)
    gs = gacc[...]
    gr = gm[...].astype(F32) + norm_back(gs, xhat, inv, gain[...])
    gres[...] = gr
    low = gr.astype(BF)
    rl[...] = low
    put_rows(rlt, low.T, blocks)
    vec[0:1, :] = jnp.sum(gs * xhat, 0, keepdims=True)
    vec[1:2, :] = jnp.sum(gs, 0, keepdims=True)
    vec[2:3, :] = jnp.sum(gr, 0, keepdims=True)
    vec[3:8, :] = jnp.zeros((5, vec.shape[1]), F32)


def attention_back_kernel(first, sc, *refs):
    n1, n1t, rl, rlt, att, lse, w_ref, wo = refs[:8]
    at = 8
    if not first:
        gf_in = refs[at]
        at += 1
    keep, send, gf = refs[at:]
    seq = n1.shape[0]
    half = keep.shape[1]
    scale = HEAD_DIM**-0.5
    w = jnp.concatenate([w_ref[0], w_ref[1], w_ref[2]], axis=1)
    qkv = mm(n1[...], w).astype(BF)
    q, k, v = qkv[:, :PAIR], qkv[:, PAIR : 2 * PAIR], qkv[:, 2 * PAIR :]
    qs = q * jnp.asarray(scale, BF)
    ga = mm_t(rl[...], wo[...]).astype(BF)
    kt = k.T
    lane = lax.broadcasted_iota(jnp.int32, (seq, PAIR), 1)
    visible = lax.broadcasted_iota(jnp.int32, (seq, 1), 0) < sc[1]
    zero = jnp.zeros_like(q)
    dqt = []
    dk = jnp.zeros((seq, PAIR), F32)
    dv = jnp.zeros((seq, PAIR), F32)
    for h in range(2):
        mine = (lane >= h * HEAD_DIM) & (lane < (h + 1) * HEAD_DIM)
        s = jnp.where(visible, mm_t(jnp.where(mine, k, zero), qs), -1e30)
        p = jnp.exp(s - lse[h : h + 1, :])
        dp = mm_t(jnp.where(mine, v, zero), ga)
        row = jnp.sum(p * dp, 0, keepdims=True)
        ds = (p * (dp - row) * scale).astype(BF)
        dk += mm(ds, jnp.where(mine, q, zero))
        dv += mm(p.astype(BF), jnp.where(mine, ga, zero))
        dqt.append(mm(kt[h * HEAD_DIM : (h + 1) * HEAD_DIM], ds))
    dq = jnp.concatenate(dqt, 0).T
    d = jnp.concatenate([dq.astype(BF), dk.astype(BF), dv.astype(BF)], axis=1)
    g = mm_t(d, w)
    begin = pl.program_id(0) == 0

    @pl.when(begin)
    def _():
        gf[...] = g if first else gf_in[...] + g

    @pl.when(jnp.logical_not(begin))
    def _():
        gf[...] += g

    core = sc[0]
    dw = mm(n1t[...], d).astype(BF)
    dwo = mm(rlt[...], att[...]).astype(BF)
    parts = [dw[:, c * PAIR : (c + 1) * PAIR] for c in range(3)] + [dwo]
    for c, part in enumerate(parts):
        top, low = part[:half], part[half:]
        keep[c] = jnp.where(core == 0, top, low)
        send[c] = jnp.where(core == 0, low, top)


def last_kernel(sc, tok, gres, gf, gain, gt, gtl, vec):
    xhat, inv = normalize(tok[...].astype(F32))
    g = gf[...]
    out = gres[...] + norm_back(g, xhat, inv, gain[...])
    gt[...] = out
    gtl[...] = out.astype(BF)
    vec[0:1, :] = jnp.sum(g * xhat, 0, keepdims=True)
    vec[1:2, :] = jnp.sum(g, 0, keepdims=True)
    vec[2:8, :] = jnp.zeros((6, vec.shape[1]), F32)


def permute_program(
    dp_n,
    mp_n,
    tokens,
    lengths,
    ln1_gain,
    ln1_shift,
    w_qkv,
    w_out,
    b_out,
    ln2_gain,
    ln2_shift,
    w_up,
    b_up,
    w_down,
    b_down,
    cotangent,
):
    chips, seq, width = tokens.shape
    feat = w_qkv.shape[2]
    hidden = w_up.shape[1]
    tile = hidden // 4
    pairs = feat // PAIR
    bits = dp_n.bit_length() - 1
    half = width // 2
    mp = lax.axis_index("mp")
    dp = lax.axis_index("dp")
    core = dp & 1
    two = dp & 3
    quarter = ((two & 1) << 1) | (two >> 1)
    i32 = jnp.int32

    def swap_y(x):
        return lax.ppermute(x, "mp", [(i, i ^ 1) for i in range(mp_n)])

    def swap_d(x, bit):
        return lax.ppermute(x, "dp", [(i, i ^ (1 << bit)) for i in range(dp_n)])

    own_sc = jnp.stack([mp, lengths[mp]]).astype(i32)
    peer_sc = jnp.stack([1 - mp, lengths[1 - mp]]).astype(i32)
    row = lambda v: v.reshape(1, -1)
    g1, s1, g2, s2, bo, bd = map(row, (ln1_gain, ln1_shift, ln2_gain, ln2_shift, b_out, b_down))

    hw = feat // 2
    wo_r0 = swap_y(lax.dynamic_slice_in_dim(w_out, core * hw, hw, 0))
    wo_r1 = swap_d(wo_r0, 0)
    wo_oth = jnp.where(core == 0, jnp.concatenate([wo_r0, wo_r1], 0), jnp.concatenate([wo_r1, wo_r0], 0))
    bu_own = b_up.reshape(4, tile)
    bu_oth = swap_y(bu_own)

    def attention(sc):
        return call(
            attention_kernel,
            "attention_fwd",
            [sds((seq, feat), BF), sds((pairs, 8, seq), F32)],
            [tokens, g1, s1, w_qkv],
            2 * seq * width * 3 * feat + 4 * seq * seq * feat,
            grid=(pairs,),
            in_specs=[
                chip_spec(tokens.shape),
                whole(g1.shape),
                whole(s1.shape),
                pl.BlockSpec((3, width, PAIR), lambda i, sc: (0, 0, i)),
            ],
            out_specs=[
                pl.BlockSpec((seq, PAIR), lambda i, sc: (0, i)),
                pl.BlockSpec((None, 8, seq), lambda i, sc: (i, 0, 0)),
            ],
            scalars=sc,
            scratch=[pltpu.VMEM((seq, width), BF)],
        )

    att_peer, lse_peer = attention(peer_sc)
    att_oth, lse_oth = swap_y(att_peer), swap_y(lse_peer)

    wu_r, wd_r = [None] * 4, [None] * 4
    for name, store, axis, src in (("u", wu_r, 1, w_up), ("d", wd_r, 0, w_down)):
        store[0] = swap_y(lax.dynamic_slice_in_dim(src, quarter * tile, tile, axis))
        store[1] = swap_d(store[0], 0)
        store[2] = swap_d(store[0], 1)
        store[3] = swap_d(store[2], 0)

    att_own, lse_own = attention(own_sc)

    n1, n1t, gm, gmt, vec_g = call(
        functools.partial(prepare_kernel, dp_n),
        "prepare",
        [sds((seq, width), BF), sds((width, seq), BF), sds((seq, width), BF), sds((width, seq), BF), sds((8, width), F32)],
        [tokens, cotangent, g1, s1],
        20 * seq * width,
        in_specs=[chip_spec(tokens.shape), chip_spec(cotangent.shape), whole(g1.shape), whole(s1.shape)],
        scalars=own_sc,
    )
    resid, n2, n2t = call(
        functools.partial(project_kernel, dp_n),
        "project",
        [sds((seq, width), F32), sds((seq, width), BF), sds((width, seq), BF)],
        [tokens, att_own, att_oth, w_out, wo_oth, bo, g2, s2],
        4 * seq * width * feat,
        in_specs=[chip_spec(tokens.shape)] + [whole(a.shape) for a in (att_own, att_oth, w_out, wo_oth, bo, g2, s2)],
        scalars=own_sc,
    )
    n1t, gmt, n2t = (order_rows(t, dp_n) for t in (n1t, gmt, n2t))

    own_half, oth_half = mp * 4, (1 - mp) * 4

    def mlp(first, cross, wus, wds, bias, slots, base, accs, specs):
        sc = [core]
        for a in slots:
            sc += [a, base + a]
        outs = [
            sds((2, half, 2 * tile), BF),
            sds((2, half, 2 * tile), BF),
            sds((seq, width), F32),
            sds((seq, width), F32),
            sds((8, tile), F32),
        ]
        args = [n2, n2t, gm, gmt, *wus, *wds, bias, *accs]
        in_specs = [whole(a.shape) for a in args]
        if specs:
            in_specs[4:8] = specs
        return call(
            functools.partial(mlp_kernel, 2, first, cross),
            "mlp_tiles",
            outs,
            args,
            12 * seq * width * 2 * tile,
            in_specs=in_specs,
            scalars=jnp.stack(sc).astype(i32),
            aliases={} if first else {10: 2, 11: 3, 12: 4},
        )

    def own_specs(a):
        return [pl.BlockSpec((width, tile), lambda i, sc, t=t: (0, t)) for t in (a, a + 1)] + [
            pl.BlockSpec((tile, width), lambda i, sc, t=t: (t, 0)) for t in (a, a + 1)
        ]

    pieces = []
    accs = []
    const = lambda v: jnp.asarray(v, i32)
    for a in (0, 2):
        k, s, *accs = mlp(
            a == 0, False, [w_up] * 2, [w_down] * 2, bu_own, [const(a), const(a + 1)], own_half, accs, own_specs(a)
        )
        pieces.append((k, s))
    mine = [quarter, quarter ^ 2, quarter ^ 1, quarter ^ 3]
    for a in (0, 2):
        k, s, *accs = mlp(
            False, True, wu_r[a : a + 2], wd_r[a : a + 2], bu_oth, mine[a : a + 2], oth_half, accs, None
        )
        pieces.append((k, s))
    macc, gacc, db = accs

    out_own, gres, rl, rlt, vec_mid = call(
        functools.partial(middle_kernel, dp_n),
        "middle",
        [sds((seq, width), BF), sds((seq, width), F32), sds((seq, width), BF), sds((width, seq), BF), sds((8, width), F32)],
        [resid, macc, gacc, gm, bd, g2],
        40 * seq * width,
        scalars=own_sc,
    )
    out_oth = swap_y(out_own)
    rlt = order_rows(rlt, dp_n)

    hq = width // 4
    wq_r = [None] * 4
    wq_r[0] = swap_y(lax.dynamic_slice_in_dim(w_qkv, quarter * hq, hq, 1))
    wq_r[1] = swap_d(wq_r[0], 0)
    wq_r[2] = swap_d(wq_r[0], 1)
    wq_r[3] = swap_d(wq_r[2], 0)
    wq_oth = jnp.concatenate(wq_r, 1)
    for r in range(4):
        wq_oth = lax.dynamic_update_slice_in_dim(wq_oth, wq_r[r], mine[r] * hq, 1)

    def attention_back(first, wq, wo, att, lse, accs):
        args = [n1, n1t, rl, rlt, att, lse, wq, wo, *accs]
        in_specs = [whole(a.shape) for a in args]
        in_specs[4] = pl.BlockSpec((seq, PAIR), lambda i, sc: (0, i))
        in_specs[5] = pl.BlockSpec((None, 8, seq), lambda i, sc: (i, 0, 0))
        in_specs[6] = pl.BlockSpec((3, width, PAIR), lambda i, sc: (0, 0, i))
        in_specs[7] = pl.BlockSpec((PAIR, width), lambda i, sc: (i, 0))
        piece = pl.BlockSpec((4, half, PAIR), lambda i, sc: (0, 0, i))
        return call(
            functools.partial(attention_back_kernel, first),
            "attention_bwd",
            [sds((4, half, feat), BF), sds((4, half, feat), BF), sds((seq, width), F32)],
            args,
            2 * seq * width * feat * 11 + 10 * seq * seq * feat,
            grid=(pairs,),
            in_specs=in_specs,
            out_specs=[piece, piece, whole((seq, width))],
            scalars=jnp.stack([core, own_sc[1]]).astype(i32),
            aliases={} if first else {9: 2},
        )

    k, s, gf = attention_back(True, w_qkv, w_out, att_own, lse_own, [])
    pieces.append((k, s))
    k, s, gf = attention_back(False, wq_oth, wo_oth, att_oth, lse_oth, [gf])
    pieces.append((k, s))

    gt_own, gt_low, vec_last = call(
        last_kernel,
        "last",
        [sds((seq, width), F32), sds((seq, width), BF), sds((8, width), F32)],
        [tokens, gres, gf, g1],
        30 * seq * width,
        in_specs=[chip_spec(tokens.shape)] + [whole(a.shape) for a in (gres, gf, g1)],
        scalars=own_sc,
    )
    gt_oth = swap_y(gt_low).astype(F32)

    def add(a, b):
        return (a.astype(F32) + b.astype(F32)).astype(BF)

    def split(x, bit):
        n = x.shape[1] // 2
        b = (dp >> bit) & 1
        return (
            lax.dynamic_slice_in_dim(x, b * n, n, 1),
            lax.dynamic_slice_in_dim(x, (1 - b) * n, n, 1),
        )

    state = [add(k, swap_d(s, 0)) for k, s in pieces]
    for bit in range(1, bits):
        parts = [split(x, bit) for x in state]
        got = [swap_d(s, bit) for _, s in parts]
        if bit == 1:
            got[2], got[3] = got[3], got[2]
        state = [add(p[0], g) for p, g in zip(parts, got)]
    own1, own2, oth1, oth2, at_own, at_oth = state
    rows = own1.shape[1]
    got1, got2, got_at = swap_y(oth1), swap_y(oth2), swap_y(at_oth)

    slots = jnp.stack([got1[..., :tile], got1[..., tile:], got2[..., :tile], got2[..., tile:]])
    got = [lax.dynamic_index_in_dim(slots, slot_of(a, two), 0, keepdims=False) for a in range(4)]
    mine_mlp = [own1[..., :tile], own1[..., tile:], own2[..., :tile], own2[..., tile:]]
    total = jnp.concatenate([m.astype(F32) + g.astype(F32) for m, g in zip(mine_mlp, got)], -1)
    total_at = at_own.astype(F32) + got_at.astype(F32)

    vecs = jnp.concatenate([vec_g[:1], vec_mid[:3], vec_last[:2], db.reshape(-1, width)], 0)
    for bit in range(bits):
        vecs = vecs + swap_d(vecs, bit)
    vecs = vecs + swap_y(vecs)
    shard = lax.dynamic_slice_in_dim(vecs[:6], dp * rows, rows, 1)
    bias = vecs[6:].reshape(mp_n, hidden)
    cols = hidden // dp_n
    bias = lax.dynamic_slice(bias, (mp, dp * cols), (1, cols))

    def both(own, oth):
        return jnp.where(mp == 0, jnp.stack([own, oth]), jnp.stack([oth, own]))

    return (
        both(out_own, out_oth),
        both(gt_own, gt_oth),
        shard[4],
        shard[5],
        total_at[:3],
        total_at[3].T,
        shard[3],
        shard[1],
        shard[2],
        total[0],
        bias,
        total[1].T,
        shard[0],
    )


def slot_of(a, two):
    q = ((two & 1) << 1) | (two >> 1)
    d = q ^ a
    return ((d & 1) << 1) | (d >> 1)


MESH = pl.DeviceIdType.MESH
ROWS = 48
VMEM_ALL = 67043328


def place_rows(ref, value):
    for b in range(16):
        p = bit_reverse(b, 4)
        ref[p * ROWS : (p + 1) * ROWS, :] = value[b * ROWS : (b + 1) * ROWS, :]


def store_rows(ref, index, value, turn):
    rows = value.shape[0] // 8
    for b in range(8):
        c, i, j = b // 4, (b // 2) % 2, b % 2
        if i == j:
            at = pl.ds(b * rows, rows)
        else:
            at = pl.ds(aligned((4 * c + 1) * rows + (i * turn + j * (1 - turn)) * rows, 16), rows)
        ref[(*index, at, slice(None))] = value[b * rows : (b + 1) * rows]


def aligned(v, n):
    return pl.multiple_of(v, n)


def layer_kernel(
    lens, tok_h, cot_h, g1_v, s1_v, g2_v, s2_v, b_out_v, b_down_v, bu, wq_h, wo_h, wu_h, wd_h,
    out_h, gt_h, gt_far, d_qkv, d_out, d_up, d_down, vec_out,
    tok, n1, n1t, gm, gmt, n2, n2t, resid, macc, gacc, att, lse, wq, wo, wu, wd, bu_oth, bias_rows,
    grad, rc, rx, rz, rw, ry, ac, ax, az, aw, ay, ob, gl, vs, vr,
    loc, agl_s, agl_r, att_s, att_r, m_s, m_r, a_s, a_r, e_s, e_r, o_sem,
):
    dp, mp = lax.axis_index("dp"), lax.axis_index("mp")
    core, x, z0, z1 = dp % 2, (dp // 2) % 2, (dp // 4) % 2, dp // 8
    to_c = (dp + 1 - 2 * core, mp)
    to_x = (dp + 2 - 4 * x, mp)
    to_z = (dp + 4 - 8 * z0, mp)
    to_w = (dp + 8 - 16 * z1, mp)
    to_y = (dp, 1 - mp)
    seq, width = n1.shape
    g1, s1, g2, s2, b_out, b_down = (v[...].reshape(1, width) for v in (g1_v, s1_v, g2_v, s2_v, b_out_v, b_down_v))

    def remote(src, dst, ss, rs, dev):
        return pltpu.make_async_remote_copy(
            src_ref=src, dst_ref=dst, send_sem=ss, recv_sem=rs, device_id=dev, device_id_type=MESH
        )

    def arrived(dst, rs, dev):
        remote(dst, dst, rs, rs, dev).wait_recv()

    def sent(src, ss, dev):
        remote(src, src, ss, ss, dev).wait_send()

    def local(src, dst, sem):
        return pltpu.make_async_copy(src, dst, sem)

    peer_tok = local(tok_h.at[1 - mp], tok.at[0], loc.at[0])
    own_tok = local(tok_h.at[mp], tok.at[1], loc.at[1])
    cot = local(cot_h.at[mp], gm, loc.at[2])
    wq_in = [local(wq_h.at[:, :, pl.ds(p * PAIR, PAIR)], wq.at[pl.ds(3 * p, 3)], loc.at[3 + p]) for p in range(3)]
    wo_in = local(wo_h, wo.at[pl.ds(0, 3)], loc.at[6])
    wu_in = [local(wu_h.at[:, pl.ds(j * PAIR, PAIR)], wu.at[j], loc.at[7 + j]) for j in range(12)]
    wd_in = local(wd_h, wd.at[pl.ds(0, 4)], loc.at[19])
    for c in [peer_tok] + wq_in + wu_in[:3] + [own_tok, cot, wo_in] + wu_in[3:] + [wd_in]:
        c.start()

    barrier = pltpu.get_barrier_semaphore()
    for dev in (to_c, to_x, to_z, to_w, to_y):
        pl.semaphore_signal(barrier, inc=1, device_id=dev, device_id_type=MESH)
    pl.semaphore_wait(barrier, 5)

    def span(i, other, at, n):
        unit = 16 if i == 0 else 96 if i < 5 else 48
        rows = pl.ds(aligned(at * unit, 16), n * unit)
        if i == 0:
            return wo.at[pl.ds(3 * other, 3), rows, :]
        if i < 5:
            return wu.at[pl.ds(12 * other + 3 * (i - 1), 3), rows, :]
        return wd.at[4 * other + i - 5, rows, :]

    def half_rows(other, c):
        return wq.at[pl.ds(9 * other, 9), pl.ds(aligned(c * 384, 384), 384), :]

    def axes_of(i):
        return (z0, x, to_z, to_x) if i >= 5 else (x, z0, to_x, to_z)

    def spot(i, r):
        if i == 9:
            return half_rows(1, core if r == 0 else 1 - core)
        first, second = axes_of(i)[:2]
        own = core * 4 + second * 2
        return [(own + first, 1), (own + 1 - first, 1), (core * 4 + (1 - second) * 2, 2), ((1 - core) * 4, 4)][r]

    def landed(i, r):
        return spot(i, r) if i == 9 else span(i, 1, *spot(i, r))

    def passed(i, r):
        if i == 9:
            return half_rows(int(r > 0), core)
        first, second = axes_of(i)[:2]
        own = core * 4 + second * 2
        if r == 0:
            return wo_h.at[:, pl.ds(aligned((own + first) * 16, 16), 16), :] if i == 0 else (
                wd_h.at[i - 5, pl.ds(aligned((own + first) * 48, 16), 48), :] if i >= 5 else span(i, 0, own + first, 1)
            )
        return span(i, 1, *[(own + first, 1), (own, 2), (core * 4, 4)][r - 1])

    def toward(i, r):
        return to_c if r == 3 else to_y if r == 0 else axes_of(i)[1 + r]

    def pass_on(i, r):
        if r > 0:
            before = 0 if i == 9 else r - 1
            arrived(landed(i, before), agl_r.at[i, before], to_y)
        into = landed(i, 0) if r == 0 else passed(i, r)
        remote(passed(i, r), into, agl_s.at[i, r], agl_r.at[i, r], toward(i, r)).start()

    def have(i):
        arrived(landed(i, 3), agl_r.at[i, 3], to_c)

    bu_copy = remote(bu, bu_oth, agl_s.at[10, 0], agl_r.at[10, 0], to_y)
    bu_copy.start()
    for i in (0, 5):
        pass_on(i, 0)
    vs[0] = jnp.zeros_like(vs[0])

    lane = lax.broadcasted_iota(jnp.int32, (seq, PAIR), 1)
    place = lax.broadcasted_iota(jnp.int32, (seq, 1), 0)
    scale = HEAD_DIM**-0.5
    own_len = lens[mp]

    peer_tok.wait()
    for c in wq_in + wu_in[:3]:
        c.wait()
    pass_on(1, 0)

    def att_copy(i):
        return (
            remote(att.at[i], att.at[6 + i], att_s.at[0, i], att_r.at[0, i], to_y),
            remote(lse.at[i], lse.at[6 + i], att_s.at[1, i], att_r.at[1, i], to_y),
        )

    def attend(i, _):
        chip, pair = i // 3, i % 3

        @pl.when(i == 3)
        def _():
            own_tok.wait()

        @pl.when(pair == 0)
        def _():
            xhat, _ = normalize(tok[chip].astype(F32))
            normed = (xhat * g1 + s1).astype(BF)
            n1[...] = normed

            @pl.when(chip == 1)
            def _():
                place_rows(n1t, normed.T)

        w = jnp.concatenate([wq[3 * pair], wq[3 * pair + 1], wq[3 * pair + 2]], axis=1)
        qkv = mm(n1[...], w).astype(BF)
        q = qkv[:, :PAIR] * jnp.asarray(scale, BF)
        k = qkv[:, PAIR : 2 * PAIR]
        vt = qkv[:, 2 * PAIR :].T
        visible = place < lens[(1 - mp) * (1 - chip) + mp * chip]
        outs = []
        for h in range(2):
            mine = (lane >= h * HEAD_DIM) & (lane < (h + 1) * HEAD_DIM)
            s = jnp.where(visible, mm_t(jnp.where(mine, k, jnp.zeros_like(k)), q), -1e30)
            top = jnp.max(s, 0, keepdims=True)
            e = jnp.exp(s - top)
            total = jnp.sum(e, 0, keepdims=True)
            lse[i, h : h + 1, :] = top + jnp.log(total)
            o = mm(vt[h * HEAD_DIM : (h + 1) * HEAD_DIM], e.astype(BF))
            outs.append(o / total)
        lse[i, 2:8, :] = jnp.zeros((6, seq), F32)
        att[i] = jnp.concatenate(outs, 0).T.astype(BF)

        @pl.when(chip == 0)
        def _():
            for c in att_copy(i):
                c.start()

        for when, steps in (
            (1, [(0, 1)]),
            (2, [(2, 0), (6, 0), (1, 1), (5, 1), (0, 2), (3, 0), (7, 0), (4, 0), (8, 0), (9, 0)]),
            (3, [(5, 2)]),
            (4, [(1, 2), (0, 3)]),
            (5, [(2, 1)]),
        ):

            @pl.when(i == when)
            def _(when=when, steps=steps):
                if when == 2:
                    for c in wu_in[3:]:
                        c.wait()
                for step in steps:
                    pass_on(*step)

        return 0

    lax.fori_loop(0, 6, attend, 0)

    cot.wait()
    visible = place < own_len
    g = jnp.where(visible, gm[...].astype(F32), 0.0)
    g_low = g.astype(BF)
    gm[...] = g_low
    place_rows(gmt, g_low.T)
    vs[0, 0:1, :] = jnp.sum(g, 0, keepdims=True)
    wo_in.wait()
    have(0)
    for i in range(3):
        arrived(att.at[6 + i], att_r.at[0, i], to_y)
        arrived(lse.at[6 + i], att_r.at[1, i], to_y)
    blocks = jnp.concatenate([att[3 + p] for p in range(6)], axis=1)
    r = tok[1].astype(F32) + mm(blocks, wo[...].reshape(6 * PAIR, width)) + b_out
    resid[...] = r
    xhat, _ = normalize(r)
    normed = (xhat * g2 + s2).astype(BF)
    n2[...] = normed
    place_rows(n2t, normed.T)
    macc[...] = jnp.zeros_like(macc)
    gacc[...] = jnp.zeros_like(gacc)

    half = 384

    def halved(n, turn):
        first, second = turn * x + (1 - turn) * z0, turn * z0 + (1 - turn) * x
        return sum(b * (384 >> k) for k, b in enumerate((core, first, second, z1)[:n]))

    def given(n, turn):
        first, second = turn * x + (1 - turn) * z0, turn * z0 + (1 - turn) * x
        return halved(n, turn) + (1 - (core, first, second, z1)[n]) * (384 >> n)

    def partner(n, turn):
        if n == 0:
            return to_c
        if n == 3:
            return to_w
        by_x = turn if n == 1 else 1 - turn
        return (dp + by_x * (2 - 4 * x) + (1 - by_x) * (4 - 8 * z0), mp)

    m_buf = [rc, rx, rz, rw]

    def m_copy(n, t):
        rows = 384 >> n
        turn = t % 2
        src = grad.at[t, :, pl.ds(aligned(given(n, turn), 16), rows), :]
        return remote(src, m_buf[n].at[t], m_s.at[n, t], m_r.at[n, t], partner(n, turn))

    def m_step(n, t):
        rows = 384 >> n
        turn = t % 2
        at = pl.ds(aligned(halved(n + 1, turn), 16), rows)
        arrived(m_buf[n].at[t], m_r.at[n, t], to_c)
        merge = n == 2 and t < 4
        if merge:
            arrived(ry.at[t], m_r.at[4, t], to_y)
        for w in range(2):
            total = grad[t, w, at, :].astype(F32) + m_buf[n][t, w].astype(F32)
            if n == 3:
                (d_up, d_down)[w][:, t * 384 : (t + 1) * 384] = total
                continue
            if merge:
                total += ry[t, w].astype(F32)
            grad[t, w, at, :] = total.astype(BF)
        if n < 2 or merge:
            m_copy(n + 1, t).start()
        elif n == 2:
            m_y(t).start()

    def m_step0(t):
        arrived(rc.at[t], m_r.at[0, t], to_c)
        at = pl.ds(aligned(core * 384, 384), 384)
        for w in range(2):
            grad[t, w, at, :] = (grad[t, w, at, :].astype(F32) + rc[t, w].astype(F32)).astype(BF)
        m_copy(1, t).start()

    def m_y(t):
        src = grad.at[t, :, pl.ds(aligned(halved(3, t % 2), 16), 2 * ROWS), :]
        return remote(src, ry.at[t - 4], m_s.at[4, t], m_r.at[4, t - 4], to_y)

    def tile(t, _):
        for when, steps, ready in (
            (0, [(6, 1), (3, 1), (2, 2)], []),
            (1, [(1, 3), (5, 3), (7, 1), (6, 2), (8, 1), (4, 1), (3, 2)], []),
            (2, [(7, 2), (6, 3), (8, 2)], []),
            (3, [(2, 3), (4, 2)], []),
            (4, [(7, 3), (3, 3)], [1, 5]),
            (5, [(8, 3)], [2, 6]),
            (6, [(4, 3)], [3, 7]),
            (7, [(9, 3)], [4, 8]),
        ):

            @pl.when(t == when)
            def _(when=when, steps=steps, ready=ready):
                if when == 0:
                    wd_in.wait()
                for i in ready:
                    have(i)
                for step in steps:
                    pass_on(*step)

        late = t // 4
        unit = t % 4
        wut = jnp.concatenate([wu[3 * t], wu[3 * t + 1], wu[3 * t + 2]], axis=1)
        wdt = wd[t]
        u = mm(n2[...], wut) + bias_rows[pl.ds(t, 1), :]
        act, slope = gelu_pair(u)
        act = act.astype(BF)
        gp = (mm_t(gm[...], wdt) * slope).astype(BF)
        row = 8 + 4 * (mp + late - 2 * mp * late) + unit
        vs[0, pl.ds(row, 1), 0:384] = jnp.sum(gp.astype(F32), 0, keepdims=True)
        macc[...] += mm(act, wdt)
        gacc[...] += mm_t(gp, wut)
        turn = t % 2
        store_rows(grad, (t, 0), mm(n2t[...], gp).astype(BF), turn)
        store_rows(grad, (t, 1), mm(gmt[...], act).astype(BF), turn)
        m_copy(0, t).start()

        @pl.when(t >= 1)
        def _():
            m_step0(t - 1)

        return 0

    arrived(bu_oth, agl_r.at[10, 0], to_y)
    for j in range(4):
        bias_rows[j : j + 1, :] = bu[j * 384 : (j + 1) * 384].reshape(1, 384)
        bias_rows[4 + j : 5 + j, :] = bu_oth[j * 384 : (j + 1) * 384].reshape(1, 384)
    lax.fori_loop(0, 8, tile, 0)

    r = resid[...]
    ob[...] = jnp.where(visible, r + macc[...] + b_down, 0.0).astype(BF)
    out_own = local(ob, out_h.at[mp], o_sem.at[0])
    out_far = remote(ob, out_h.at[mp], e_s.at[0], e_r.at[0], to_y)
    out_own.start()
    out_far.start()
    xhat, inv = normalize(r)
    gs = gacc[...]
    gres = gm[...].astype(F32) + norm_back(gs, xhat, inv, g2)
    low = gres.astype(BF)
    n2[...] = low
    place_rows(n2t, low.T)
    vs[0, 1:2, :] = jnp.sum(gs * xhat, 0, keepdims=True)
    vs[0, 2:3, :] = jnp.sum(gs, 0, keepdims=True)
    vs[0, 3:4, :] = jnp.sum(gres, 0, keepdims=True)
    resid[...] = gres
    gacc[...] = jnp.zeros_like(gacc)
    have(9)
    for i in range(1, 5):
        for r in range(4):
            sent(passed(i, r), agl_s.at[i, r], to_c)

    a_buf = [ac, ax, az, aw]

    def a_turn(p):
        return 1 - p % 3 % 2

    def a_copy(n, p):
        rows = 384 >> n
        turn = a_turn(p)
        src = wu.at[pl.ds(4 * p, 4), pl.ds(aligned(given(n, turn), 16), rows), :]
        return remote(src, a_buf[n].at[p], a_s.at[n, p], a_r.at[n, p], partner(n, turn))

    def a_step(n, p):
        rows = 384 >> n
        arrived(a_buf[n].at[p], a_r.at[n, p], to_c)
        merge = n == 2 and p < 3
        if merge:
            arrived(ay.at[p], a_r.at[4, p], to_y)
        at = pl.ds(aligned(halved(n + 1, a_turn(p)), 16), rows)
        for w in range(4):
            total = wu[4 * p + w, at, :].astype(F32) + a_buf[n][p, w].astype(F32)
            if n == 3:
                cols = slice(p * PAIR, (p + 1) * PAIR)
                if w < 3:
                    d_qkv[w, :, cols] = total
                else:
                    d_out[:, cols] = total
                continue
            if merge:
                total += ay[p, w].astype(F32)
            wu[4 * p + w, at, :] = total.astype(BF)
        if n < 2 or merge:
            a_copy(n + 1, p).start()
        elif n == 2:
            a_y(p).start()

    def a_y(p):
        src = wu.at[pl.ds(4 * p, 4), pl.ds(aligned(halved(3, a_turn(p)), 16), 2 * ROWS), :]
        return remote(src, ay.at[p - 3], a_s.at[4, p], a_r.at[4, p - 3], to_y)

    zero = jnp.zeros((seq, PAIR), BF)

    def back(k, _):
        p = (k + 3) % 6
        w = jnp.concatenate([wq[3 * p], wq[3 * p + 1], wq[3 * p + 2]], axis=1)
        qkv = mm(n1[...], w).astype(BF)
        q, key, v = qkv[:, :PAIR], qkv[:, PAIR : 2 * PAIR], qkv[:, 2 * PAIR :]
        q_s = q * jnp.asarray(scale, BF)
        ga = mm_t(n2[...], wo[p]).astype(BF)
        kt = key.T
        dqt = []
        dk = jnp.zeros((seq, PAIR), F32)
        dv = jnp.zeros((seq, PAIR), F32)
        for h in range(2):
            mine = (lane >= h * HEAD_DIM) & (lane < (h + 1) * HEAD_DIM)
            s = jnp.where(visible, mm_t(jnp.where(mine, key, zero), q_s), -1e30)
            prob = jnp.exp(s - lse[3 + p, h : h + 1, :])
            d_prob = mm_t(jnp.where(mine, v, zero), ga)
            row = jnp.sum(prob * d_prob, 0, keepdims=True)
            ds = (prob * (d_prob - row) * scale).astype(BF)
            dk += mm(ds, jnp.where(mine, q, zero))
            dv += mm(prob.astype(BF), jnp.where(mine, ga, zero))
            dqt.append(mm(kt[h * HEAD_DIM : (h + 1) * HEAD_DIM], ds))
        dq = jnp.concatenate(dqt, 0).T
        d = jnp.concatenate([dq.astype(BF), dk.astype(BF), dv.astype(BF)], axis=1)
        gacc[...] += mm_t(d, w)
        dw = mm(n1t[...], d).astype(BF)
        turn = a_turn(p)
        for c in range(3):
            store_rows(wu, (4 * p + c,), dw[:, c * PAIR : (c + 1) * PAIR], turn)
        store_rows(wu, (4 * p + 3,), mm(n2t[...], att[3 + p]).astype(BF), turn)
        a_copy(0, p).start()
        for when, steps in (
            (0, [(m_step, 1, 4), (m_step, 0, 7), (m_step, 1, 1)]),
            (1, [(m_step, 1, 5), (m_step, 1, 6), (m_step, 1, 2), (m_step, 2, 4)]),
            (2, [(m_step, 1, 3)]),
            (3, [(m_step, 1, 0), (m_step, 2, 5), (m_step, 1, 7), (a_step, 0, 4), (a_step, 0, 3), (m_step, 2, 6)]),
            (4, [(m_step, 2, 7)]),
            (5, [(a_step, 0, 0), (a_step, 0, 1)]),
        ):

            @pl.when(k == when)
            def _(steps=steps):
                for step in steps:
                    step[0](*step[1:])

        return 0

    lax.fori_loop(0, 6, back, 0)

    chunk = seq // 4

    def gt_copy(j):
        rows = pl.ds(j * chunk, chunk)
        return remote(gl.at[rows, :], gt_far.at[rows, :], e_s.at[1 + j], e_r.at[1 + j], to_y)

    gain_sum = jnp.zeros((1, width), F32)
    shift_sum = jnp.zeros((1, width), F32)
    for j in range(4):
        rows = slice(j * chunk, (j + 1) * chunk)
        xhat, inv = normalize(tok[1, rows].astype(F32))
        gf = gacc[rows]
        gt = resid[rows] + norm_back(gf, xhat, inv, g1)
        resid[rows] = gt
        gl[rows] = gt.astype(BF)
        gt_copy(j).start()
        gain_sum += jnp.sum(gf * xhat, 0, keepdims=True)
        shift_sum += jnp.sum(gf, 0, keepdims=True)
        if j == 0:
            a_step(0, 2)
    gt_own = local(resid, gt_h, o_sem.at[1])
    gt_own.start()
    vs[0, 4:5, :] = gain_sum
    vs[0, 5:6, :] = shift_sum
    v_dev = [to_c, to_z, to_w, to_x, to_y]

    def v_copy(n):
        return remote(vs.at[n], vr.at[n], e_s.at[5 + n], e_r.at[5 + n], v_dev[n])

    def v_step(n):
        arrived(vr.at[n], e_r.at[5 + n], v_dev[n])
        if n < 4:
            vs[n + 1] = vs[n] + vr[n]
            v_copy(n + 1).start()
        else:
            vec_out[...] = vs[4] + vr[4]

    v_copy(0).start()
    for step in (
        (m_step, 2, 3), (a_step, 0, 5), (m_step, 2, 2), (m_step, 2, 1), (a_step, 1, 3), (a_step, 1, 4), (v_step, 0),
        (a_step, 1, 0), (m_step, 2, 0), (a_step, 2, 3), (a_step, 1, 5), (a_step, 1, 1), (a_step, 2, 4), (v_step, 1),
        (a_step, 1, 2), (a_step, 2, 0), (a_step, 2, 5), (a_step, 2, 1), (v_step, 2), (a_step, 2, 2), (m_step, 3, 2),
        (m_step, 3, 3), (v_step, 3), (m_step, 3, 1), (a_step, 3, 1), (a_step, 3, 0), (m_step, 3, 0), (a_step, 3, 2),
    ):
        step[0](*step[1:])

    v_step(4)

    bu_copy.wait_send()
    for i in (0, 5, 6, 7, 8, 9):
        for r in (0, 3) if i == 9 else range(4):
            sent(passed(i, r), agl_s.at[i, r], to_c)
    for i in range(3):
        for c in att_copy(i):
            c.wait_send()

    def drain_m(t, _):
        for n in range(3):
            m_copy(n, t).wait_send()

        @pl.when(t < 4)
        def _():
            m_copy(3, t).wait_send()

        @pl.when(t >= 4)
        def _():
            m_y(t).wait_send()

        return 0

    lax.fori_loop(0, 8, drain_m, 0)

    def drain_a(p, _):
        for n in range(3):
            a_copy(n, p).wait_send()

        @pl.when(p < 3)
        def _():
            a_copy(3, p).wait_send()

        @pl.when(p >= 3)
        def _():
            a_y(p).wait_send()

        return 0

    lax.fori_loop(0, 6, drain_a, 0)
    for j in range(4):
        gt_copy(j).wait_send()
        arrived(gt_far.at[pl.ds(j * chunk, chunk), :], e_r.at[1 + j], to_y)
    for n in range(5):
        v_copy(n).wait_send()
    out_own.wait()
    out_far.wait_send()
    arrived(out_h.at[1 - mp], e_r.at[0], to_y)
    gt_own.wait()


def finish_kernel(
    out_h, gt_h, gt_far, d_qkv, d_out, d_up, d_down, vec,
    out_f, gt_f, g1_f, s1_f, qkv_f, wo_f, bo_f, g2_f, s2_f, up_f, bu_f, down_f, bd_f,
    ob, gb, far, in_sem, out_sem,
):
    dp, mp = lax.axis_index("dp"), lax.axis_index("mp")
    seq, width = far.shape
    chunk = seq // 4
    parts = [pl.ds(j * chunk, chunk) for j in range(4)]
    fars = [pltpu.make_async_copy(gt_far.at[r], far.at[r], in_sem.at[j]) for j, r in enumerate(parts)]
    owns = [pltpu.make_async_copy(gt_h.at[r], gb.at[mp, r], in_sem.at[4 + j]) for j, r in enumerate(parts)]
    outs = [pltpu.make_async_copy(out_h.at[c], ob.at[c], in_sem.at[8 + c]) for c in range(2)]
    for c in fars + owns + outs:
        c.start()
    leave = []

    def go(src, dst):
        leave.append(pltpu.make_async_copy(src, dst, out_sem.at[len(leave)]))
        leave[-1].start()

    for j, r in enumerate(parts):
        fars[j].wait()
        gb[1 - mp, r] = far[r].astype(F32)
        go(gb.at[1 - mp, r], gt_f.at[1 - mp, r])
        owns[j].wait()
        go(gb.at[mp, r], gt_f.at[mp, r])
    for c in range(2):
        outs[c].wait()
        go(ob.at[c], out_f.at[c])
    qkv_f[...] = d_qkv[...]
    up_f[...] = d_up[...]
    wo_f[...] = d_out[...]
    down_f[...] = d_down[...]
    turned = pltpu.roll(vec[0:8, :], (width - dp * ROWS) % width, 1)
    for row, ref in enumerate((bd_f, g2_f, s2_f, bo_f, g1_f, s1_f)):
        ref[...] = turned[row : row + 1, :ROWS].reshape(ROWS)
    tile = d_up.shape[1] // 4
    bias = vec[pl.ds(8 + 4 * mp + dp // 4, 1), 0:tile]
    bias = pltpu.roll(jnp.broadcast_to(bias, (8, tile)), (tile - dp % 4 * 2 * ROWS) % tile, 1)
    bu_f[...] = bias[0:1, : 2 * ROWS]
    for c in leave:
        c.wait()


def kernel_program(
    mp_n, tokens, lengths, ln1_gain, ln1_shift, w_qkv, w_out, b_out, ln2_gain, ln2_shift, w_up, b_up, w_down, b_down, cotangent
):
    seq, width = tokens.shape[1:]
    feat, hidden = w_qkv.shape[2], w_up.shape[1]
    tile = hidden // 4
    args = [
        lengths, tokens, cotangent, ln1_gain, ln1_shift, ln2_gain, ln2_shift, b_out, b_down,
        b_up, w_qkv, w_out.reshape(3, PAIR, width), w_up, w_down.reshape(4, tile, width),
    ]
    hbm, vmem = pl.BlockSpec(memory_space=pl.ANY), pl.BlockSpec(memory_space=pltpu.VMEM)
    outs = [
        sds(tokens.shape, BF),
        sds((seq, width), F32),
        sds((seq, width), BF),
        sds((3, ROWS, feat), F32),
        sds((ROWS, feat), F32),
        sds((ROWS, hidden), F32),
        sds((ROWS, hidden), F32),
        sds((16, width), F32),
    ]
    v = pltpu.VMEM
    act = v((seq, width), BF)
    act_t = v((width, seq), BF)
    wide = v((seq, width), F32)
    scratch = [
        v((2, seq, width), BF), act, act_t, act, act_t, act, act_t, wide, wide, wide,
        v((9, seq, PAIR), BF), v((9, 8, seq), F32),
        v((18, width, PAIR), BF), v((6, PAIR, width), BF), v((24, width, PAIR), BF), v((8, tile, width), BF), v((hidden,), F32), v((8, tile), F32),
        v((8, 2, width, tile), BF),
        v((8, 2, 384, tile), BF), v((8, 2, 192, tile), BF), v((8, 2, 96, tile), BF), v((4, 2, 48, tile), BF), v((4, 2, 96, tile), BF),
        v((6, 4, 384, PAIR), BF), v((6, 4, 192, PAIR), BF), v((6, 4, 96, PAIR), BF), v((3, 4, 48, PAIR), BF), v((3, 4, 96, PAIR), BF),
        act, act, v((5, 16, width), F32), v((5, 16, width), F32),
    ]
    dma = pltpu.SemaphoreType.DMA
    scratch += [
        dma((20,)), dma((11, 4)), dma((11, 4)), dma((2, 3)), dma((2, 3)), dma((5, 8)), dma((5, 8)), dma((5, 6)), dma((5, 6)),
        dma((10,)), dma((10,)), dma((2,)),
    ]
    results = pl.pallas_call(
        layer_kernel,
        name="layer",
        out_shape=outs,
        in_specs=[pl.BlockSpec(memory_space=pltpu.SMEM), hbm, hbm] + [vmem] * 7 + [hbm] * 4,
        out_specs=[hbm] * 3 + [vmem] * 5,
        scratch_shapes=scratch,
        compiler_params=pltpu.CompilerParams(collective_id=0, has_side_effects=True, vmem_limit_bytes=VMEM_ALL),
    )(*args)
    shard = sds((ROWS,), F32)
    finals = [
        sds(tokens.shape, BF), sds(tokens.shape, F32), shard, shard, sds((3, ROWS, feat), F32), sds((ROWS, feat), F32), shard, shard,
        shard, sds((ROWS, hidden), F32), sds((1, 2 * ROWS), F32), sds((ROWS, hidden), F32), shard,
    ]
    finished = list(
        pl.pallas_call(
            finish_kernel,
            name="finish",
            out_shape=finals,
            in_specs=[hbm] * 3 + [vmem] * 5,
            out_specs=[hbm] * 2 + [vmem] * 11,
            scratch_shapes=[v(tokens.shape, BF), v(tokens.shape, F32), v((seq, width), BF), dma((12,)), dma((12,))],
            compiler_params=pltpu.CompilerParams(vmem_limit_bytes=VMEM_ALL),
        )(*results)
    )
    for i in (5, 11):
        finished[i] = finished[i].T
    return tuple(finished)


def solution(mesh):
    dp_n, mp_n = mesh.shape["dp"], mesh.shape["mp"]
    body = functools.partial(kernel_program, mp_n) if dp_n == 16 else functools.partial(permute_program, dp_n, mp_n)
    return jax.shard_map(
        body,
        mesh=mesh,
        in_specs=(
            P("dp", None, None),
            P("dp"),
            P(),
            P(),
            P(None, None, "mp"),
            P("mp", None),
            P(),
            P(),
            P(),
            P(None, "mp"),
            P("mp"),
            P("mp", None),
            P(),
            P("dp", None, None),
        ),
        out_specs=(
            P("dp", None, None),
            P("dp", None, None),
            P("dp"),
            P("dp"),
            P(None, "dp", "mp"),
            P("mp", "dp"),
            P("dp"),
            P("dp"),
            P("dp"),
            P("dp", "mp"),
            P("mp", "dp"),
            P("mp", "dp"),
            P("dp"),
        ),
        check_vma=False,
    )
```

```python
import functools

import jax
import jax.numpy as jnp
from jax import lax
from jax.experimental import pallas as pl
from jax.experimental.pallas import tpu as pltpu
from jax.sharding import PartitionSpec as P

HEAD_DIM = 64
PAIR = 2 * HEAD_DIM
BF = jnp.bfloat16
F32 = jnp.float32
EPS = 1e-05
LIMIT = 40 * 1024 * 1024

TAIL_P = 0.3
TAIL_C = (
    0.11962929256864907,
    0.12075406313917503,
    0.09991275007605285,
    0.12856432480895655,
    -0.05368921426491713,
    0.2063600527786208,
    -0.1572071533588575,
    0.03567581131365836,
)


def mm(a, b):
    return lax.dot_general(a, b, (((1,), (0,)), ((), ())), preferred_element_type=F32)


def mm_t(a, b):
    return lax.dot_general(a, b, (((1,), (1,)), ((), ())), preferred_element_type=F32)


def normalize(x):
    mean = jnp.mean(x, -1, keepdims=True)
    center = x - mean
    var = jnp.mean(center * center, -1, keepdims=True)
    inv = lax.rsqrt(var + EPS)
    return center * inv, inv


def norm_back(grad, xhat, inv, gain):
    d = grad * gain
    m1 = jnp.mean(d, -1, keepdims=True)
    m2 = jnp.mean(d * xhat, -1, keepdims=True)
    return inv * (d - m1 - xhat * m2)


def bit_reverse(index, bits):
    out = 0
    for b in range(bits):
        out = (out << 1) | ((index >> b) & 1)
    return out


def put_rows(ref, value, blocks):
    rows = value.shape[0] // blocks
    bits = blocks.bit_length() - 1
    if rows % 16:
        ref[...] = value
        return
    for b in range(blocks):
        d = bit_reverse(b, bits)
        ref[d * rows : (d + 1) * rows, :] = value[b * rows : (b + 1) * rows, :]


def order_rows(value, blocks):
    rows = value.shape[0] // blocks
    if rows % 16 == 0:
        return value
    bits = blocks.bit_length() - 1
    split = value.reshape((2,) * bits + (rows, value.shape[1]))
    split = split.transpose(tuple(reversed(range(bits))) + (bits, bits + 1))
    return split.reshape(value.shape)


def call(body, name, out_shape, args, flops, grid=None, in_specs=None, out_specs=None, scalars=None, scratch=(), aliases=None):
    nbytes = sum(a.size * a.dtype.itemsize for a in args)
    nbytes += sum(o.size * o.dtype.itemsize for o in out_shape)
    if in_specs is None:
        in_specs = [whole(a.shape) for a in args]
    if out_specs is None:
        out_specs = [whole(o.shape) for o in out_shape]
    return pl.pallas_call(
        body,
        name=name,
        out_shape=out_shape,
        grid_spec=pltpu.PrefetchScalarGridSpec(
            num_scalar_prefetch=1,
            grid=grid or (1,),
            in_specs=in_specs,
            out_specs=out_specs,
            scratch_shapes=list(scratch),
        ),
        input_output_aliases=aliases or {},
        compiler_params=pltpu.CompilerParams(vmem_limit_bytes=LIMIT),
        cost_estimate=pl.CostEstimate(flops=flops, bytes_accessed=nbytes, transcendentals=0),
    )(scalars, *args)


def whole(shape):
    return pl.BlockSpec(shape, lambda *_: (0,) * len(shape))


def sds(shape, dtype):
    return jax.ShapeDtypeStruct(shape, dtype)


def chip_spec(shape):
    return pl.BlockSpec((None,) + tuple(shape[1:]), lambda i, sc: (sc[0], 0, 0))


def attention_kernel(sc, tok, gain, shift, w_ref, att_ref, lse_ref, normed):
    @pl.when(pl.program_id(0) == 0)
    def _():
        xhat, _ = normalize(tok[...].astype(F32))
        normed[...] = (xhat * gain[...] + shift[...]).astype(BF)

    seq = normed.shape[0]
    w = jnp.concatenate([w_ref[0], w_ref[1], w_ref[2]], axis=1)
    qkv = mm(normed[...], w).astype(BF)
    scale = HEAD_DIM**-0.5
    q = qkv[:, :PAIR] * jnp.asarray(scale, BF)
    k = qkv[:, PAIR : 2 * PAIR]
    vt = qkv[:, 2 * PAIR :].T
    lane = lax.broadcasted_iota(jnp.int32, (seq, PAIR), 1)
    visible = lax.broadcasted_iota(jnp.int32, (seq, 1), 0) < sc[1]
    outs = []
    for h in range(2):
        mine = (lane >= h * HEAD_DIM) & (lane < (h + 1) * HEAD_DIM)
        kh = jnp.where(mine, k, jnp.zeros_like(k))
        s = jnp.where(visible, mm_t(kh, q), -1e30)
        top = jnp.max(s, 0, keepdims=True)
        e = jnp.exp(s - top)
        total = jnp.sum(e, 0, keepdims=True)
        lse_ref[h : h + 1, :] = top + jnp.log(total)
        o = mm(vt[h * HEAD_DIM : (h + 1) * HEAD_DIM], e.astype(BF))
        outs.append(o / total)
    att_ref[...] = jnp.concatenate(outs, 0).T.astype(BF)
    lse_ref[2:8, :] = jnp.zeros((6, seq), F32)


def prepare_kernel(blocks, sc, tok, cot, gain, shift, n1, n1t, gm, gmt, vec):
    xhat, _ = normalize(tok[...].astype(F32))
    normed = (xhat * gain[...] + shift[...]).astype(BF)
    n1[...] = normed
    put_rows(n1t, normed.T, blocks)
    seq = normed.shape[0]
    visible = lax.broadcasted_iota(jnp.int32, (seq, 1), 0) < sc[1]
    g = jnp.where(visible, cot[...].astype(F32), 0.0)
    gl = g.astype(BF)
    gm[...] = gl
    put_rows(gmt, gl.T, blocks)
    vec[...] = jnp.broadcast_to(jnp.sum(g, 0, keepdims=True), vec.shape)


def project_kernel(blocks, sc, tok, att_a, att_b, wo_a, wo_b, b_out, gain, shift, resid, n2, n2t):
    x = tok[...].astype(F32)
    r = x + mm(att_a[...], wo_a[...]) + mm(att_b[...], wo_b[...]) + b_out[...]
    resid[...] = r
    xhat, _ = normalize(r)
    normed = (xhat * gain[...] + shift[...]).astype(BF)
    n2[...] = normed
    put_rows(n2t, normed.T, blocks)


def gelu_pair(u):
    z = jnp.abs(u)
    t = 1.0 / (1.0 + TAIL_P * z)
    poly = TAIL_C[-1]
    for c in TAIL_C[-2::-1]:
        poly = poly * t + c
    e = jnp.exp(-0.5 * u * u)
    tail = e * (poly * t)
    cdf = jnp.where(u < 0, tail, 1.0 - tail)
    return u * cdf, cdf + u * e * 0.3989422804014327


def mlp_kernel(tiles, first, cross, sc, *refs):
    n2, n2t, gm, gmt = refs[:4]
    wu = refs[4 : 4 + tiles]
    wd = refs[4 + tiles : 4 + 2 * tiles]
    bu = refs[4 + 2 * tiles]
    at = 5 + 2 * tiles
    if not first:
        macc_in, gacc_in, db_in = refs[at : at + 3]
        at += 3
    keep, send, macc, gacc, db = refs[at:]
    width = wu[0].shape[1]
    half = keep.shape[1]
    core = sc[0]
    db[...] = jnp.zeros_like(db) if first else db_in[...]
    for t in range(tiles):
        wut, wdt = wu[t][...], wd[t][...]
        u = mm(n2[...], wut) + bu[pl.ds(sc[1 + 2 * t], 1), :]
        act, slope = gelu_pair(u)
        act = act.astype(BF)
        gp = (mm_t(gm[...], wdt) * slope).astype(BF)
        db[pl.ds(sc[2 + 2 * t], 1), :] = jnp.sum(gp.astype(F32), 0, keepdims=True)
        m, g = mm(act, wdt), mm_t(gp, wut)
        if t == 0 and first:
            macc[...], gacc[...] = m, g
        elif t == 0:
            macc[...], gacc[...] = macc_in[...] + m, gacc_in[...] + g
        else:
            macc[...] += m
            gacc[...] += g
        for which, (lhs, rhs) in enumerate(((n2t, gp), (gmt, act))):
            grad = mm(lhs[...], rhs).astype(BF)
            top, low = grad[:half], grad[half:]
            other = (t ^ 1) if cross else t
            keep[which, :, t * width : (t + 1) * width] = jnp.where(core == 0, top, low)
            send[which, :, other * width : (other + 1) * width] = jnp.where(core == 0, low, top)


def middle_kernel(blocks, sc, resid, macc, gacc, gm, b_down, gain, out, gres, rl, rlt, vec):
    r = resid[...]
    seq = r.shape[0]
    visible = lax.broadcasted_iota(jnp.int32, (seq, 1), 0) < sc[1]
    out[...] = jnp.where(visible, r + macc[...] + b_down[...], 0.0).astype(BF)
    xhat, inv = normalize(r)
    gs = gacc[...]
    gr = gm[...].astype(F32) + norm_back(gs, xhat, inv, gain[...])
    gres[...] = gr
    low = gr.astype(BF)
    rl[...] = low
    put_rows(rlt, low.T, blocks)
    vec[0:1, :] = jnp.sum(gs * xhat, 0, keepdims=True)
    vec[1:2, :] = jnp.sum(gs, 0, keepdims=True)
    vec[2:3, :] = jnp.sum(gr, 0, keepdims=True)
    vec[3:8, :] = jnp.zeros((5, vec.shape[1]), F32)


def attention_back_kernel(first, sc, *refs):
    n1, n1t, rl, rlt, att, lse, w_ref, wo = refs[:8]
    at = 8
    if not first:
        gf_in = refs[at]
        at += 1
    keep, send, gf = refs[at:]
    seq = n1.shape[0]
    half = keep.shape[1]
    scale = HEAD_DIM**-0.5
    w = jnp.concatenate([w_ref[0], w_ref[1], w_ref[2]], axis=1)
    qkv = mm(n1[...], w).astype(BF)
    q, k, v = qkv[:, :PAIR], qkv[:, PAIR : 2 * PAIR], qkv[:, 2 * PAIR :]
    qs = q * jnp.asarray(scale, BF)
    ga = mm_t(rl[...], wo[...]).astype(BF)
    kt = k.T
    lane = lax.broadcasted_iota(jnp.int32, (seq, PAIR), 1)
    visible = lax.broadcasted_iota(jnp.int32, (seq, 1), 0) < sc[1]
    zero = jnp.zeros_like(q)
    dqt = []
    dk = jnp.zeros((seq, PAIR), F32)
    dv = jnp.zeros((seq, PAIR), F32)
    for h in range(2):
        mine = (lane >= h * HEAD_DIM) & (lane < (h + 1) * HEAD_DIM)
        s = jnp.where(visible, mm_t(jnp.where(mine, k, zero), qs), -1e30)
        p = jnp.exp(s - lse[h : h + 1, :])
        dp = mm_t(jnp.where(mine, v, zero), ga)
        row = jnp.sum(p * dp, 0, keepdims=True)
        ds = (p * (dp - row) * scale).astype(BF)
        dk += mm(ds, jnp.where(mine, q, zero))
        dv += mm(p.astype(BF), jnp.where(mine, ga, zero))
        dqt.append(mm(kt[h * HEAD_DIM : (h + 1) * HEAD_DIM], ds))
    dq = jnp.concatenate(dqt, 0).T
    d = jnp.concatenate([dq.astype(BF), dk.astype(BF), dv.astype(BF)], axis=1)
    g = mm_t(d, w)
    begin = pl.program_id(0) == 0

    @pl.when(begin)
    def _():
        gf[...] = g if first else gf_in[...] + g

    @pl.when(jnp.logical_not(begin))
    def _():
        gf[...] += g

    core = sc[0]
    dw = mm(n1t[...], d).astype(BF)
    dwo = mm(rlt[...], att[...]).astype(BF)
    parts = [dw[:, c * PAIR : (c + 1) * PAIR] for c in range(3)] + [dwo]
    for c, part in enumerate(parts):
        top, low = part[:half], part[half:]
        keep[c] = jnp.where(core == 0, top, low)
        send[c] = jnp.where(core == 0, low, top)


def last_kernel(sc, tok, gres, gf, gain, gt, gtl, vec):
    xhat, inv = normalize(tok[...].astype(F32))
    g = gf[...]
    out = gres[...] + norm_back(g, xhat, inv, gain[...])
    gt[...] = out
    gtl[...] = out.astype(BF)
    vec[0:1, :] = jnp.sum(g * xhat, 0, keepdims=True)
    vec[1:2, :] = jnp.sum(g, 0, keepdims=True)
    vec[2:8, :] = jnp.zeros((6, vec.shape[1]), F32)


def permute_program(
    dp_n,
    mp_n,
    tokens,
    lengths,
    ln1_gain,
    ln1_shift,
    w_qkv,
    w_out,
    b_out,
    ln2_gain,
    ln2_shift,
    w_up,
    b_up,
    w_down,
    b_down,
    cotangent,
):
    chips, seq, width = tokens.shape
    feat = w_qkv.shape[2]
    hidden = w_up.shape[1]
    tile = hidden // 4
    pairs = feat // PAIR
    bits = dp_n.bit_length() - 1
    half = width // 2
    mp = lax.axis_index("mp")
    dp = lax.axis_index("dp")
    core = dp & 1
    two = dp & 3
    quarter = ((two & 1) << 1) | (two >> 1)
    i32 = jnp.int32

    def swap_y(x):
        return lax.ppermute(x, "mp", [(i, i ^ 1) for i in range(mp_n)])

    def swap_d(x, bit):
        return lax.ppermute(x, "dp", [(i, i ^ (1 << bit)) for i in range(dp_n)])

    own_sc = jnp.stack([mp, lengths[mp]]).astype(i32)
    peer_sc = jnp.stack([1 - mp, lengths[1 - mp]]).astype(i32)
    row = lambda v: v.reshape(1, -1)
    g1, s1, g2, s2, bo, bd = map(row, (ln1_gain, ln1_shift, ln2_gain, ln2_shift, b_out, b_down))

    hw = feat // 2
    wo_r0 = swap_y(lax.dynamic_slice_in_dim(w_out, core * hw, hw, 0))
    wo_r1 = swap_d(wo_r0, 0)
    wo_oth = jnp.where(core == 0, jnp.concatenate([wo_r0, wo_r1], 0), jnp.concatenate([wo_r1, wo_r0], 0))
    bu_own = b_up.reshape(4, tile)
    bu_oth = swap_y(bu_own)

    def attention(sc):
        return call(
            attention_kernel,
            "attention_fwd",
            [sds((seq, feat), BF), sds((pairs, 8, seq), F32)],
            [tokens, g1, s1, w_qkv],
            2 * seq * width * 3 * feat + 4 * seq * seq * feat,
            grid=(pairs,),
            in_specs=[
                chip_spec(tokens.shape),
                whole(g1.shape),
                whole(s1.shape),
                pl.BlockSpec((3, width, PAIR), lambda i, sc: (0, 0, i)),
            ],
            out_specs=[
                pl.BlockSpec((seq, PAIR), lambda i, sc: (0, i)),
                pl.BlockSpec((None, 8, seq), lambda i, sc: (i, 0, 0)),
            ],
            scalars=sc,
            scratch=[pltpu.VMEM((seq, width), BF)],
        )

    att_peer, lse_peer = attention(peer_sc)
    att_oth, lse_oth = swap_y(att_peer), swap_y(lse_peer)

    wu_r, wd_r = [None] * 4, [None] * 4
    for name, store, axis, src in (("u", wu_r, 1, w_up), ("d", wd_r, 0, w_down)):
        store[0] = swap_y(lax.dynamic_slice_in_dim(src, quarter * tile, tile, axis))
        store[1] = swap_d(store[0], 0)
        store[2] = swap_d(store[0], 1)
        store[3] = swap_d(store[2], 0)

    att_own, lse_own = attention(own_sc)

    n1, n1t, gm, gmt, vec_g = call(
        functools.partial(prepare_kernel, dp_n),
        "prepare",
        [sds((seq, width), BF), sds((width, seq), BF), sds((seq, width), BF), sds((width, seq), BF), sds((8, width), F32)],
        [tokens, cotangent, g1, s1],
        20 * seq * width,
        in_specs=[chip_spec(tokens.shape), chip_spec(cotangent.shape), whole(g1.shape), whole(s1.shape)],
        scalars=own_sc,
    )
    resid, n2, n2t = call(
        functools.partial(project_kernel, dp_n),
        "project",
        [sds((seq, width), F32), sds((seq, width), BF), sds((width, seq), BF)],
        [tokens, att_own, att_oth, w_out, wo_oth, bo, g2, s2],
        4 * seq * width * feat,
        in_specs=[chip_spec(tokens.shape)] + [whole(a.shape) for a in (att_own, att_oth, w_out, wo_oth, bo, g2, s2)],
        scalars=own_sc,
    )
    n1t, gmt, n2t = (order_rows(t, dp_n) for t in (n1t, gmt, n2t))

    own_half, oth_half = mp * 4, (1 - mp) * 4

    def mlp(first, cross, wus, wds, bias, slots, base, accs, specs):
        sc = [core]
        for a in slots:
            sc += [a, base + a]
        outs = [
            sds((2, half, 2 * tile), BF),
            sds((2, half, 2 * tile), BF),
            sds((seq, width), F32),
            sds((seq, width), F32),
            sds((8, tile), F32),
        ]
        args = [n2, n2t, gm, gmt, *wus, *wds, bias, *accs]
        in_specs = [whole(a.shape) for a in args]
        if specs:
            in_specs[4:8] = specs
        return call(
            functools.partial(mlp_kernel, 2, first, cross),
            "mlp_tiles",
            outs,
            args,
            12 * seq * width * 2 * tile,
            in_specs=in_specs,
            scalars=jnp.stack(sc).astype(i32),
            aliases={} if first else {10: 2, 11: 3, 12: 4},
        )

    def own_specs(a):
        return [pl.BlockSpec((width, tile), lambda i, sc, t=t: (0, t)) for t in (a, a + 1)] + [
            pl.BlockSpec((tile, width), lambda i, sc, t=t: (t, 0)) for t in (a, a + 1)
        ]

    pieces = []
    accs = []
    const = lambda v: jnp.asarray(v, i32)
    for a in (0, 2):
        k, s, *accs = mlp(
            a == 0, False, [w_up] * 2, [w_down] * 2, bu_own, [const(a), const(a + 1)], own_half, accs, own_specs(a)
        )
        pieces.append((k, s))
    mine = [quarter, quarter ^ 2, quarter ^ 1, quarter ^ 3]
    for a in (0, 2):
        k, s, *accs = mlp(
            False, True, wu_r[a : a + 2], wd_r[a : a + 2], bu_oth, mine[a : a + 2], oth_half, accs, None
        )
        pieces.append((k, s))
    macc, gacc, db = accs

    out_own, gres, rl, rlt, vec_mid = call(
        functools.partial(middle_kernel, dp_n),
        "middle",
        [sds((seq, width), BF), sds((seq, width), F32), sds((seq, width), BF), sds((width, seq), BF), sds((8, width), F32)],
        [resid, macc, gacc, gm, bd, g2],
        40 * seq * width,
        scalars=own_sc,
    )
    out_oth = swap_y(out_own)
    rlt = order_rows(rlt, dp_n)

    hq = width // 4
    wq_r = [None] * 4
    wq_r[0] = swap_y(lax.dynamic_slice_in_dim(w_qkv, quarter * hq, hq, 1))
    wq_r[1] = swap_d(wq_r[0], 0)
    wq_r[2] = swap_d(wq_r[0], 1)
    wq_r[3] = swap_d(wq_r[2], 0)
    wq_oth = jnp.concatenate(wq_r, 1)
    for r in range(4):
        wq_oth = lax.dynamic_update_slice_in_dim(wq_oth, wq_r[r], mine[r] * hq, 1)

    def attention_back(first, wq, wo, att, lse, accs):
        args = [n1, n1t, rl, rlt, att, lse, wq, wo, *accs]
        in_specs = [whole(a.shape) for a in args]
        in_specs[4] = pl.BlockSpec((seq, PAIR), lambda i, sc: (0, i))
        in_specs[5] = pl.BlockSpec((None, 8, seq), lambda i, sc: (i, 0, 0))
        in_specs[6] = pl.BlockSpec((3, width, PAIR), lambda i, sc: (0, 0, i))
        in_specs[7] = pl.BlockSpec((PAIR, width), lambda i, sc: (i, 0))
        piece = pl.BlockSpec((4, half, PAIR), lambda i, sc: (0, 0, i))
        return call(
            functools.partial(attention_back_kernel, first),
            "attention_bwd",
            [sds((4, half, feat), BF), sds((4, half, feat), BF), sds((seq, width), F32)],
            args,
            2 * seq * width * feat * 11 + 10 * seq * seq * feat,
            grid=(pairs,),
            in_specs=in_specs,
            out_specs=[piece, piece, whole((seq, width))],
            scalars=jnp.stack([core, own_sc[1]]).astype(i32),
            aliases={} if first else {9: 2},
        )

    k, s, gf = attention_back(True, w_qkv, w_out, att_own, lse_own, [])
    pieces.append((k, s))
    k, s, gf = attention_back(False, wq_oth, wo_oth, att_oth, lse_oth, [gf])
    pieces.append((k, s))

    gt_own, gt_low, vec_last = call(
        last_kernel,
        "last",
        [sds((seq, width), F32), sds((seq, width), BF), sds((8, width), F32)],
        [tokens, gres, gf, g1],
        30 * seq * width,
        in_specs=[chip_spec(tokens.shape)] + [whole(a.shape) for a in (gres, gf, g1)],
        scalars=own_sc,
    )
    gt_oth = swap_y(gt_low).astype(F32)

    def add(a, b):
        return (a.astype(F32) + b.astype(F32)).astype(BF)

    def split(x, bit):
        n = x.shape[1] // 2
        b = (dp >> bit) & 1
        return (
            lax.dynamic_slice_in_dim(x, b * n, n, 1),
            lax.dynamic_slice_in_dim(x, (1 - b) * n, n, 1),
        )

    state = [add(k, swap_d(s, 0)) for k, s in pieces]
    for bit in range(1, bits):
        parts = [split(x, bit) for x in state]
        got = [swap_d(s, bit) for _, s in parts]
        if bit == 1:
            got[2], got[3] = got[3], got[2]
        state = [add(p[0], g) for p, g in zip(parts, got)]
    own1, own2, oth1, oth2, at_own, at_oth = state
    rows = own1.shape[1]
    got1, got2, got_at = swap_y(oth1), swap_y(oth2), swap_y(at_oth)

    slots = jnp.stack([got1[..., :tile], got1[..., tile:], got2[..., :tile], got2[..., tile:]])
    got = [lax.dynamic_index_in_dim(slots, slot_of(a, two), 0, keepdims=False) for a in range(4)]
    mine_mlp = [own1[..., :tile], own1[..., tile:], own2[..., :tile], own2[..., tile:]]
    total = jnp.concatenate([m.astype(F32) + g.astype(F32) for m, g in zip(mine_mlp, got)], -1)
    total_at = at_own.astype(F32) + got_at.astype(F32)

    vecs = jnp.concatenate([vec_g[:1], vec_mid[:3], vec_last[:2], db.reshape(-1, width)], 0)
    for bit in range(bits):
        vecs = vecs + swap_d(vecs, bit)
    vecs = vecs + swap_y(vecs)
    shard = lax.dynamic_slice_in_dim(vecs[:6], dp * rows, rows, 1)
    bias = vecs[6:].reshape(mp_n, hidden)
    cols = hidden // dp_n
    bias = lax.dynamic_slice(bias, (mp, dp * cols), (1, cols))

    def both(own, oth):
        return jnp.where(mp == 0, jnp.stack([own, oth]), jnp.stack([oth, own]))

    return (
        both(out_own, out_oth),
        both(gt_own, gt_oth),
        shard[4],
        shard[5],
        total_at[:3],
        total_at[3].T,
        shard[3],
        shard[1],
        shard[2],
        total[0],
        bias,
        total[1].T,
        shard[0],
    )


def slot_of(a, two):
    q = ((two & 1) << 1) | (two >> 1)
    d = q ^ a
    return ((d & 1) << 1) | (d >> 1)


MESH = pl.DeviceIdType.MESH
ROWS = 48
VMEM_ALL = 67043328


FIRST_ROWS = 1


def place_rows(ref, value):
    for b in range(16):
        p = bit_reverse(b, 4)
        ref[p * ROWS : (p + 1) * ROWS, :] = value[b * ROWS : (b + 1) * ROWS, :]


def store_rows(ref, index, value, turn):
    rows = value.shape[0] // 8
    for b in range(8):
        c, i, j = b // 4, (b // 2) % 2, b % 2
        if i == j:
            at = pl.ds(b * rows, rows)
        else:
            at = pl.ds(aligned((4 * c + 1) * rows + (i * turn + j * (1 - turn)) * rows, 16), rows)
        ref[(*index, at, slice(None))] = value[b * rows : (b + 1) * rows]


def aligned(v, n):
    return pl.multiple_of(v, n)


def layer_kernel(
    lens, tok_h, cot_h, g1_v, s1_v, g2_v, s2_v, b_out_v, b_down_v, bu, wq_h, wo_h, wu_h, wd_h,
    out_h, gt_h, gt_far, d_qkv, d_out, d_up, d_down, vec_out,
    tok, n1, n1t, gm, gmt, n2, n2t, resid, macc, gacc, att, lse, wq, wo, wu, wd, bu_oth, bias_rows,
    grad, rc, rx, rz, rw, ry, ac, ax, az, aw, ay, ob, gl, vs, vr,
    loc, agl_s, agl_r, att_s, att_r, m_s, m_r, a_s, a_r, e_s, e_r, o_sem,
):
    dp, mp = lax.axis_index("dp"), lax.axis_index("mp")
    core, x, z0, z1 = dp % 2, (dp // 2) % 2, (dp // 4) % 2, dp // 8
    to_c = (dp + 1 - 2 * core, mp)
    to_x = (dp + 2 - 4 * x, mp)
    to_z = (dp + 4 - 8 * z0, mp)
    to_w = (dp + 8 - 16 * z1, mp)
    to_y = (dp, 1 - mp)
    seq, width = n1.shape
    g1, s1, g2, s2, b_out, b_down = (v[...].reshape(1, width) for v in (g1_v, s1_v, g2_v, s2_v, b_out_v, b_down_v))

    def remote(src, dst, ss, rs, dev):
        return pltpu.make_async_remote_copy(
            src_ref=src, dst_ref=dst, send_sem=ss, recv_sem=rs, device_id=dev, device_id_type=MESH
        )

    def arrived(dst, rs, dev):
        remote(dst, dst, rs, rs, dev).wait_recv()

    def sent(src, ss, dev):
        remote(src, src, ss, ss, dev).wait_send()

    def local(src, dst, sem):
        return pltpu.make_async_copy(src, dst, sem)

    peer_tok = local(tok_h.at[1 - mp], tok.at[0], loc.at[0])
    own_tok = local(tok_h.at[mp], tok.at[1], loc.at[1])
    cot = local(cot_h.at[mp], gm, loc.at[2])
    wq_in = [local(wq_h.at[:, :, pl.ds(p * PAIR, PAIR)], wq.at[pl.ds(3 * p, 3)], loc.at[3 + p]) for p in range(3)]
    wo_in = local(wo_h, wo.at[pl.ds(0, 3)], loc.at[6])
    wu_in = [local(wu_h.at[:, pl.ds(j * PAIR, PAIR)], wu.at[j], loc.at[7 + j]) for j in range(12)]
    wd_in = local(wd_h, wd.at[pl.ds(0, 4)], loc.at[19])
    for c in [peer_tok] + wq_in + wu_in[:3] + [own_tok, cot, wo_in] + wu_in[3:] + [wd_in]:
        c.start()

    barrier = pltpu.get_barrier_semaphore()
    for dev in (to_c, to_x, to_z, to_w, to_y):
        pl.semaphore_signal(barrier, inc=1, device_id=dev, device_id_type=MESH)
    pl.semaphore_wait(barrier, 5)

    def span(i, other, at, n):
        unit = 16 if i == 0 else 96 if i < 5 else 48
        rows = pl.ds(aligned(at * unit, 16), n * unit)
        if i == 0:
            return wo.at[pl.ds(3 * other, 3), rows, :]
        if i < 5:
            return wu.at[pl.ds(12 * other + 3 * (i - 1), 3), rows, :]
        return wd.at[4 * other + i - 5, rows, :]

    def half_rows(other, c):
        return wq.at[pl.ds(9 * other, 9), pl.ds(aligned(c * 384, 384), 384), :]

    def axes_of(i):
        return (z0, x, to_z, to_x) if i >= 5 else (x, z0, to_x, to_z)

    def spot(i, r):
        if i == 9:
            return half_rows(1, core if r == 0 else 1 - core)
        first, second = axes_of(i)[:2]
        own = core * 4 + second * 2
        return [(own + first, 1), (own + 1 - first, 1), (core * 4 + (1 - second) * 2, 2), ((1 - core) * 4, 4)][r]

    def landed(i, r):
        return spot(i, r) if i == 9 else span(i, 1, *spot(i, r))

    def passed(i, r):
        if i == 9:
            return half_rows(int(r > 0), core)
        first, second = axes_of(i)[:2]
        own = core * 4 + second * 2
        if r == 0:
            return wo_h.at[:, pl.ds(aligned((own + first) * 16, 16), 16), :] if i == 0 else (
                wd_h.at[i - 5, pl.ds(aligned((own + first) * 48, 16), 48), :] if i >= 5 else span(i, 0, own + first, 1)
            )
        return span(i, 1, *[(own + first, 1), (own, 2), (core * 4, 4)][r - 1])

    def toward(i, r):
        return to_c if r == 3 else to_y if r == 0 else axes_of(i)[1 + r]

    def pass_on(i, r):
        if r > 0:
            before = 0 if i == 9 else r - 1
            arrived(landed(i, before), agl_r.at[i, before], to_y)
        into = landed(i, 0) if r == 0 else passed(i, r)
        remote(passed(i, r), into, agl_s.at[i, r], agl_r.at[i, r], toward(i, r)).start()

    def have(i):
        arrived(landed(i, 3), agl_r.at[i, 3], to_c)

    bu_copy = remote(bu, bu_oth, agl_s.at[10, 0], agl_r.at[10, 0], to_y)
    bu_copy.start()
    for i in (0, 5):
        pass_on(i, 0)
    vs[0] = jnp.zeros_like(vs[0])

    lane = lax.broadcasted_iota(jnp.int32, (seq, PAIR), 1)
    place = lax.broadcasted_iota(jnp.int32, (seq, 1), 0)
    scale = HEAD_DIM**-0.5
    own_len = lens[mp]

    peer_tok.wait()
    for c in wq_in + wu_in[:3]:
        c.wait()
    pass_on(1, 0)

    def att_copy(i):
        return (
            remote(att.at[i], att.at[6 + i], att_s.at[0, i], att_r.at[0, i], to_y),
            remote(lse.at[i], lse.at[6 + i], att_s.at[1, i], att_r.at[1, i], to_y),
        )

    def attend(i, _):
        chip, pair = i // 3, i % 3

        @pl.when(i == 3)
        def _():
            own_tok.wait()

        @pl.when(pair == 0)
        def _():
            xhat, _ = normalize(tok[chip].astype(F32))
            normed = (xhat * g1 + s1).astype(BF)
            n1[...] = normed

            @pl.when(chip == 1)
            def _():
                place_rows(n1t, normed.T)

        w = jnp.concatenate([wq[3 * pair], wq[3 * pair + 1], wq[3 * pair + 2]], axis=1)
        qkv = mm(n1[...], w).astype(BF)
        q = qkv[:, :PAIR] * jnp.asarray(scale, BF)
        k = qkv[:, PAIR : 2 * PAIR]
        vt = qkv[:, 2 * PAIR :].T
        visible = place < lens[(1 - mp) * (1 - chip) + mp * chip]
        outs = []
        for h in range(2):
            mine = (lane >= h * HEAD_DIM) & (lane < (h + 1) * HEAD_DIM)
            s = jnp.where(visible, mm_t(jnp.where(mine, k, jnp.zeros_like(k)), q), -1e30)
            top = jnp.max(s, 0, keepdims=True)
            e = jnp.exp(s - top)
            total = jnp.sum(e, 0, keepdims=True)
            lse[i, h : h + 1, :] = top + jnp.log(total)
            o = mm(vt[h * HEAD_DIM : (h + 1) * HEAD_DIM], e.astype(BF))
            outs.append(o / total)
        lse[i, 2:8, :] = jnp.zeros((6, seq), F32)
        att[i] = jnp.concatenate(outs, 0).T.astype(BF)

        @pl.when(chip == 0)
        def _():
            for c in att_copy(i):
                c.start()

        for when, steps in (
            (1, [(0, 1)]),
            (2, [(2, 0), (6, 0), (1, 1), (3, 0), (7, 0), (4, 0), (8, 0), (5, 1), (9, 0), (0, 2)]),
            (3, [(5, 2)]),
            (4, [(1, 2), (0, 3)]),
            (5, [(2, 1), (6, 1)]),
        ):

            @pl.when(i == when)
            def _(when=when, steps=steps):
                if when == 2:
                    for c in wu_in[3:]:
                        c.wait()
                for step in steps:
                    pass_on(*step)

        return 0

    lax.fori_loop(0, 6, attend, 0)

    cot.wait()
    visible = place < own_len
    g = jnp.where(visible, gm[...].astype(F32), 0.0)
    g_low = g.astype(BF)
    gm[...] = g_low
    place_rows(gmt, g_low.T)
    vs[0, 0:1, :] = jnp.sum(g, 0, keepdims=True)
    wo_in.wait()
    have(0)
    for i in range(3):
        arrived(att.at[6 + i], att_r.at[0, i], to_y)
        arrived(lse.at[6 + i], att_r.at[1, i], to_y)
    blocks = jnp.concatenate([att[3 + p] for p in range(6)], axis=1)
    r = tok[1].astype(F32) + mm(blocks, wo[...].reshape(6 * PAIR, width)) + b_out
    resid[...] = r
    xhat, _ = normalize(r)
    normed = (xhat * g2 + s2).astype(BF)
    n2[...] = normed
    place_rows(n2t, normed.T)
    macc[...] = jnp.zeros_like(macc)
    gacc[...] = jnp.zeros_like(gacc)

    half = 384

    def m_turn(t):
        a, b = t % 2, t // 2 % 2
        return a

    def halved(n, turn):
        first, second = turn * x + (1 - turn) * z0, turn * z0 + (1 - turn) * x
        return sum(b * (384 >> k) for k, b in enumerate((core, first, second, z1)[:n]))

    def given(n, turn):
        first, second = turn * x + (1 - turn) * z0, turn * z0 + (1 - turn) * x
        return halved(n, turn) + (1 - (core, first, second, z1)[n]) * (384 >> n)

    def partner(n, turn):
        if n == 0:
            return to_c
        if n == 3:
            return to_w
        by_x = turn if n == 1 else 1 - turn
        return (dp + by_x * (2 - 4 * x) + (1 - by_x) * (4 - 8 * z0), mp)

    m_buf = [rc, rx, rz, rw]

    def m_copy(n, t):
        rows = 384 >> n
        turn = m_turn(t)
        src = grad.at[t, :, pl.ds(aligned(given(n, turn), 16), rows), :]
        return remote(src, m_buf[n].at[t], m_s.at[n, t], m_r.at[n, t], partner(n, turn))

    def m_step(n, t):
        rows = 384 >> n
        turn = m_turn(t)
        at = pl.ds(aligned(halved(n + 1, turn), 16), rows)
        arrived(m_buf[n].at[t], m_r.at[n, t], to_c)
        merge = n == 2 and t < 4
        if merge:
            arrived(ry.at[t], m_r.at[4, t], to_y)
        for w in range(2):
            total = grad[t, w, at, :].astype(F32) + m_buf[n][t, w].astype(F32)
            if n == 3:
                (d_up, d_down)[w][:, t * 384 : (t + 1) * 384] = total
                continue
            if merge:
                total += ry[t, w].astype(F32)
            grad[t, w, at, :] = total.astype(BF)
        if n < 2 or merge:
            m_copy(n + 1, t).start()
        elif n == 2:
            m_y(t).start()

    def m_step0(t):
        arrived(rc.at[t], m_r.at[0, t], to_c)
        at = pl.ds(aligned(core * 384, 384), 384)
        for w in range(2):
            grad[t, w, at, :] = (grad[t, w, at, :].astype(F32) + rc[t, w].astype(F32)).astype(BF)
        m_copy(1, t).start()

    def m_y(t):
        src = grad.at[t, :, pl.ds(aligned(halved(3, m_turn(t)), 16), 2 * ROWS), :]
        return remote(src, ry.at[t - 4], m_s.at[4, t], m_r.at[4, t - 4], to_y)

    def tile(t, _):
        for when, steps, ready in (
            (0, [(3, 1), (2, 2), (1, 3)], []),
            (1, [(7, 1), (6, 2), (4, 1), (5, 3), (8, 1), (3, 2)], []),
            (2, [(7, 2), (6, 3), (8, 2)], []),
            (3, [(2, 3), (4, 2)], []),
            (4, [(7, 3), (3, 3)], [1, 5]),
            (5, [(8, 3)], [2, 6]),
            (6, [(4, 3)], [3, 7]),
            (7, [(9, 3)], [4, 8]),
        ):

            @pl.when(t == when)
            def _(when=when, steps=steps, ready=ready):
                if when == 0:
                    wd_in.wait()
                for i in ready:
                    have(i)
                for step in steps:
                    pass_on(*step)

        late = t // 4
        unit = t % 4
        wut = jnp.concatenate([wu[3 * t], wu[3 * t + 1], wu[3 * t + 2]], axis=1)
        wdt = wd[t]
        u = mm(n2[...], wut) + bias_rows[pl.ds(t, 1), :]
        act, slope = gelu_pair(u)
        act = act.astype(BF)
        gp = (mm_t(gm[...], wdt) * slope).astype(BF)
        row = 8 + 4 * (mp + late - 2 * mp * late) + unit
        vs[0, pl.ds(row, 1), 0:384] = jnp.sum(gp.astype(F32), 0, keepdims=True)
        macc[...] += mm(act, wdt)
        gacc[...] += mm_t(gp, wut)
        turn = m_turn(t)
        store_rows(grad, (t, 0), mm(n2t[...], gp).astype(BF), turn)
        store_rows(grad, (t, 1), mm(gmt[...], act).astype(BF), turn)
        m_copy(0, t).start()

        @pl.when(t >= 1)
        def _():
            m_step0(t - 1)

        return 0

    arrived(bu_oth, agl_r.at[10, 0], to_y)
    for j in range(4):
        bias_rows[j : j + 1, :] = bu[j * 384 : (j + 1) * 384].reshape(1, 384)
        bias_rows[4 + j : 5 + j, :] = bu_oth[j * 384 : (j + 1) * 384].reshape(1, 384)
    lax.fori_loop(0, 8, tile, 0)

    r = resid[...]
    ob[...] = jnp.where(visible, r + macc[...] + b_down, 0.0).astype(BF)
    out_own = local(ob, out_h.at[mp], o_sem.at[0])
    out_far = remote(ob, out_h.at[mp], e_s.at[0], e_r.at[0], to_y)
    out_own.start()
    out_far.start()
    xhat, inv = normalize(r)
    gs = gacc[...]
    gres = gm[...].astype(F32) + norm_back(gs, xhat, inv, g2)
    low = gres.astype(BF)
    n2[...] = low
    place_rows(n2t, low.T)
    vs[0, 1:2, :] = jnp.sum(gs * xhat, 0, keepdims=True)
    vs[0, 2:3, :] = jnp.sum(gs, 0, keepdims=True)
    vs[0, 3:4, :] = jnp.sum(gres, 0, keepdims=True)
    resid[...] = gres
    gacc[...] = jnp.zeros_like(gacc)
    m_step(1, 3)
    have(9)
    for i in range(1, 5):
        for r in range(4):
            sent(passed(i, r), agl_s.at[i, r], to_c)

    a_buf = [ac, ax, az, aw]

    def a_turn(p):
        q = p % 3
        return 1 + -1 * (q % 2)

    def a_copy(n, p):
        rows = 384 >> n
        turn = a_turn(p)
        src = wu.at[pl.ds(4 * p, 4), pl.ds(aligned(given(n, turn), 16), rows), :]
        return remote(src, a_buf[n].at[p], a_s.at[n, p], a_r.at[n, p], partner(n, turn))

    def a_step(n, p):
        rows = 384 >> n
        arrived(a_buf[n].at[p], a_r.at[n, p], to_c)
        merge = n == 2 and p < 3
        if merge:
            arrived(ay.at[p], a_r.at[4, p], to_y)
        at = pl.ds(aligned(halved(n + 1, a_turn(p)), 16), rows)
        for w in range(4):
            total = wu[4 * p + w, at, :].astype(F32) + a_buf[n][p, w].astype(F32)
            if n == 3:
                cols = slice(p * PAIR, (p + 1) * PAIR)
                if w < 3:
                    d_qkv[w, :, cols] = total
                else:
                    d_out[:, cols] = total
                continue
            if merge:
                total += ay[p, w].astype(F32)
            wu[4 * p + w, at, :] = total.astype(BF)
        if n < 2 or merge:
            a_copy(n + 1, p).start()
        elif n == 2:
            a_y(p).start()

    def a_y(p):
        src = wu.at[pl.ds(4 * p, 4), pl.ds(aligned(halved(3, a_turn(p)), 16), 2 * ROWS), :]
        return remote(src, ay.at[p - 3], a_s.at[4, p], a_r.at[4, p - 3], to_y)

    zero = jnp.zeros((seq, PAIR), BF)

    def back(k, _):
        p = (k + 3) % 6
        w = jnp.concatenate([wq[3 * p], wq[3 * p + 1], wq[3 * p + 2]], axis=1)
        qkv = mm(n1[...], w).astype(BF)
        q, key, v = qkv[:, :PAIR], qkv[:, PAIR : 2 * PAIR], qkv[:, 2 * PAIR :]
        q_s = q * jnp.asarray(scale, BF)
        ga = mm_t(n2[...], wo[p]).astype(BF)
        kt = key.T
        dqt = []
        dk = jnp.zeros((seq, PAIR), F32)
        dv = jnp.zeros((seq, PAIR), F32)
        for h in range(2):
            mine = (lane >= h * HEAD_DIM) & (lane < (h + 1) * HEAD_DIM)
            s = jnp.where(visible, mm_t(jnp.where(mine, key, zero), q_s), -1e30)
            prob = jnp.exp(s - lse[3 + p, h : h + 1, :])
            d_prob = mm_t(jnp.where(mine, v, zero), ga)
            row = jnp.sum(prob * d_prob, 0, keepdims=True)
            ds = (prob * (d_prob - row) * scale).astype(BF)
            dk += mm(ds, jnp.where(mine, q, zero))
            dv += mm(prob.astype(BF), jnp.where(mine, ga, zero))
            dqt.append(mm(kt[h * HEAD_DIM : (h + 1) * HEAD_DIM], ds))
        dq = jnp.concatenate(dqt, 0).T
        d = jnp.concatenate([dq.astype(BF), dk.astype(BF), dv.astype(BF)], axis=1)
        gacc[...] += mm_t(d, w)
        dw = mm(n1t[...], d).astype(BF)
        turn = a_turn(p)
        for c in range(3):
            store_rows(wu, (4 * p + c,), dw[:, c * PAIR : (c + 1) * PAIR], turn)
        store_rows(wu, (4 * p + 3,), mm(n2t[...], att[3 + p]).astype(BF), turn)
        a_copy(0, p).start()
        for when, steps in (
            (0, [(m_step, 1, 4), (m_step, 1, 5), (m_step, 0, 7), (m_step, 1, 1)]),
            (2, [(m_step, 2, 4), (m_step, 1, 6), (m_step, 1, 0)]),
            (3, [(m_step, 1, 7), (m_step, 2, 5), (a_step, 0, 3), (m_step, 1, 2), (a_step, 0, 5), (a_step, 0, 4), (m_step, 2, 6)]),
            (4, [(a_step, 0, 0), (m_step, 2, 7), (m_step, 2, 0), (m_step, 2, 1)]),
            (5, [(a_step, 0, 1), (a_step, 1, 4)]),
        ):

            @pl.when(k == when)
            def _(steps=steps):
                for step in steps:
                    step[0](*step[1:])

        return 0

    lax.fori_loop(0, 6, back, 0)

    chunk = seq // 4

    def gt_copy(j):
        rows = pl.ds(j * chunk, chunk)
        return remote(gl.at[rows, :], gt_far.at[rows, :], e_s.at[1 + j], e_r.at[1 + j], to_y)

    gain_sum = jnp.zeros((1, width), F32)
    shift_sum = jnp.zeros((1, width), F32)
    for j in range(4):
        rows = slice(j * chunk, (j + 1) * chunk)
        xhat, inv = normalize(tok[1, rows].astype(F32))
        gf = gacc[rows]
        gt = resid[rows] + norm_back(gf, xhat, inv, g1)
        resid[rows] = gt
        gl[rows] = gt.astype(BF)
        if j < FIRST_ROWS:
            gt_copy(j).start()
        gain_sum += jnp.sum(gf * xhat, 0, keepdims=True)
        shift_sum += jnp.sum(gf, 0, keepdims=True)
        if j == 0:
            a_step(0, 2)
    gt_own = local(resid, gt_h, o_sem.at[1])
    gt_own.start()
    vs[0, 4:5, :] = gain_sum
    vs[0, 5:6, :] = shift_sum
    v_dev = [to_c, to_z, to_w, to_x, to_y]

    def v_copy(n):
        return remote(vs.at[n], vr.at[n], e_s.at[5 + n], e_r.at[5 + n], v_dev[n])

    def gt_send(j):
        gt_copy(j).start()

    def v_step(n):
        arrived(vr.at[n], e_r.at[5 + n], v_dev[n])
        if n < 4:
            vs[n + 1] = vs[n] + vr[n]
            v_copy(n + 1).start()
        else:
            vec_out[...] = vs[4] + vr[4]

    v_copy(0).start()
    for step in (
        (gt_send, 2), (a_step, 1, 3), (m_step, 2, 3), (m_step, 3, 1), (v_step, 0), (a_step, 2, 3), (m_step, 2, 2),
        (gt_send, 3), (a_step, 1, 0), (a_step, 1, 1), (a_step, 1, 5), (v_step, 1), (a_step, 2, 0), (a_step, 2, 4),
        (a_step, 1, 2), (a_step, 2, 5), (a_step, 2, 1), (gt_send, 1), (m_step, 3, 2), (v_step, 2), (m_step, 3, 3),
        (m_step, 3, 0), (a_step, 2, 2), (v_step, 3), (a_step, 3, 1), (a_step, 3, 0), (a_step, 3, 2),
    ):
        step[0](*step[1:])

    v_step(4)

    bu_copy.wait_send()
    for i in (0, 5, 6, 7, 8, 9):
        for r in (0, 3) if i == 9 else range(4):
            sent(passed(i, r), agl_s.at[i, r], to_c)
    for i in range(3):
        for c in att_copy(i):
            c.wait_send()

    def drain_m(t, _):
        for n in range(3):
            m_copy(n, t).wait_send()

        @pl.when(t < 4)
        def _():
            m_copy(3, t).wait_send()

        @pl.when(t >= 4)
        def _():
            m_y(t).wait_send()

        return 0

    lax.fori_loop(0, 8, drain_m, 0)

    def drain_a(p, _):
        for n in range(3):
            a_copy(n, p).wait_send()

        @pl.when(p < 3)
        def _():
            a_copy(3, p).wait_send()

        @pl.when(p >= 3)
        def _():
            a_y(p).wait_send()

        return 0

    lax.fori_loop(0, 6, drain_a, 0)
    for j in range(4):
        gt_copy(j).wait_send()
        arrived(gt_far.at[pl.ds(j * chunk, chunk), :], e_r.at[1 + j], to_y)
    for n in range(5):
        v_copy(n).wait_send()
    out_own.wait()
    out_far.wait_send()
    arrived(out_h.at[1 - mp], e_r.at[0], to_y)
    gt_own.wait()


def finish_kernel(
    out_h, gt_h, gt_far, d_qkv, d_out, d_up, d_down, vec,
    out_f, gt_f, g1_f, s1_f, qkv_f, wo_f, bo_f, g2_f, s2_f, up_f, bu_f, down_f, bd_f,
    ob, gb, far, qkv, wo, up, down, in_sem, out_sem,
):
    dp, mp = lax.axis_index("dp"), lax.axis_index("mp")
    seq, width = far.shape
    chunk = seq // 4
    parts = [pl.ds(j * chunk, chunk) for j in range(4)]
    fars = [pltpu.make_async_copy(gt_far.at[r], far.at[r], in_sem.at[j]) for j, r in enumerate(parts)]
    owns = [pltpu.make_async_copy(gt_h.at[r], gb.at[mp, r], in_sem.at[4 + j]) for j, r in enumerate(parts)]
    outs = [pltpu.make_async_copy(out_h.at[c], ob.at[c], in_sem.at[8 + c]) for c in range(2)]
    small = [(d_qkv, qkv, qkv_f), (d_out, wo, wo_f), (d_up, up, up_f), (d_down, down, down_f)]
    grads = [pltpu.make_async_copy(a, b, in_sem.at[10 + j]) for j, (a, b, _) in enumerate(small)]
    for c in fars + owns + outs + grads:
        c.start()
    leave = []

    def go(src, dst):
        leave.append(pltpu.make_async_copy(src, dst, out_sem.at[len(leave)]))
        leave[-1].start()

    for j, r in enumerate(parts):
        fars[j].wait()
        gb[1 - mp, r] = far[r].astype(F32)
        go(gb.at[1 - mp, r], gt_f.at[1 - mp, r])
        owns[j].wait()
        go(gb.at[mp, r], gt_f.at[mp, r])
    for c in range(2):
        outs[c].wait()
        go(ob.at[c], out_f.at[c])
    for c, (_, b, f) in zip(grads, small):
        c.wait()
        go(b, f)
    turned = pltpu.roll(vec[0:8, :], (width - dp * ROWS) % width, 1)
    for row, ref in enumerate((bd_f, g2_f, s2_f, bo_f, g1_f, s1_f)):
        ref[...] = turned[row : row + 1, :ROWS].reshape(ROWS)
    tile = up.shape[1] // 4
    bias = vec[pl.ds(8 + 4 * mp + dp // 4, 1), 0:tile]
    bias = pltpu.roll(jnp.broadcast_to(bias, (8, tile)), (tile - dp % 4 * 2 * ROWS) % tile, 1)
    bu_f[...] = bias[0:1, : 2 * ROWS]
    for c in leave:
        c.wait()


def kernel_program(
    mp_n, tokens, lengths, ln1_gain, ln1_shift, w_qkv, w_out, b_out, ln2_gain, ln2_shift, w_up, b_up, w_down, b_down, cotangent
):
    seq, width = tokens.shape[1:]
    feat, hidden = w_qkv.shape[2], w_up.shape[1]
    tile = hidden // 4
    args = [
        lengths, tokens, cotangent, ln1_gain, ln1_shift, ln2_gain, ln2_shift, b_out, b_down,
        b_up, w_qkv, w_out.reshape(3, PAIR, width), w_up, w_down.reshape(4, tile, width),
    ]
    hbm, vmem = pl.BlockSpec(memory_space=pl.ANY), pl.BlockSpec(memory_space=pltpu.VMEM)
    outs = [
        sds(tokens.shape, BF),
        sds((seq, width), F32),
        sds((seq, width), BF),
        sds((3, ROWS, feat), F32),
        sds((ROWS, feat), F32),
        sds((ROWS, hidden), F32),
        sds((ROWS, hidden), F32),
        sds((16, width), F32),
    ]
    v = pltpu.VMEM
    act = v((seq, width), BF)
    act_t = v((width, seq), BF)
    wide = v((seq, width), F32)
    scratch = [
        v((2, seq, width), BF), act, act_t, act, act_t, act, act_t, wide, wide, wide,
        v((9, seq, PAIR), BF), v((9, 8, seq), F32),
        v((18, width, PAIR), BF), v((6, PAIR, width), BF), v((24, width, PAIR), BF), v((8, tile, width), BF), v((hidden,), F32), v((8, tile), F32),
        v((8, 2, width, tile), BF),
        v((8, 2, 384, tile), BF), v((8, 2, 192, tile), BF), v((8, 2, 96, tile), BF), v((4, 2, 48, tile), BF), v((4, 2, 96, tile), BF),
        v((6, 4, 384, PAIR), BF), v((6, 4, 192, PAIR), BF), v((6, 4, 96, PAIR), BF), v((3, 4, 48, PAIR), BF), v((3, 4, 96, PAIR), BF),
        act, act, v((5, 16, width), F32), v((5, 16, width), F32),
    ]
    dma = pltpu.SemaphoreType.DMA
    scratch += [
        dma((20,)), dma((11, 4)), dma((11, 4)), dma((2, 3)), dma((2, 3)), dma((5, 8)), dma((5, 8)), dma((5, 6)), dma((5, 6)),
        dma((10,)), dma((10,)), dma((2,)),
    ]
    results = pl.pallas_call(
        layer_kernel,
        name="layer",
        out_shape=outs,
        in_specs=[pl.BlockSpec(memory_space=pltpu.SMEM), hbm, hbm] + [vmem] * 7 + [hbm] * 4,
        out_specs=[hbm] * 3 + [vmem] * 5,
        scratch_shapes=scratch,
        compiler_params=pltpu.CompilerParams(collective_id=0, has_side_effects=True, vmem_limit_bytes=VMEM_ALL),
    )(*args)
    shard = sds((ROWS,), F32)
    finals = [
        sds(tokens.shape, BF), sds(tokens.shape, F32), shard, shard, sds((3, ROWS, feat), F32), sds((ROWS, feat), F32), shard, shard,
        shard, sds((ROWS, hidden), F32), sds((1, 2 * ROWS), F32), sds((ROWS, hidden), F32), shard,
    ]
    finished = list(
        pl.pallas_call(
            finish_kernel,
            name="finish",
            out_shape=finals,
            in_specs=[hbm] * 7 + [vmem],
            out_specs=[vmem if f.shape in (shard.shape, (1, 2 * ROWS)) else hbm for f in finals],
            scratch_shapes=[v(tokens.shape, BF), v(tokens.shape, F32), v((seq, width), BF)]
            + [v(r.shape, F32) for r in results[3:7]]
            + [dma((14,)), dma((14,))],
            compiler_params=pltpu.CompilerParams(vmem_limit_bytes=VMEM_ALL),
        )(*results)
    )
    for i in (5, 11):
        finished[i] = finished[i].T
    return tuple(finished)


def solution(mesh):
    dp_n, mp_n = mesh.shape["dp"], mesh.shape["mp"]
    body = functools.partial(kernel_program, mp_n) if dp_n == 16 else functools.partial(permute_program, dp_n, mp_n)
    return jax.shard_map(
        body,
        mesh=mesh,
        in_specs=(
            P("dp", None, None),
            P("dp"),
            P(),
            P(),
            P(None, None, "mp"),
            P("mp", None),
            P(),
            P(),
            P(),
            P(None, "mp"),
            P("mp"),
            P("mp", None),
            P(),
            P("dp", None, None),
        ),
        out_specs=(
            P("dp", None, None),
            P("dp", None, None),
            P("dp"),
            P("dp"),
            P(None, "dp", "mp"),
            P("mp", "dp"),
            P("dp"),
            P("dp"),
            P("dp"),
            P("dp", "mp"),
            P("mp", "dp"),
            P("mp", "dp"),
            P("dp"),
        ),
        check_vma=False,
    )
```
